32 devices in a mesh: row: 4 (over z), col: 8 (over y, x, core).
Axes of the slice: x: 2, y: 2, z: 4, core: 2. Of those that a mesh axis runs over, the one named last changes fastest.
Arguments:
- inputs: bfloat16 [4096, 2048], P('row', 'col'), may hold values from -6 to 6
- norm1_gain: float32 [2048], P('col'), may hold values from 0.5 to 1.5
- norm1_shift: float32 [2048], P('col'), may hold values from -4 to 4
- query_weight: float32 [2048, 2048], P('row', 'col'), may hold values from -0.125 to 0.125
- query_bias: float32 [2048], P('col'), may hold values from -4 to 4
- key_weight: float32 [2048, 2048], P('row', 'col'), may hold values from -0.125 to 0.125
- value_weight: float32 [2048, 2048], P('row', 'col'), may hold values from -0.125 to 0.125
- value_bias: float32 [2048], P('col'), may hold values from -4 to 4
- output_weight: float32 [2048, 2048], P('col', 'row'), may hold values from -0.375 to 0.375
- output_bias: float32 [2048], P('col'), may hold values from -4 to 4
- norm2_gain: float32 [2048], P('col'), may hold values from 0.5 to 1.5
- norm2_shift: float32 [2048], P('col'), may hold values from -4 to 4
- expand_weight: float32 [2048, 8192], P('row', 'col'), may hold values from -1 to 1
- expand_bias: float32 [8192], P('col'), may hold values from -4 to 4
- contract_weight: float32 [8192, 2048], P('col', 'row'), may hold values from -0.0625 to 0.0625
- contract_bias: float32 [2048], P('col'), may hold values from -4 to 4
- cotangent: bfloat16 [4096, 2048], P('row', 'col'), may hold values from -6 to 6
Outputs:
- outputs: bfloat16 [4096, 2048], P('row', 'col')
- input_grad: float32 [4096, 2048], P('row', 'col')
- norm1_gain_grad: float32 [2048], P(('col', 'row'))
- norm1_shift_grad: float32 [2048], P(('col', 'row'))
- query_weight_grad: float32 [2048, 2048], P('row', 'col')
- query_bias_grad: float32 [2048], P(('col', 'row'))
- key_weight_grad: float32 [2048, 2048], P('row', 'col')
- value_weight_grad: float32 [2048, 2048], P('row', 'col')
- value_bias_grad: float32 [2048], P(('col', 'row'))
- output_weight_grad: float32 [2048, 2048], P('col', 'row')
- output_bias_grad: float32 [2048], P(('col', 'row'))
- norm2_gain_grad: float32 [2048], P(('col', 'row'))
- norm2_shift_grad: float32 [2048], P(('col', 'row'))
- expand_weight_grad: float32 [2048, 8192], P('row', 'col')
- expand_bias_grad: float32 [8192], P(('col', 'row'))
- contract_weight_grad: float32 [8192, 2048], P('col', 'row')
- contract_bias_grad: float32 [2048], P(('col', 'row'))
The draws below stay inside these ranges and needn't reach their ends.
All inputs are finite; a program needn't handle non-finite values.
Results may differ from the reference program's by a relative error of at most 0.013.
Values may be sent and summed in bfloat16 or wider, within the bound.
A program may use at most 128 MiB of HBM per device.

```python
import math
import jax
import jax.numpy as jnp
from jax import lax

D = 2048
FF = 8192
HEADS = 16
HEAD = 128
LEN = 1024
TOKENS = 4096


def draw_expand_weight(key, part):
    entry_key = jax.random.fold_in(key, 11)
    column_key = jax.random.fold_in(key, 23)
    entries = jnp.clip(jax.random.normal(entry_key, (D, FF), jnp.float32), -4.0, 4.0)
    columns = jnp.clip(jax.random.normal(column_key, (1, FF), jnp.float32), -4.0, 4.0)
    return ((entries + 0.5 * columns) * float(D) ** (-0.5)).astype(jnp.float32)


def level_of(own_key, shape, pieces, low, largest):
    level, own = 1.0, jax.random.fold_in(own_key, 6)
    for dim, blocks in pieces:
        heights = jnp.exp(jax.random.uniform(jax.random.fold_in(own, dim), (blocks,), jnp.float32, low / len(pieces), largest / len(pieces)))
        level = level * jnp.repeat(heights, shape[dim] // blocks).reshape([-1 if axis == dim else 1 for axis in range(len(shape))])
    return level


def noise(stream_key, dims, width, bound, split=(), held_as=jnp.bfloat16):
    values = jax.random.normal(stream_key, dims, jnp.float32) * width
    if len(split) > 0:
        values = level_of(stream_key, dims, split, -0.22, 0.18) * values
    return jnp.clip(values, min=-bound, max=bound).astype(held_as)


def setup_inputs(seed: int = 0) -> dict:
    arg_keys = jax.random.split(jax.random.key(seed), 18)
    return {
        "inputs": noise(arg_keys[0], (TOKENS, D), 1.0, 6.0, ((0, 4), (1, 8))),
        "norm1_gain": jnp.clip(1.0 + 0.1 * jax.random.normal(arg_keys[1], (D,), jnp.float32), 0.5, 1.5),
        "norm1_shift": noise(arg_keys[2], (D,), 0.3, 4.0, ((0, 8),), jnp.float32),
        "query_weight": noise(arg_keys[3], (D, D), D ** -0.5, 0.125, ((0, 4), (1, 8)), jnp.float32),
        "query_bias": noise(arg_keys[4], (D,), 0.5, 4.0, ((0, 8),), jnp.float32),
        "key_weight": noise(arg_keys[5], (D, D), D ** -0.5, 0.125, ((0, 4), (1, 8)), jnp.float32),
        "value_weight": noise(arg_keys[6], (D, D), D ** -0.5, 0.125, ((0, 4), (1, 8)), jnp.float32),
        "value_bias": noise(arg_keys[7], (D,), 0.5, 4.0, ((0, 8),), jnp.float32),
        "output_weight": noise(arg_keys[8], (D, D), (D // 8) ** -0.5, 0.375, ((0, 8), (1, 4)), jnp.float32),
        "output_bias": noise(arg_keys[9], (D,), 0.5, 4.0, ((0, 8),), jnp.float32),
        "norm2_gain": jnp.clip(1.0 + 0.1 * jax.random.normal(arg_keys[10], (D,), jnp.float32), 0.5, 1.5),
        "norm2_shift": noise(arg_keys[11], (D,), 0.3, 4.0, ((0, 8),), jnp.float32),
        "expand_weight": draw_expand_weight(jax.random.fold_in(arg_keys[17], 71), 0),
        "expand_bias": noise(arg_keys[13], (FF,), 0.5, 4.0, ((0, 8),), jnp.float32),
        "contract_weight": noise(arg_keys[14], (FF, D), FF ** -0.5, 0.0625, ((0, 8), (1, 4)), jnp.float32),
        "contract_bias": noise(arg_keys[15], (D,), 0.5, 4.0, ((0, 8),), jnp.float32),
        "cotangent": noise(arg_keys[16], (TOKENS, D), 1.0, 6.0, ((0, 4), (1, 8))),
    }


@jax.custom_vjp
def low(v):
    return lax.optimization_barrier(v.astype(jnp.bfloat16)).astype(jnp.float32)

@jax.custom_vjp
def low_back(v):
    return v

def low_keep(v):
    return (low(v), None)

def low_pass(kept, grad):
    return (grad,)

def back_keep(v):
    return (v, None)

def back_low(kept, grad):
    return (low(grad),)
low.defvjp(low_keep, low_pass)
low_back.defvjp(back_keep, back_low)
epsilon = 1e-05

def product(first_operand, second_operand):
    return jnp.dot(first_operand, second_operand, precision=lax.Precision.HIGHEST)

def normalize(values, gain, shift):
    average = lax.optimization_barrier(jnp.mean(values, axis=-1, keepdims=True))
    centred = values - average
    variance = lax.optimization_barrier(jnp.mean(centred * centred, axis=-1, keepdims=True))
    return centred * lax.rsqrt(variance + epsilon) * gain + shift

def gelu_tanh(values):
    return jax.nn.gelu(values, approximate=True)

def attend_sequence(carry, sequence):
    query_rows, key_rows, value_rows = sequence
    position = jnp.arange(LEN)
    distance = (position[None, :] - position[:, None]).astype(jnp.float32)
    slopes = jnp.exp2(-8.0 * (jnp.arange(HEADS) + 1).astype(jnp.float32) / HEADS)
    scores = jnp.einsum('qhd,khd->hqk', query_rows, key_rows, precision=lax.Precision.HIGHEST) * (1.0 / math.sqrt(HEAD))
    scores = scores + slopes[:, None, None] * distance[None]
    scores = low_back(jnp.where(distance[None] <= 0, scores, -jnp.inf))
    weights = low(jax.nn.softmax(scores, axis=-1))
    attended = jnp.einsum('hqk,khd->qhd', weights, value_rows, precision=lax.Precision.HIGHEST)
    return (carry, attended)

def by_sequence(matrix):
    return matrix.reshape(TOKENS // LEN, LEN, HEADS, HEAD)

def layer(inputs, norm1_gain, norm1_shift, query_weight, query_bias, key_weight, value_weight, value_bias, output_weight, output_bias, norm2_gain, norm2_shift, expand_weight, expand_bias, contract_weight, contract_bias):
    normed1 = low(normalize(inputs, norm1_gain, norm1_shift))
    query_rows = low_back(low(product(normed1, low(query_weight)) + query_bias))
    key_rows = low_back(low(product(normed1, low(key_weight))))
    value_rows = low_back(low(product(normed1, low(value_weight)) + value_bias))
    _, attended = lax.scan(jax.checkpoint(attend_sequence), None, (by_sequence(query_rows), by_sequence(key_rows), by_sequence(value_rows)))
    attended = low_back(low(attended.reshape(TOKENS, D)))
    branch = low_back(product(attended, low(output_weight)) + output_bias)
    middle = inputs + branch
    normed2 = low(normalize(middle, norm2_gain, norm2_shift))
    expanded = low_back(product(normed2, low(expand_weight)) + expand_bias)
    hidden = low(gelu_tanh(expanded))
    contracted = low_back(product(hidden, low(contract_weight)) + contract_bias)
    return middle + contracted

def reference(inputs, norm1_gain, norm1_shift, query_weight, query_bias, key_weight, value_weight, value_bias, output_weight, output_bias, norm2_gain, norm2_shift, expand_weight, expand_bias, contract_weight, contract_bias, cotangent):
    floats = tuple((argument.astype(jnp.float32) for argument in (inputs, norm1_gain, norm1_shift, query_weight, query_bias, key_weight, value_weight, value_bias, output_weight, output_bias, norm2_gain, norm2_shift, expand_weight, expand_bias, contract_weight, contract_bias)))
    result, pullback = jax.vjp(layer, *floats)
    gradients = pullback(cotangent.astype(jnp.float32))
    return (result.astype(jnp.bfloat16), gradients[0], gradients[1], gradients[2], gradients[3], gradients[4], gradients[5], gradients[6], gradients[7], gradients[8], gradients[9], gradients[10], gradients[11], gradients[12], gradients[13], gradients[14], gradients[15])
```

```python
import functools
import math

import jax
import jax.numpy as jnp
from jax import lax
from jax.experimental import pallas as pl
from jax.experimental.pallas import tpu as pltpu
from jax.sharding import PartitionSpec as P

D = 2048
HEADS = 16
HEAD = 128
LEN = 1024

epsilon = 1e-05
MESH = pl.DeviceIdType.MESH
bf16 = jnp.bfloat16
f32 = jnp.float32


def product(first_operand, second_operand):
    return jnp.dot(first_operand, second_operand, preferred_element_type=f32)


def product_back(first_operand, second_operand):
    return lax.dot_general(
        first_operand, second_operand, (((1,), (1,)), ((), ())), preferred_element_type=f32
    )


def token_sum(first_operand, second_operand):
    return lax.dot_general(
        first_operand, second_operand, (((0,), (0,)), ((), ())), preferred_element_type=f32
    )


def gelu_tanh(values):
    return jax.nn.gelu(values, approximate=True)


def flip(index, dim):
    step = 1 << dim
    bit = (index // step) % 2
    return index + (1 - 2 * bit) * step


def flip_mask(index, mask):
    dim = 0
    while mask >> dim:
        if (mask >> dim) & 1:
            index = flip(index, dim)
        dim += 1
    return index


def chip_order(chunk, bits):
    dims = list(range(1, bits))
    start = chunk % len(dims)
    return dims[start:] + dims[:start]


def masks_over(dims):
    masks = [0]
    for dim in dims:
        masks = masks + [m | (1 << dim) for m in masks]
    return masks


def remote(src, dst, send, recv, peer):
    copy = pltpu.make_async_remote_copy(
        src_ref=src,
        dst_ref=dst,
        send_sem=send,
        recv_sem=recv,
        device_id={"col": peer},
        device_id_type=MESH,
    )
    copy.start()
    return copy


def greet(peers):
    barrier = pltpu.get_barrier_semaphore()
    for peer in peers:
        pl.semaphore_signal(barrier, inc=1, device_id={"col": peer}, device_id_type=MESH)
    pl.semaphore_wait(barrier, len(peers))


def gather_steps(me, bits, chunks, source, place, sems):
    chip_send, chip_recv, mate_send, mate_recv = sems
    mate = flip(me, 0)
    held = [[me] for _ in range(chunks)]
    waiting = [[] for _ in range(chunks)]
    mates = []
    sent = []

    def to_mate(c, blocks, base):
        for i, b in enumerate(blocks):
            src = source(c) if base + i == 0 else place(b, c)
            mates.append(
                remote(
                    src, place(b, c), mate_send.at[c, base + i], mate_recv.at[c, base + i], mate
                )
            )

    def stage(c, s):
        order = chip_order(c, bits)
        if s == 0:
            new, base = [me], 0
        else:
            for copy in waiting[c]:
                copy.wait_recv()
            base = len(held[c])
            new = [flip(b, order[s - 1]) for b in held[c]]
            held[c] = held[c] + new
        if s < bits - 1:
            copies = []
            for i, b in enumerate(held[c]):
                slot = (1 << s) - 1 + i
                src = source(c) if i == 0 else place(b, c)
                copies.append(
                    remote(
                        src,
                        place(b, c),
                        chip_send.at[c, slot],
                        chip_recv.at[c, slot],
                        flip(me, order[s]),
                    )
                )
            waiting[c] = copies
            sent.extend(copies)
        to_mate(c, new, base)

    def finish():
        for copy in sent:
            copy.wait_send()
        for copy in mates:
            copy.wait()

    return stage, finish


def gather_sems(n, chunks):
    return [
        pltpu.SemaphoreType.DMA((chunks, n)),
        pltpu.SemaphoreType.DMA((chunks, n)),
        pltpu.SemaphoreType.DMA((chunks, n)),
        pltpu.SemaphoreType.DMA((chunks, n)),
    ]


def scatter_steps(me, bits, chunks, partial, rows, first, later, sems):
    core_send, core_recv, chip_send, chip_recv = sems
    mate = flip(me, 0)
    dims = list(range(1, bits))
    every = masks_over(dims)
    core_copies = {}
    chip_copies = {}
    done = []

    def start(c):
        lead = chip_order(c, bits)[0]
        ranked = sorted(every, key=lambda m: (0 if (m >> lead) & 1 else 1, m))
        for m in ranked:
            slot = m >> 1
            core_copies[c, m] = remote(
                partial.at[rows(flip_mask(mate, m), c)],
                first.at[slot, c],
                core_send.at[c, slot],
                core_recv.at[c, slot],
                mate,
            )

    def stage(c, s):
        order = chip_order(c, bits)
        rest = order[s + 1 :] if s >= 0 else order
        base = sum(1 << (bits - 2 - k) for k in range(max(s, 0)))
        if s == 0:
            lead = order[0]
            ranked = sorted(every, key=lambda m: (0 if (m >> lead) & 1 else 1, m))
            for m in ranked:
                copy = core_copies[c, m]
                copy.wait_recv()
                slot = m >> 1
                total = first[slot, c].astype(f32) + partial[
                    rows(flip_mask(me, m), c)
                ].astype(f32)
                first[slot, c] = total.astype(first.dtype)
                if (m >> lead) & 1:
                    send_chip(c, s, m, rest, base)
        else:
            before = order[s:]
            last = sum(1 << (bits - 2 - k) for k in range(s - 1))
            for i, m in enumerate(masks_over(before)):
                chip_copies[c, s - 1, m].wait_recv()
                slot = m >> 1
                total = first[slot, c].astype(f32) + later[last + i, c].astype(f32)
                first[slot, c] = total.astype(first.dtype)
            for m in masks_over(rest):
                send_chip(c, s, m | (1 << order[s]), rest, base)

    def send_chip(c, s, m, rest, base):
        dim = chip_order(c, bits)[s]
        kept = m & ~(1 << dim)
        i = masks_over(rest).index(kept)
        chip_copies[c, s, kept] = remote(
            first.at[m >> 1, c],
            later.at[base + i, c],
            chip_send.at[c, base + i],
            chip_recv.at[c, base + i],
            flip(me, dim),
        )

    def total(c):
        s = bits - 1
        last = sum(1 << (bits - 2 - k) for k in range(s - 1))
        chip_copies[c, s - 1, 0].wait_recv()
        return first[0, c].astype(f32) + later[last, c].astype(f32)

    def finish():
        for copy in core_copies.values():
            copy.wait_send()
        for copy in chip_copies.values():
            copy.wait_send()

    return start, stage, total, finish


def scatter_scratch(n, chunks, sub, width):
    half = n // 2
    return [
        pltpu.VMEM((half, chunks, sub, width), bf16),
        pltpu.VMEM((max(half - 1, 1), chunks, sub, width), bf16),
        pltpu.SemaphoreType.DMA((chunks, half)),
        pltpu.SemaphoreType.DMA((chunks, half)),
        pltpu.SemaphoreType.DMA((chunks, half)),
        pltpu.SemaphoreType.DMA((chunks, half)),
    ]


def gather_kernel(n, chunks, *refs):
    x_ref, y_ref, xo_ref, yo_ref = refs[:4]
    sems = refs[4:8]
    own = refs[8]
    bits = n.bit_length() - 1
    me = lax.axis_index("col")
    width = x_ref.shape[1]
    sub = x_ref.shape[0] // chunks

    def columns(b):
        return pl.ds(pl.multiple_of(b * width, width), width)

    def pick(c):
        return (x_ref, xo_ref) if c < chunks else (y_ref, yo_ref)

    def source(c):
        return pick(c)[0].at[pl.ds((c % chunks) * sub, sub)]

    def place(b, c):
        return pick(c)[1].at[pl.ds((c % chunks) * sub, sub), columns(b)]

    locals_ = [
        pltpu.make_async_copy(x_ref, xo_ref.at[:, columns(me)], own.at[0]),
        pltpu.make_async_copy(y_ref, yo_ref.at[:, columns(me)], own.at[1]),
    ]
    for copy in locals_:
        copy.start()
    greet([flip(me, d) for d in range(bits)])
    stage, finish = gather_steps(me, bits, 2 * chunks, source, place, sems)
    for s in range(bits):
        for c in range(2 * chunks):
            stage(c, s)
    finish()
    for copy in locals_:
        copy.wait()


def gather_features(x, y, n, collective_id):
    chunks = 2
    vmem = pl.BlockSpec(memory_space=pltpu.VMEM)
    shape = jax.ShapeDtypeStruct((x.shape[0], n * x.shape[1]), x.dtype)
    return pl.pallas_call(
        functools.partial(gather_kernel, n, chunks),
        out_shape=(shape, shape),
        in_specs=[vmem, vmem],
        out_specs=(vmem, vmem),
        scratch_shapes=gather_sems(n, 2 * chunks) + [pltpu.SemaphoreType.DMA((2,))],
        compiler_params=pltpu.CompilerParams(
            collective_id=collective_id, has_side_effects=True, vmem_limit_bytes=40 << 20
        ),
        cost_estimate=pl.CostEstimate(flops=0, bytes_accessed=100 << 20, transcendentals=0),
    )(x, y)


def row_stats(values):
    average = jnp.mean(values, axis=1, keepdims=True)
    centred = values - average
    variance = jnp.mean(centred * centred, axis=1, keepdims=True)
    inverse = lax.rsqrt(variance + epsilon)
    return centred * inverse, inverse


def norm_back(upstream, xhat, inverse, gain):
    scaled = upstream * gain
    mean_scaled = jnp.mean(scaled, axis=1, keepdims=True)
    mean_product = jnp.mean(scaled * xhat, axis=1, keepdims=True)
    return inverse * (scaled - mean_scaled - xhat * mean_product)


def forward_kernel(n, chunks, *refs):
    partial, x_ref, bias, gain, shift, middle, normed = refs[:7]
    first, later = refs[7:9]
    scatter_sems, sems = refs[9:13], refs[13:17]
    x_rows, x_sem = refs[17:19]
    bits = n.bit_length() - 1
    me = lax.axis_index("col")
    block = partial.shape[0] // n
    sub = block // chunks

    def rows(b, c):
        return pl.ds(pl.multiple_of(b * block + c * sub, sub), sub)

    def place(b, c):
        return normed.at[rows(b, c)]

    x_copy = pltpu.make_async_copy(
        x_ref.at[pl.ds(pl.multiple_of(me * block, block), block)], x_rows, x_sem
    )
    x_copy.start()
    greet([flip(me, d) for d in range(bits)])
    start, add, total, end_scatter = scatter_steps(
        me, bits, chunks, partial, rows, first, later, scatter_sems
    )
    stage, end_gather = gather_steps(me, bits, chunks, lambda c: place(me, c), place, sems)
    for c in range(chunks):
        start(c)
    for s in range(bits - 1):
        for c in range(chunks):
            add(c, s)
    x_copy.wait()
    for c in range(chunks):
        here = pl.ds(c * sub, sub)
        values = x_rows[here].astype(f32) + (total(c) + bias[...])
        middle[here] = values
        xhat, _ = row_stats(values)
        normed[rows(me, c)] = (xhat * gain[...] + shift[...]).astype(bf16)
        stage(c, 0)
    for s in range(1, bits):
        for c in range(chunks):
            stage(c, s)
    end_scatter()
    end_gather()


def forward_join(partial, x_full, bias, gain, shift, n, collective_id):
    chunks = 2
    tokens, width = partial.shape
    block = tokens // n
    vmem = pl.BlockSpec(memory_space=pltpu.VMEM)
    return pl.pallas_call(
        functools.partial(forward_kernel, n, chunks),
        out_shape=(
            jax.ShapeDtypeStruct((block, width), f32),
            jax.ShapeDtypeStruct((tokens, width), bf16),
        ),
        in_specs=[vmem, pl.BlockSpec(memory_space=pl.ANY), vmem, vmem, vmem],
        out_specs=(vmem, vmem),
        scratch_shapes=scatter_scratch(n, chunks, block // chunks, width)
        + gather_sems(n, chunks)
        + [pltpu.VMEM((block, width), bf16), pltpu.SemaphoreType.DMA],
        compiler_params=pltpu.CompilerParams(
            collective_id=collective_id, has_side_effects=True, vmem_limit_bytes=40 << 20
        ),
        cost_estimate=pl.CostEstimate(flops=0, bytes_accessed=150 << 20, transcendentals=0),
    )(partial, x_full, bias, gain, shift)


def backward_kernel(n, chunks, *refs):
    partial, middle, g_ref, gain, middle_grad, sums, proj = refs[:7]
    first, later = refs[7:9]
    scatter_sems, sems = refs[9:13], refs[13:17]
    g_rows, g_sem = refs[17:19]
    bits = n.bit_length() - 1
    me = lax.axis_index("col")
    block = partial.shape[0] // n
    sub = block // chunks

    def rows(b, c):
        return pl.ds(pl.multiple_of(b * block + c * sub, sub), sub)

    def place(b, c):
        return proj.at[rows(b, c)]

    g_copy = pltpu.make_async_copy(
        g_ref.at[pl.ds(pl.multiple_of(me * block, block), block)], g_rows, g_sem
    )
    g_copy.start()
    greet([flip(me, d) for d in range(bits)])
    start, add, total, end_scatter = scatter_steps(
        me, bits, chunks, partial, rows, first, later, scatter_sems
    )
    stage, end_gather = gather_steps(me, bits, chunks, lambda c: place(me, c), place, sems)
    for c in range(chunks):
        start(c)
    for s in range(bits - 1):
        for c in range(chunks):
            add(c, s)
    g_copy.wait()
    sums[...] = jnp.zeros_like(sums)
    for c in range(chunks):
        here = pl.ds(c * sub, sub)
        xhat, inverse = row_stats(middle[here])
        upstream = total(c)
        grad = g_rows[here].astype(f32) + norm_back(upstream, xhat, inverse, gain[...])
        middle_grad[here] = grad
        low = grad.astype(bf16)
        proj[rows(me, c)] = low
        stage(c, 0)
        sums[0:1] += jnp.sum(upstream * xhat, axis=0, keepdims=True)
        sums[1:2] += jnp.sum(upstream, axis=0, keepdims=True)
        sums[2:3] += jnp.sum(low.astype(f32), axis=0, keepdims=True)
    for s in range(1, bits):
        for c in range(chunks):
            stage(c, s)
    end_scatter()
    end_gather()


def backward_join(partial, middle, gradient, gain, n, collective_id):
    chunks = 2
    tokens, width = partial.shape
    block = tokens // n
    vmem = pl.BlockSpec(memory_space=pltpu.VMEM)
    return pl.pallas_call(
        functools.partial(backward_kernel, n, chunks),
        out_shape=(
            jax.ShapeDtypeStruct((block, width), f32),
            jax.ShapeDtypeStruct((8, width), f32),
            jax.ShapeDtypeStruct((tokens, width), bf16),
        ),
        in_specs=[vmem, vmem, pl.BlockSpec(memory_space=pl.ANY), vmem],
        out_specs=(vmem, vmem, vmem),
        scratch_shapes=scatter_scratch(n, chunks, block // chunks, width)
        + gather_sems(n, chunks)
        + [pltpu.VMEM((block, width), bf16), pltpu.SemaphoreType.DMA],
        compiler_params=pltpu.CompilerParams(
            collective_id=collective_id, has_side_effects=True, vmem_limit_bytes=40 << 20
        ),
        cost_estimate=pl.CostEstimate(flops=0, bytes_accessed=150 << 20, transcendentals=0),
    )(partial, middle, gradient, gain)


def exchange(me, n, staged, out, rows, send, recv, width):
    copies = []
    for i in range(1, n):
        peer = lax.rem(me + i, n)
        columns = pl.ds(pl.multiple_of(peer * width, width), width)
        copies.append(
            remote(staged.at[:, columns], out.at[rows], send.at[i], recv.at[i], peer)
        )
    return copies


def result_kernel(n, chunks, *refs):
    partial, middle, bias, out = refs[:4]
    first, later = refs[4:6]
    scatter_sems = refs[6:10]
    staged, send, recv, own = refs[10:14]
    bits = n.bit_length() - 1
    me = lax.axis_index("col")
    block = partial.shape[0] // n
    sub = block // chunks
    width = out.shape[1]

    def rows(b, c):
        return pl.ds(pl.multiple_of(b * block + c * sub, sub), sub)

    greet([lax.rem(me + i, n) for i in range(1, n)])
    start, add, total, end_scatter = scatter_steps(
        me, bits, chunks, partial, rows, first, later, scatter_sems
    )
    for c in range(chunks):
        start(c)
    for s in range(bits - 1):
        for c in range(chunks):
            add(c, s)
    copies, locals_ = [], []
    mine = pl.ds(pl.multiple_of(me * width, width), width)
    for c in range(chunks):
        here = pl.ds(c * sub, sub)
        staged[here] = (middle[here] + (total(c) + bias[...])).astype(bf16)
        copies += exchange(
            me, n, staged.at[here], out, rows(me, c), send.at[c], recv.at[c], width
        )
        local = pltpu.make_async_copy(staged.at[here, mine], out.at[rows(me, c)], own.at[c])
        local.start()
        locals_.append(local)
    end_scatter()
    for copy in copies + locals_:
        copy.wait()


def result_join(partial, middle, bias, n, collective_id):
    chunks = 2
    tokens, width = partial.shape
    block = tokens // n
    vmem = pl.BlockSpec(memory_space=pltpu.VMEM)
    return pl.pallas_call(
        functools.partial(result_kernel, n, chunks),
        out_shape=jax.ShapeDtypeStruct((tokens, width // n), bf16),
        in_specs=[vmem, vmem, vmem],
        out_specs=vmem,
        scratch_shapes=scatter_scratch(n, chunks, block // chunks, width)
        + [
            pltpu.VMEM((block, width), bf16),
            pltpu.SemaphoreType.DMA((chunks, n)),
            pltpu.SemaphoreType.DMA((chunks, n)),
            pltpu.SemaphoreType.DMA((chunks,)),
        ],
        compiler_params=pltpu.CompilerParams(
            collective_id=collective_id, has_side_effects=True, vmem_limit_bytes=40 << 20
        ),
        cost_estimate=pl.CostEstimate(flops=0, bytes_accessed=100 << 20, transcendentals=0),
    )(partial, middle, bias)


def input_kernel(n, chunks, *refs):
    partial, x_ref, middle_grad, gain, sums, out, sums_out = refs[:7]
    first, later = refs[7:9]
    scatter_sems = refs[9:13]
    staged, send, recv, own, x_rows, x_sem = refs[13:19]
    vectors, landed, vec_send, vec_recv, vec_own = refs[19:24]
    bits = n.bit_length() - 1
    me = lax.axis_index("col")
    block = partial.shape[0] // n
    sub = block // chunks
    width = out.shape[1]

    def rows(b, c):
        return pl.ds(pl.multiple_of(b * block + c * sub, sub), sub)

    x_copy = pltpu.make_async_copy(
        x_ref.at[pl.ds(pl.multiple_of(me * block, block), block)], x_rows, x_sem
    )
    x_copy.start()
    greet([lax.rem(me + i, n) for i in range(1, n)])
    start, add, total, end_scatter = scatter_steps(
        me, bits, chunks, partial, rows, first, later, scatter_sems
    )
    for c in range(chunks):
        start(c)
    for s in range(bits - 1):
        for c in range(chunks):
            add(c, s)
    x_copy.wait()
    vectors[...] = sums[...]
    copies, locals_ = [], []
    mine = pl.ds(pl.multiple_of(me * width, width), width)
    for c in range(chunks):
        here = pl.ds(c * sub, sub)
        xhat, inverse = row_stats(x_rows[here].astype(f32))
        upstream = total(c)
        staged[here] = middle_grad[here] + norm_back(upstream, xhat, inverse, gain[...])
        vectors[3:4] += jnp.sum(upstream * xhat, axis=0, keepdims=True)
        vectors[4:5] += jnp.sum(upstream, axis=0, keepdims=True)
        copies += exchange(
            me, n, staged.at[here], out, rows(me, c), send.at[c], recv.at[c], width
        )
        local = pltpu.make_async_copy(staged.at[here, mine], out.at[rows(me, c)], own.at[c])
        local.start()
        locals_.append(local)
    vec = []
    for i in range(1, n):
        peer = lax.rem(me + i, n)
        columns = pl.ds(pl.multiple_of(peer * width, width), width)
        vec.append(
            remote(vectors.at[:, columns], landed.at[i], vec_send.at[i], vec_recv.at[i], peer)
        )
    local = pltpu.make_async_copy(vectors.at[:, mine], landed.at[0], vec_own)
    local.start()
    local.wait()
    for copy in vec:
        copy.wait()
    summed = landed[0]
    for i in range(1, n):
        summed = summed + landed[i]
    sums_out[...] = summed
    end_scatter()
    for copy in copies + locals_:
        copy.wait()


def input_join(partial, x_full, middle_grad, gain, sums, n, collective_id):
    chunks = 2
    tokens, width = partial.shape
    block = tokens // n
    vmem = pl.BlockSpec(memory_space=pltpu.VMEM)
    return pl.pallas_call(
        functools.partial(input_kernel, n, chunks),
        out_shape=(
            jax.ShapeDtypeStruct((tokens, width // n), f32),
            jax.ShapeDtypeStruct((8, width // n), f32),
        ),
        in_specs=[vmem, pl.BlockSpec(memory_space=pl.ANY), vmem, vmem, vmem],
        out_specs=(vmem, vmem),
        scratch_shapes=scatter_scratch(n, chunks, block // chunks, width)
        + [
            pltpu.VMEM((block, width), f32),
            pltpu.SemaphoreType.DMA((chunks, n)),
            pltpu.SemaphoreType.DMA((chunks, n)),
            pltpu.SemaphoreType.DMA((chunks,)),
            pltpu.VMEM((block, width), bf16),
            pltpu.SemaphoreType.DMA,
            pltpu.VMEM((8, width), f32),
            pltpu.VMEM((n, 8, width // n), f32),
            pltpu.SemaphoreType.DMA((n,)),
            pltpu.SemaphoreType.DMA((n,)),
            pltpu.SemaphoreType.DMA,
        ],
        compiler_params=pltpu.CompilerParams(
            collective_id=collective_id, has_side_effects=True, vmem_limit_bytes=40 << 20
        ),
        cost_estimate=pl.CostEstimate(flops=0, bytes_accessed=120 << 20, transcendentals=0),
    )(partial, x_full, middle_grad, gain, sums)


def ring(values):
    n = lax.axis_size("row")
    return lax.ppermute(values, "row", [(i, (i + 1) % n) for i in range(n)])


def gather_ring(piece, axis):
    n = lax.axis_size("row")
    me = lax.axis_index("row")
    size = piece.shape[axis]
    shape = list(piece.shape)
    shape[axis] = n * size
    whole = jnp.zeros(shape, piece.dtype)
    for hop in range(n):
        owner = lax.rem(me - hop + n, n)
        whole = lax.dynamic_update_slice_in_dim(whole, piece, owner * size, axis)
        if hop < n - 1:
            piece = ring(piece)
    return whole


def scatter_ring(part):
    n = lax.axis_size("row")
    me = lax.axis_index("row")
    moving = part(lax.rem(me + n - 1, n)).astype(bf16)
    for hop in range(1, n):
        moving = ring(moving)
        term = part(lax.rem(me + 2 * n - 1 - hop, n))
        summed = moving.astype(f32) + term
        moving = summed.astype(bf16)
    return summed


def attend_scores(query_rows, key_rows, slopes):
    length = query_rows.shape[0]
    position = jnp.arange(length)
    distance = (position[None, :] - position[:, None]).astype(f32)
    raw_scores = jnp.einsum(
        "qhd,khd->hqk", query_rows, key_rows, preferred_element_type=f32
    ) * (1.0 / math.sqrt(query_rows.shape[2]))
    raw_scores = raw_scores + slopes[:, None, None] * distance[None]
    return jnp.where(distance[None] <= 0, raw_scores, -jnp.inf)


def attend_forward(sequence, slopes):
    query_rows, key_rows, value_rows = sequence
    scores = attend_scores(query_rows, key_rows, slopes)
    row_max = jnp.max(scores, axis=2, keepdims=True)
    exponent = jnp.exp(scores - row_max)
    summed = jnp.sum(exponent, axis=2, keepdims=True)
    weights = (exponent / summed).astype(bf16)
    result = jnp.einsum("hqk,khd->qhd", weights, value_rows, preferred_element_type=f32)
    return (result.astype(bf16), (row_max + jnp.log(summed))[:, :, 0])


def attend_backward(sequence, slopes):
    query_rows, key_rows, value_rows, result_grad, logsum = sequence
    score_scale = 1.0 / math.sqrt(query_rows.shape[2])
    probability = jnp.exp(attend_scores(query_rows, key_rows, slopes) - logsum[:, :, None])
    weights = probability.astype(bf16)
    value_grad = jnp.einsum("hqk,qhd->khd", weights, result_grad, preferred_element_type=f32)
    weight_grad = jnp.einsum(
        "qhd,khd->hqk", result_grad, value_rows, preferred_element_type=f32
    )
    row_inner = jnp.sum(probability * weight_grad, axis=2, keepdims=True)
    score_grad = (probability * (weight_grad - row_inner)).astype(bf16)
    query_grad = (
        jnp.einsum("hqk,khd->qhd", score_grad, key_rows, preferred_element_type=f32)
        * score_scale
    )
    key_grad = (
        jnp.einsum("hqk,qhd->khd", score_grad, query_rows, preferred_element_type=f32)
        * score_scale
    )
    return (query_grad.astype(bf16), key_grad.astype(bf16), value_grad.astype(bf16))


def per_device(
    inputs,
    norm1_gain,
    norm1_shift,
    query_weight,
    query_bias,
    key_weight,
    value_weight,
    value_bias,
    output_weight,
    output_bias,
    norm2_gain,
    norm2_shift,
    expand_weight,
    expand_bias,
    contract_weight,
    contract_bias,
    cotangent,
):
    cols = lax.axis_size("col")
    rows = lax.axis_size("row")
    row = lax.axis_index("row")
    tokens, width = inputs.shape
    heads_here = width // HEAD
    depth = query_weight.shape[0]
    hidden_width = expand_weight.shape[1]

    vectors = jnp.stack(
        [norm1_gain, norm1_shift, output_bias, norm2_gain, norm2_shift, contract_bias]
    )
    vectors = lax.all_gather(vectors, "col", axis=1, tiled=True)
    gain1, shift1, bias_o, gain2, shift2, bias_c = [vectors[i : i + 1] for i in range(6)]

    in_piece = jnp.concatenate(
        [query_weight.astype(bf16), key_weight.astype(bf16), value_weight.astype(bf16)], axis=1
    )
    in_copy = gather_ring(in_piece, 0)
    output_copy = gather_ring(output_weight.astype(bf16), 1)
    expand_copy = gather_ring(expand_weight.astype(bf16), 0)
    contract_copy = gather_ring(contract_weight.astype(bf16), 1)

    input_rows, down_rows = gather_features(inputs, cotangent, cols, 1)
    xhat1, _ = row_stats(input_rows.astype(f32))
    first_rows = (xhat1 * gain1 + shift1).astype(bf16)

    in_bias = jnp.concatenate([query_bias, jnp.zeros_like(query_bias), value_bias])
    projected = (product(first_rows, in_copy) + in_bias).astype(bf16)
    query_rows = projected[:, :width]
    key_rows = projected[:, width : 2 * width]
    value_rows = projected[:, 2 * width :]
    head_index = lax.axis_index("col") * heads_here + jnp.arange(heads_here)
    slopes = jnp.exp2(-8.0 * (head_index + 1).astype(f32) / HEADS)

    def by_sequence(matrix):
        return matrix.reshape(tokens // LEN, LEN, heads_here, HEAD)

    attended, logsum = lax.map(
        lambda sequence: attend_forward(sequence, slopes),
        (by_sequence(query_rows), by_sequence(key_rows), by_sequence(value_rows)),
    )
    attended = attended.reshape(tokens, width)
    branch = product(attended, output_copy).astype(bf16)
    middle, second_rows = forward_join(branch, input_rows, bias_o, gain2, shift2, cols, 2)

    expanded = product(second_rows, expand_copy) + expand_bias
    hidden = gelu_tanh(expanded).astype(bf16)

    def contract_part(chunk):
        piece = lax.dynamic_slice_in_dim(down_rows, chunk * depth, depth, 1)
        return token_sum(hidden, piece)

    contract_weight_grad = scatter_ring(contract_part)
    contracted = product(hidden, contract_copy).astype(bf16)
    outputs = result_join(contracted, middle, bias_c, cols, 3)

    hidden_grad = product_back(down_rows, contract_copy)
    _, gelu_back = jax.vjp(gelu_tanh, expanded)
    expanded_grad = gelu_back(hidden_grad)[0].astype(bf16)

    def expand_part(chunk):
        piece = lax.dynamic_slice_in_dim(second_rows, chunk * depth, depth, 1)
        return token_sum(piece, expanded_grad)

    expand_weight_grad = scatter_ring(expand_part)
    second_grad = product_back(expanded_grad, expand_copy).astype(bf16)
    middle_grad, sums, proj_rows = backward_join(second_grad, middle, down_rows, gain2, cols, 4)

    def output_part(chunk):
        piece = lax.dynamic_slice_in_dim(proj_rows, chunk * depth, depth, 1)
        return token_sum(attended, piece)

    output_weight_grad = scatter_ring(output_part)
    attended_grad = product_back(proj_rows, output_copy).astype(bf16)
    query_grad, key_grad, value_grad = lax.map(
        lambda sequence: attend_backward(sequence, slopes),
        (
            by_sequence(query_rows),
            by_sequence(key_rows),
            by_sequence(value_rows),
            by_sequence(attended_grad),
            logsum,
        ),
    )
    query_grad = query_grad.reshape(tokens, width)
    key_grad = key_grad.reshape(tokens, width)
    value_grad = value_grad.reshape(tokens, width)
    in_grad = jnp.concatenate([query_grad, key_grad, value_grad], axis=1)

    def in_part(chunk):
        piece = lax.dynamic_slice_in_dim(first_rows, chunk * depth, depth, 1)
        return token_sum(piece, in_grad)

    in_weight_grad = scatter_ring(in_part)
    first_grad = product_back(in_grad, in_copy).astype(bf16)
    input_grad, sums = input_join(first_grad, input_rows, middle_grad, gain1, sums, cols, 5)

    query_bias_grad = jnp.sum(query_grad.astype(f32), axis=0)
    value_bias_grad = jnp.sum(value_grad.astype(f32), axis=0)
    contract_bias_grad = jnp.sum(cotangent.astype(f32), axis=0)
    expand_bias_grad = jnp.sum(expanded_grad.astype(f32), axis=0)
    small = jnp.concatenate(
        [
            sums[:5],
            query_bias_grad[None],
            value_bias_grad[None],
            contract_bias_grad[None],
        ]
    )
    share = width // rows
    small = small.reshape(8, rows, share).transpose(1, 0, 2)
    wide = expand_bias_grad.reshape(rows, hidden_width // rows)
    packed = jnp.concatenate([small.reshape(rows, 8 * share), wide], axis=1)
    packed = lax.psum_scatter(packed, "row", scatter_dimension=0, tiled=True)[0]
    vector = packed[: 8 * share].reshape(8, share)
    expand_bias_grad = packed[8 * share :]
    return (
        outputs,
        input_grad,
        vector[3],
        vector[4],
        in_weight_grad[:, :width],
        vector[5],
        in_weight_grad[:, width : 2 * width],
        in_weight_grad[:, 2 * width :],
        vector[6],
        output_weight_grad,
        vector[2],
        vector[0],
        vector[1],
        expand_weight_grad,
        expand_bias_grad,
        contract_weight_grad,
        vector[7],
    )


def solution(mesh):
    in_specs = (
        P("row", "col"),
        P("col"),
        P("col"),
        P("row", "col"),
        P("col"),
        P("row", "col"),
        P("row", "col"),
        P("col"),
        P("col", "row"),
        P("col"),
        P("col"),
        P("col"),
        P("row", "col"),
        P("col"),
        P("col", "row"),
        P("col"),
        P("row", "col"),
    )
    out_specs = (
        P("row", "col"),
        P("row", "col"),
        P(("col", "row")),
        P(("col", "row")),
        P("row", "col"),
        P(("col", "row")),
        P("row", "col"),
        P("row", "col"),
        P(("col", "row")),
        P("col", "row"),
        P(("col", "row")),
        P(("col", "row")),
        P(("col", "row")),
        P("row", "col"),
        P(("col", "row")),
        P("col", "row"),
        P(("col", "row")),
    )
    return jax.shard_map(
        per_device, mesh=mesh, in_specs=in_specs, out_specs=out_specs, check_vma=False
    )
```

```python
import functools
import math

import jax
import jax.numpy as jnp
from jax import lax
from jax.experimental import pallas as pl
from jax.experimental.pallas import tpu as pltpu
from jax.sharding import PartitionSpec as P

HEADS = 16
HEAD = 128
LEN = 1024

epsilon = 1e-05
MESH = pl.DeviceIdType.MESH
bf16 = jnp.bfloat16
f32 = jnp.float32


def flip(index, dim):
    step = 1 << dim
    bit = (index // step) % 2
    return index + (1 - 2 * bit) * step


def flip_mask(index, mask):
    dim = 0
    while mask >> dim:
        if (mask >> dim) & 1:
            index = flip(index, dim)
        dim += 1
    return index


def chip_order(chunk, bits):
    dims = list(range(1, bits))
    start = chunk % len(dims)
    return dims[start:] + dims[:start]


def masks_over(dims):
    masks = [0]
    for dim in dims:
        masks = masks + [m | (1 << dim) for m in masks]
    return masks


def remote(src, dst, send, recv, peer, axis="col"):
    return pltpu.make_async_remote_copy(
        src_ref=src,
        dst_ref=dst,
        send_sem=send,
        recv_sem=recv,
        device_id={axis: peer},
        device_id_type=MESH,
    )


def span(index, size):
    return pl.ds(pl.multiple_of(index * size, size), size)


def dot(a, b, ca, cb):
    return lax.dot_general(a, b, (((ca,), (cb,)), ((), ())), preferred_element_type=f32)


def row_stats(values):
    average = jnp.mean(values, axis=1, keepdims=True)
    centred = values - average
    variance = jnp.mean(centred * centred, axis=1, keepdims=True)
    inverse = lax.rsqrt(variance + epsilon)
    return centred * inverse, inverse


def norm_back(upstream, xhat, inverse, gain):
    scaled = upstream * gain
    mean_scaled = jnp.mean(scaled, axis=1, keepdims=True)
    mean_product = jnp.mean(scaled * xhat, axis=1, keepdims=True)
    return inverse * (scaled - mean_scaled - xhat * mean_product)


class Gather:
    def __init__(self, me, bits, chunks, place, sems, base=0):
        self.me, self.bits, self.chunks, self.place = me, bits, chunks, place
        self.chip_send, self.chip_recv, self.mate_send, self.mate_recv = sems
        self.base = base
        self.held = [[me] for _ in range(chunks)]
        self.waiting = [[] for _ in range(chunks)]
        self.mates, self.sent = [], []

    def stage(self, c, s):
        order = chip_order(c, self.bits)
        if s == 0:
            new, base = [self.me], 0
        else:
            for copy in self.waiting[c]:
                copy.wait_recv()
            base = len(self.held[c])
            new = [flip(b, order[s - 1]) for b in self.held[c]]
            self.held[c] = self.held[c] + new
        if s < self.bits - 1:
            copies = []
            for i, b in enumerate(self.held[c]):
                slot = (1 << s) - 1 + i
                home = self.place(b, c)
                copy = remote(
                    home,
                    home,
                    self.chip_send.at[self.base + c, slot],
                    self.chip_recv.at[self.base + c, slot],
                    flip(self.me, order[s]),
                )
                copy.start()
                copies.append(copy)
            self.waiting[c] = copies
            self.sent.extend(copies)
        for i, b in enumerate(new):
            home = self.place(b, c)
            copy = remote(
                home,
                home,
                self.mate_send.at[self.base + c, base + i],
                self.mate_recv.at[self.base + c, base + i],
                flip(self.me, 0),
            )
            copy.start()
            self.mates.append(copy)

    def all(self, s):
        for c in range(self.chunks):
            self.stage(c, s)

    def finish(self):
        for copy in self.sent:
            copy.wait_send()
        for copy in self.mates:
            copy.wait()


class Scatter:
    def __init__(self, me, bits, chunks, partial, rows, first, later, sems):
        self.me, self.bits, self.chunks = me, bits, chunks
        self.partial, self.rows, self.first, self.later = partial, rows, first, later
        self.core_send, self.core_recv, self.chip_send, self.chip_recv = sems
        self.core, self.chip = {}, {}

    def ranked(self, c):
        lead = chip_order(c, self.bits)[0]
        every = masks_over(list(range(1, self.bits)))
        return lead, sorted(every, key=lambda m: (0 if (m >> lead) & 1 else 1, m))

    def base(self, s):
        return sum(1 << (self.bits - 2 - k) for k in range(s))

    def start(self, c):
        mate = flip(self.me, 0)
        for m in self.ranked(c)[1]:
            slot = m >> 1
            copy = remote(
                self.partial.at[self.rows(flip_mask(mate, m), c)],
                self.first.at[slot, c],
                self.core_send.at[c, slot],
                self.core_recv.at[c, slot],
                mate,
            )
            copy.start()
            self.core[c, m] = copy

    def send(self, c, s, m):
        order = chip_order(c, self.bits)
        kept = m & ~(1 << order[s])
        i = self.base(s) + masks_over(order[s + 1 :]).index(kept)
        copy = remote(
            self.first.at[m >> 1, c],
            self.later.at[i, c],
            self.chip_send.at[c, i],
            self.chip_recv.at[c, i],
            flip(self.me, order[s]),
        )
        copy.start()
        self.chip[c, s, kept] = copy

    def add(self, c, s):
        order = chip_order(c, self.bits)
        if s == 0:
            lead, ranked = self.ranked(c)
            for m in ranked:
                self.core[c, m].wait_recv()
                slot = m >> 1
                mine = self.partial[self.rows(flip_mask(self.me, m), c)]
                total = self.first[slot, c].astype(f32) + mine.astype(f32)
                self.first[slot, c] = total.astype(bf16)
                if (m >> lead) & 1:
                    self.send(c, s, m)
        else:
            for i, m in enumerate(masks_over(order[s:])):
                self.chip[c, s - 1, m].wait_recv()
                slot = m >> 1
                here = self.later[self.base(s - 1) + i, c]
                total = self.first[slot, c].astype(f32) + here.astype(f32)
                self.first[slot, c] = total.astype(bf16)
            for m in masks_over(order[s + 1 :]):
                self.send(c, s, m | (1 << order[s]))

    def total(self, c):
        s = self.bits - 2
        self.chip[c, s, 0].wait_recv()
        return self.first[0, c].astype(f32) + self.later[self.base(s), c].astype(f32)

    def begin(self):
        for c in range(self.chunks):
            self.start(c)

    def all(self, s):
        for c in range(self.chunks):
            self.add(c, s)

    def finish(self):
        for copy in list(self.core.values()) + list(self.chip.values()):
            copy.wait_send()


QKV, OUT, UP, DOWN = range(4)
CHUNKS = 4
VMEM_LIMIT = 65024 << 10


def layer_kernel(n, ranks, *refs):
    (
        x_hbm, cot_hbm, q_hbm, k_hbm, v_hbm, o_hbm, up_hbm, down_hbm,
        vec_ref, in_bias, up_bias,
        out_hbm, xg_hbm, qg_hbm, kg_hbm, vg_hbm, og_hbm, upg_hbm, downg_hbm, small_ref,
        w_in, w_out, w_up, w_down, normed1, down_rows, buf_a, buf_b, first, later,
        qkv, attended, slope_grad, hidden, slots_down, slots_up,
        stage_a, stage_b, middle, middle_grad, x_own, logsum, kv_sum, vectors, sums,
        local_sums, up_sums, landed, row_landed,
        local_sem, gather_a, gather_b, gather_c, gather_d,
        scatter_a, scatter_b, scatter_c, scatter_d,
        z_send, z_recv, g_send, g_recv, vec_send, vec_recv, ex_send, ex_recv,
        row_send, row_recv, free_sem,
    ) = refs
    bits = n.bit_length() - 1
    me = lax.axis_index("col")
    row = lax.axis_index("row")
    tokens, width = normed1.shape
    share = width // n
    depth = width // ranks
    units = hidden.shape[1]
    block = tokens // n
    sub = block // CHUNKS
    heads_here = share // HEAD
    in_width = 3 * share
    in_grad = hidden.at[:, 0:in_width]
    score_scale = 1.0 / math.sqrt(HEAD)
    right, left = row + 1, row - 1
    has_left, has_right = row > 0, row < ranks - 1
    is_end = jnp.logical_or(row == 0, row == ranks - 1)

    def local(src, dst, i):
        copy = pltpu.make_async_copy(src, dst, local_sem.at[i])
        copy.start()
        return copy

    def rows(b, c):
        return pl.ds(pl.multiple_of(b * block + c * sub, sub), sub)

    mine = span(me, share)

    def z_block(k, b):
        if k == QKV:
            return w_in.at[span(b, depth)]
        if k == OUT:
            return w_out.at[:, span(b, depth)]
        if k == UP:
            return w_up.at[span(b, depth)]
        return w_down.at[:, span(b, depth)]

    def z_copy(k, way, hop):
        b = row - hop if way == 0 else row + hop
        peer = right if way == 0 else left
        return remote(
            z_block(k, b), z_block(k, b), z_send.at[k, way, hop], z_recv.at[k, way, hop],
            peer, "row",
        )

    def z_landing(k, way, hop):
        b = row - hop if way == 0 else row + hop
        return remote(
            z_block(k, b), z_block(k, b), z_send.at[k, way, hop - 1],
            z_recv.at[k, way, hop - 1], left if way == 0 else right, "row",
        )

    def z_own(k):
        @pl.when(has_right)
        def _():
            z_copy(k, 0, 0).start()

        @pl.when(has_left)
        def _():
            z_copy(k, 1, 0).start()

    def z_pass(k, hop):
        @pl.when(row >= hop)
        def _():
            z_landing(k, 0, hop).wait_recv()
            if hop < ranks - 1:

                @pl.when(has_right)
                def _():
                    z_copy(k, 0, hop).start()

        @pl.when(row + hop <= ranks - 1)
        def _():
            z_landing(k, 1, hop).wait_recv()
            if hop < ranks - 1:

                @pl.when(has_left)
                def _():
                    z_copy(k, 1, hop).start()

    def z_sent(k):
        for hop in range(ranks - 1):

            @pl.when(jnp.logical_and(row >= hop, has_right))
            def _():
                z_copy(k, 0, hop).wait_send()

            @pl.when(jnp.logical_and(row + hop <= ranks - 1, has_left))
            def _():
                z_copy(k, 1, hop).wait_send()

    def slot(g, s):
        if g == DOWN:
            return slots_down.at[s]
        if g == UP:
            return slots_up.at[s]
        if g == OUT:
            return w_down.at[
                pl.ds(pl.multiple_of(depth + (s // ranks) * share, share), share),
                span(lax.rem(s, ranks), depth),
            ]
        return w_up.at[span(s, depth), 0:in_width]

    def last_slot(g):
        if g == QKV:
            return w_down.at[0:depth, 0:in_width]
        return slot(g, ranks)

    def term(g, c, write):
        if g == DOWN:
            tile = min(256, units)

            def step(i, _):
                value = dot(hidden[:, span(i, tile)], down_rows[:, span(c, depth)], 0, 0)
                write(span(i, tile), slice(0, depth), value)
                return 0

            lax.fori_loop(0, units // tile, step, 0)
        elif g == UP:
            tile = min(512, units)

            def step(j, _):
                value = dot(buf_a[:, span(c, depth)], slope_grad[:, span(j, tile)], 0, 0)
                write(slice(0, depth), span(j, tile), value)
                return 0

            lax.fori_loop(0, units // tile, step, 0)
        elif g == OUT:
            write(slice(0, share), slice(0, depth), dot(attended[...], down_rows[:, span(c, depth)], 0, 0))
        else:

            def step(j, _):
                value = dot(normed1[:, span(c, depth)], hidden[:, span(j, share)], 0, 0)
                write(slice(0, depth), span(j, share), value)
                return 0

            lax.fori_loop(0, 3, step, 0)

    def chunk_at(k):
        low = row < ranks // 2
        up_count = ranks - 1 - row
        from_low = jnp.where(k < up_count, ranks - 1 - k, k - up_count)
        from_high = jnp.where(k < row, k, ranks - 1 - (k - row))
        return jnp.where(low, from_low, from_high)

    def g_copy(g, c, way, to_owner=False):
        src = slot(g, c)
        dst = last_slot(g) if to_owner else slot(g, c)
        sem = g_recv.at[g, ranks] if to_owner else g_recv.at[g, c]
        return remote(src, dst, g_send.at[g, c], sem, right if way == 0 else left, "row")

    def g_start(g, c):
        @pl.when(c > row)
        def _():
            g_copy(g, c, 0).start()

        @pl.when(jnp.logical_and(c < row, c == left))
        def _():
            g_copy(g, c, 1, True).start()

        @pl.when(jnp.logical_and(c < row, c != left))
        def _():
            g_copy(g, c, 1).start()

    def g_first(g):
        @pl.when(is_end)
        def _():
            def step(k, _):
                c = chunk_at(k)
                here = slot(g, c)

                def write(r, q, value):
                    here[r, q] = value.astype(bf16)

                term(g, c, write)
                g_start(g, c)
                return 0

            lax.fori_loop(0, ranks - 1, step, 0)

    def g_pass(g, k):
        @pl.when(jnp.logical_not(is_end))
        def _():
            c = chunk_at(k)
            here = slot(g, c)
            g_copy(g, c, 0).wait_recv()

            def write(r, q, value):
                here[r, q] = (here[r, q].astype(f32) + value).astype(bf16)

            term(g, c, write)
            g_start(g, c)

    def g_own(g, write_out):
        here, other = slot(g, row), last_slot(g)

        @pl.when(has_left)
        def _():
            g_copy(g, row, 0).wait_recv()

        @pl.when(jnp.logical_not(has_left))
        def _():
            here[...] = jnp.zeros(here.shape, bf16)

        @pl.when(has_right)
        def _():
            g_copy(g, row, 1, True).wait_recv()

        @pl.when(jnp.logical_not(has_right))
        def _():
            other[...] = jnp.zeros(other.shape, bf16)

        def write(r, q, value):
            write_out(r, q, value + here[r, q].astype(f32) + other[r, q].astype(f32))

        term(g, row, write)

    def g_sent(g):
        for k in range(ranks - 1):
            g_copy(g, chunk_at(k), 0).wait_send()

    x_load = local(x_hbm, normed1.at[:, mine], 0)
    in_loads = [
        local(hbm, stage_a.at[0:depth, i * share : (i + 1) * share], 1 + i)
        for i, hbm in enumerate((q_hbm, k_hbm, v_hbm))
    ]
    o_load = local(o_hbm, stage_b.at[0:share, :], 4)
    cot_load = local(cot_hbm, down_rows.at[:, mine], 5)

    barrier = pltpu.get_barrier_semaphore()
    for i in range(1, n):
        pl.semaphore_signal(
            barrier, inc=1, device_id={"col": lax.rem(me + i, n)}, device_id_type=MESH
        )
    for i in range(1, ranks):
        pl.semaphore_signal(
            barrier, inc=1, device_id={"row": lax.rem(row + i, ranks)}, device_id_type=MESH
        )
    pl.semaphore_wait(barrier, n - 1 + ranks - 1)

    gather_sems = (gather_a, gather_b, gather_c, gather_d)
    scatter_sems = (scatter_a, scatter_b, scatter_c, scatter_d)
    half = tokens // 2

    def feature_place(ref):
        def place(b, c):
            return ref.at[pl.ds(c * half, half), span(b, share)]

        return place

    gather_x = Gather(me, bits, 2, feature_place(normed1), gather_sems)
    gather_g = Gather(me, bits, 2, feature_place(down_rows), gather_sems, 2)
    x_load.wait()
    gather_x.all(0)
    vectors[:, mine] = vec_ref[...]
    vec_copies = []
    for i in range(1, n):
        copy = remote(
            vectors.at[:, mine], vectors.at[:, mine], vec_send.at[i], vec_recv.at[i],
            lax.rem(me + i, n),
        )
        copy.start()
        vec_copies.append(copy)
    for copy in in_loads:
        copy.wait()
    w_in[span(row, depth)] = stage_a[:, 0:in_width].astype(bf16)
    z_own(QKV)
    up_load = local(up_hbm, stage_a, 1)
    o_load.wait()
    w_out[:, span(row, depth)] = stage_b[0:share, :].astype(bf16)
    down_load = local(down_hbm, stage_b, 2)
    cot_load.wait()
    local_sums[7:8] = jnp.sum(down_rows[:, mine].astype(f32), axis=0, keepdims=True)
    gather_x.all(1)
    up_load.wait()
    w_up[span(row, depth)] = stage_a[...].astype(bf16)
    down_load.wait()
    w_down[:, span(row, depth)] = stage_b[...].astype(bf16)
    for s in range(2, bits):
        gather_x.all(s)
    gather_g.all(0)
    gather_x.finish()
    for copy in vec_copies:
        copy.wait_recv()
    z_pass(QKV, 1)
    x_own[...] = normed1[span(me, block)]

    def norm_step(i, _):
        here = span(i, 64)
        xhat, _ = row_stats(normed1[here].astype(f32))
        normed1[here] = (xhat * vectors[0:1] + vectors[1:2]).astype(bf16)
        return 0

    lax.fori_loop(0, tokens // 64, norm_step, 0)
    for s in range(1, bits - 1):
        gather_g.all(s)
    for hop in range(2, ranks - 1):
        z_pass(QKV, hop)
    z_own(OUT)
    z_own(UP)
    gather_g.all(bits - 1)
    gather_g.finish()
    z_pass(QKV, ranks - 1)

    def qkv_step(j, _):
        columns = span(j, share)
        qkv[:, columns] = (dot(normed1[...], w_in[:, columns], 1, 0) + in_bias[:, columns]).astype(bf16)
        return 0

    lax.fori_loop(0, 3, qkv_step, 0)
    z_pass(OUT, 1)

    tile = 256

    def slope_of(h):
        number = jnp.full((1, 1), me * heads_here + h + 1, jnp.int32).astype(f32)
        return jnp.exp2(-8.0 / HEADS * number)

    def blocks(h):
        for start in range(0, tokens, LEN):
            for i in range(LEN // tile):
                seen = (i + 1) * tile
                yield slice(start + i * tile, start + seen), slice(start, start + seen), i * tile

    def scores(h, q_rows, k_rows, offset):
        q_columns = slice(h * HEAD, (h + 1) * HEAD)
        k_columns = slice(share + h * HEAD, share + (h + 1) * HEAD)
        raw = dot(qkv[q_rows, q_columns], qkv[k_rows, k_columns], 1, 1) * score_scale
        shape = raw.shape
        distance = lax.broadcasted_iota(jnp.int32, shape, 1) - (
            lax.broadcasted_iota(jnp.int32, shape, 0) + offset
        )
        raw = raw + slope_of(h) * distance.astype(f32)
        return jnp.where(distance <= 0, raw, -jnp.inf)

    def attend(h):
        v_columns = slice(2 * share + h * HEAD, 2 * share + (h + 1) * HEAD)
        for q_rows, k_rows, offset in blocks(h):
            s = scores(h, q_rows, k_rows, offset)
            top = jnp.max(s, axis=1, keepdims=True)
            exponent = jnp.exp(s - top)
            total = jnp.sum(exponent, axis=1, keepdims=True)
            weights = (exponent / total).astype(bf16)
            attended[q_rows, h * HEAD : (h + 1) * HEAD] = dot(
                weights, qkv[k_rows, v_columns], 1, 0
            ).astype(bf16)
            logsum[q_rows, h : h + 1] = top + jnp.log(total)

    for h in range(heads_here):
        attend(h)
        if h == 0:
            for hop in range(2, ranks - 1):
                z_pass(OUT, hop)
    z_pass(OUT, ranks - 1)

    column_tile = 256

    def branch_step(j, _):
        columns = span(j, column_tile)
        buf_b[:, columns] = dot(attended[...], w_out[:, columns], 1, 0).astype(bf16)
        return 0

    lax.fori_loop(0, width // column_tile, branch_step, 0)

    def scatter_of(partial):
        return Scatter(me, bits, CHUNKS, partial, rows, first, later, scatter_sems)

    def gather_of(ref):
        return Gather(me, bits, CHUNKS, lambda b, c: ref.at[rows(b, c)], gather_sems)

    scatter = scatter_of(buf_b)
    gather = gather_of(buf_a)
    scatter.begin()
    for s in range(bits - 1):
        scatter.all(s)
    z_pass(UP, 1)
    for c in range(CHUNKS):
        here = pl.ds(c * sub, sub)
        values = x_own[here].astype(f32) + (scatter.total(c) + vectors[2:3])
        middle[here] = values
        xhat, _ = row_stats(values)
        buf_a[rows(me, c)] = (xhat * vectors[3:4] + vectors[4:5]).astype(bf16)
        gather.stage(c, 0)
    for s in range(1, bits - 1):
        gather.all(s)
    scatter.finish()
    gather.all(bits - 1)
    for hop in range(2, ranks - 1):
        z_pass(UP, hop)
    z_own(DOWN)
    gather.finish()
    z_pass(UP, ranks - 1)

    row_tile = 512

    def up_step(t, _):
        here = span(lax.rem(t, tokens // row_tile), row_tile)
        columns = span(t // (tokens // row_tile), column_tile)
        u = dot(buf_a[here], w_up[:, columns], 1, 0) + up_bias[:, columns]
        square = u * u
        inner = jnp.tanh(0.7978845608 * (u + 0.044715 * (u * square)))
        outer = 0.5 * (1.0 + inner)
        hidden[here, columns] = (u * outer).astype(bf16)
        slope = outer + 0.5 * u * (1.0 - inner * inner) * (
            0.7978845608 * (1.0 + 3.0 * 0.044715 * square)
        )
        slope_grad[here, columns] = slope.astype(bf16)
        return 0

    lax.fori_loop(0, (tokens // row_tile) * (units // column_tile), up_step, 0)
    g_first(DOWN)
    z_pass(DOWN, 1)
    g_pass(DOWN, 0)
    for hop in range(2, ranks):
        z_pass(DOWN, hop)
        if hop - 1 < ranks - 1:
            g_pass(DOWN, hop - 1)

    def expanded_step(t, _):
        here = span(lax.rem(t, tokens // row_tile), row_tile)
        columns = span(t // (tokens // row_tile), column_tile)
        grad = dot(down_rows[here], w_down[columns], 1, 1)
        low = (grad * slope_grad[here, columns].astype(f32)).astype(bf16)
        slope_grad[here, columns] = low
        up_sums[:, columns] += jnp.sum(low.astype(f32), axis=0, keepdims=True)
        return 0

    up_sums[...] = jnp.zeros(up_sums.shape, f32)

    lax.fori_loop(0, (tokens // row_tile) * (units // column_tile), expanded_step, 0)
    g_first(UP)

    def second_step(t, _):
        here = span(lax.rem(t, tokens // row_tile), row_tile)
        columns = span(t // (tokens // row_tile), column_tile)
        buf_b[here, columns] = dot(slope_grad[here], w_up[columns], 1, 1).astype(bf16)
        return 0

    lax.fori_loop(0, (tokens // row_tile) * (width // column_tile), second_step, 0)
    def keep_down(r, q, value):
        stage_b[r, q] = value

    g_own(DOWN, keep_down)
    down_store = local(stage_b, downg_hbm, 0)
    scatter = scatter_of(buf_b)
    gather = gather_of(down_rows)
    scatter.begin()
    scatter.all(0)

    g_pass(UP, 0)
    for s in range(1, bits - 1):
        scatter.all(s)
    sums[...] = jnp.zeros(sums.shape, f32)
    for c in range(CHUNKS):
        here = pl.ds(c * sub, sub)
        xhat, inverse = row_stats(middle[here])
        upstream = scatter.total(c)
        grad = down_rows[rows(me, c)].astype(f32) + norm_back(upstream, xhat, inverse, vectors[3:4])
        middle_grad[here] = grad
        low = grad.astype(bf16)
        down_rows[rows(me, c)] = low
        gather.stage(c, 0)
        sums[0:1] += jnp.sum(upstream * xhat, axis=0, keepdims=True)
        sums[1:2] += jnp.sum(upstream, axis=0, keepdims=True)
        sums[2:3] += jnp.sum(low.astype(f32), axis=0, keepdims=True)
    for s in range(1, bits - 1):
        gather.all(s)
    scatter.finish()

    def contract_step(t, _):
        here = span(lax.rem(t, tokens // row_tile), row_tile)
        columns = span(t // (tokens // row_tile), column_tile)
        buf_b[here, columns] = dot(hidden[here], w_down[:, columns], 1, 0).astype(bf16)
        return 0

    lax.fori_loop(0, (tokens // row_tile) * (width // column_tile), contract_step, 0)
    for k in range(4):
        z_sent(k)

    @pl.when(has_right)
    def _():
        pl.semaphore_signal(free_sem, inc=1, device_id={"row": right}, device_id_type=MESH)

    @pl.when(has_left)
    def _():
        pl.semaphore_signal(free_sem, inc=1, device_id={"row": left}, device_id_type=MESH)

    gather.all(bits - 1)
    for k in range(1, ranks - 1):
        g_pass(UP, k)
    gather.finish()

    scatter = scatter_of(buf_b)
    scatter.begin()
    pl.semaphore_wait(free_sem, has_left.astype(jnp.int32) + has_right.astype(jnp.int32))
    g_first(OUT)

    def attended_step(i, _):
        here = span(i, row_tile)
        value = dot(down_rows[here], w_out[...], 1, 1).astype(bf16)
        hidden[here, in_width : in_width + share] = value
        return 0

    lax.fori_loop(0, tokens // row_tile, attended_step, 0)
    down_store.wait()
    if kv_sum.shape[1] == LEN:
        key_sum, value_sum = kv_sum.at[0], kv_sum.at[1]
    else:
        key_sum, value_sum = stage_b.at[:, 0:HEAD], stage_b.at[:, HEAD : 2 * HEAD]

    def attend_back(h):
        q_columns = slice(h * HEAD, (h + 1) * HEAD)
        k_columns = slice(share + h * HEAD, share + (h + 1) * HEAD)
        v_columns = slice(2 * share + h * HEAD, 2 * share + (h + 1) * HEAD)
        d_columns = slice(in_width + h * HEAD, in_width + (h + 1) * HEAD)
        for start in range(0, tokens, LEN):
            sequence = slice(start, start + LEN)
            key_sum[0:LEN] = jnp.zeros((LEN, HEAD), f32)
            value_sum[0:LEN] = jnp.zeros((LEN, HEAD), f32)
            for i in range(LEN // tile):
                seen = (i + 1) * tile
                q_rows = slice(start + i * tile, start + seen)
                k_rows = slice(start, start + seen)
                s = scores(h, q_rows, k_rows, i * tile)
                probability = jnp.exp(s - logsum[q_rows, h : h + 1])
                result_grad = hidden[q_rows, d_columns]
                weight_grad = dot(result_grad, qkv[k_rows, v_columns], 1, 1)
                inner = jnp.sum(probability * weight_grad, axis=1, keepdims=True)
                score_grad = (probability * (weight_grad - inner)).astype(bf16)
                value_sum[0:seen] += dot(probability.astype(bf16), result_grad, 0, 0)
                key_sum[0:seen] += dot(score_grad, qkv[q_rows, q_columns], 0, 0)
                hidden[q_rows, q_columns] = (
                    dot(score_grad, qkv[k_rows, k_columns], 1, 0) * score_scale
                ).astype(bf16)
            hidden[sequence, k_columns] = (key_sum[0:LEN] * score_scale).astype(bf16)
            hidden[sequence, v_columns] = value_sum[0:LEN].astype(bf16)

    for h in range(heads_here):
        attend_back(h)
        if h < bits - 1:
            scatter.all(h)
    for s in range(heads_here, bits - 1):
        scatter.all(s)
    for k in range(ranks - 1):
        g_pass(OUT, k)

    g_first(QKV)

    def keep_up(r, q, value):
        stage_a[r, q] = value

    g_own(UP, keep_up)
    up_store = local(stage_a, upg_hbm, 1)

    def exchange(staged, out, c, base):
        copies = []
        for i in range(1, n):
            peer = lax.rem(me + i, n)
            copy = remote(
                staged.at[:, span(peer, share)], out.at[rows(me, c)],
                ex_send.at[base + c, i], ex_recv.at[base + c, i], peer,
            )
            copy.start()
            copies.append(copy)
        copy = pltpu.make_async_copy(
            staged.at[:, mine], out.at[rows(me, c)], ex_send.at[base + c, 0]
        )
        copy.start()
        return copies + [copy]

    result_copies = []
    for c in range(CHUNKS):
        here = pl.ds(c * sub, sub)
        result = middle[here] + (scatter.total(c) + vectors[5:6])
        buf_b[rows(me, c)] = result.astype(bf16)
    scatter.finish()
    for c in range(CHUNKS):
        result_copies += exchange(buf_b.at[rows(me, c)], out_hbm, c, 0)

    def first_step(t, _):
        here = span(lax.rem(t, tokens // row_tile), row_tile)
        columns = span(t // (tokens // row_tile), column_tile)
        buf_a[here, columns] = dot(hidden[here, 0:in_width], w_in[columns], 1, 1).astype(bf16)
        return 0

    lax.fori_loop(0, (tokens // row_tile) * (width // column_tile), first_step, 0)
    for copy in result_copies:
        copy.wait()
    scatter = scatter_of(buf_a)
    scatter.begin()
    local_sums[5:6] = jnp.sum(hidden[:, 0:share].astype(f32), axis=0, keepdims=True)
    local_sums[6:7] = jnp.sum(
        hidden[:, 2 * share : in_width].astype(f32), axis=0, keepdims=True
    )
    for k in range(units // share):
        local_sums[8 + k : 9 + k] = up_sums[:, k * share : (k + 1) * share]
    scatter.all(0)

    def keep_out(r, q, value):
        stage_b[0:share, :] = value

    g_own(OUT, keep_out)
    out_store = local(stage_b.at[0:share], og_hbm, 0)
    for s in range(1, bits - 1):
        scatter.all(s)
    input_copies = []
    for c in range(CHUNKS):
        here = pl.ds(c * sub, sub)
        xhat, inverse = row_stats(x_own[here].astype(f32))
        upstream = scatter.total(c)
        middle_grad[here] += norm_back(upstream, xhat, inverse, vectors[0:1])
        input_copies += exchange(middle_grad.at[here], xg_hbm, c, CHUNKS)
        sums[3:4] += jnp.sum(upstream * xhat, axis=0, keepdims=True)
        sums[4:5] += jnp.sum(upstream, axis=0, keepdims=True)
    vec_back = []
    for i in range(1, n):
        peer = lax.rem(me + i, n)
        copy = remote(
            sums.at[:, span(peer, share)], landed.at[i],
            ex_send.at[2 * CHUNKS, i], ex_recv.at[2 * CHUNKS, i], peer,
        )
        copy.start()
        vec_back.append(copy)
    g_pass(QKV, 0)
    summed = sums[:, mine]
    for copy in vec_back:
        copy.wait_recv()
    for i in range(1, n):
        summed = summed + landed[i]
    local_sums[0:5] = summed[0:5]
    row_copies = []
    for i in range(1, ranks):
        copy = remote(
            local_sums, row_landed.at[i], row_send.at[i], row_recv.at[i],
            lax.rem(row + i, ranks), "row",
        )
        copy.start()
        row_copies.append(copy)
    for k in range(1, ranks - 1):
        g_pass(QKV, k)
    up_store.wait()

    def keep_in(r, q, value):
        stage_a[r, q] = value

    g_own(QKV, keep_in)
    in_stores = [
        local(stage_a.at[:, i * share : (i + 1) * share], hbm, 1 + i)
        for i, hbm in enumerate((qg_hbm, kg_hbm, vg_hbm))
    ]
    total = local_sums[...]
    for i, copy in enumerate(row_copies):
        copy.wait_recv()
        total = total + row_landed[i + 1]
    small_ref[...] = total
    for copy in vec_copies + vec_back + row_copies:
        copy.wait_send()
    for g in range(4):
        g_sent(g)
    scatter.finish()
    for copy in input_copies + in_stores + [out_store]:
        copy.wait()


def layer(arrays, hbm_weights, vectors, in_bias, up_bias, n, ranks):
    inputs, cotangent = arrays
    tokens, share = inputs.shape
    width = n * share
    depth = hbm_weights[0].shape[0]
    units = up_bias.shape[1]
    block = tokens // n
    sub = block // CHUNKS
    half = n // 2
    low = lambda *shape: pltpu.VMEM(shape, bf16)
    wide = lambda *shape: pltpu.VMEM(shape, f32)
    dma = lambda *shape: pltpu.SemaphoreType.DMA(shape)
    vmem = pl.BlockSpec(memory_space=pltpu.VMEM)
    hbm = pl.BlockSpec(memory_space=pl.ANY)
    kernel_heads = share // HEAD
    scratch = [
        low(width, 3 * share),
        low(share, width),
        low(width, units),
        low(units, width),
        low(tokens, width),
        low(tokens, width),
        low(tokens, width),
        low(tokens, width),
        low(half, CHUNKS, sub, width),
        low(half - 1, CHUNKS, sub, width),
        low(tokens, 3 * share),
        low(tokens, share),
        low(tokens, units),
        low(tokens, units),
        low(ranks + 1, units, depth),
        low(ranks + 1, depth, units),
        wide(depth, units),
        wide(units, depth),
        wide(block, width),
        wide(block, width),
        low(block, width),
        wide(tokens, kernel_heads),
        wide(2, 8 if units >= LEN and depth >= 2 * HEAD else LEN, HEAD),
        wide(8, width),
        wide(8, width),
        wide(8 + units // share, share),
        wide(1, units),
        wide(n, 8, share),
        wide(ranks, 8 + units // share, share),
        dma(8),
        dma(CHUNKS, n),
        dma(CHUNKS, n),
        dma(CHUNKS, n),
        dma(CHUNKS, n),
        dma(CHUNKS, half),
        dma(CHUNKS, half),
        dma(CHUNKS, half),
        dma(CHUNKS, half),
        dma(4, 2, ranks),
        dma(4, 2, ranks),
        dma(4, ranks + 1),
        dma(4, ranks + 1),
        dma(n),
        dma(n),
        dma(2 * CHUNKS + 1, n),
        dma(2 * CHUNKS + 1, n),
        dma(ranks),
        dma(ranks),
        pltpu.SemaphoreType.REGULAR,
    ]
    outs = (
        jax.ShapeDtypeStruct((tokens, share), bf16),
        jax.ShapeDtypeStruct((tokens, share), f32),
        jax.ShapeDtypeStruct((depth, share), f32),
        jax.ShapeDtypeStruct((depth, share), f32),
        jax.ShapeDtypeStruct((depth, share), f32),
        jax.ShapeDtypeStruct((share, depth), f32),
        jax.ShapeDtypeStruct((depth, units), f32),
        jax.ShapeDtypeStruct((units, depth), f32),
        jax.ShapeDtypeStruct((8 + units // share, share), f32),
    )
    return pl.pallas_call(
        functools.partial(layer_kernel, n, ranks),
        out_shape=outs,
        in_specs=[hbm] * 8 + [vmem] * 3,
        out_specs=tuple([hbm] * 8 + [vmem]),
        scratch_shapes=scratch,
        compiler_params=pltpu.CompilerParams(
            collective_id=1, has_side_effects=True, vmem_limit_bytes=VMEM_LIMIT
        ),
    )(inputs, cotangent, *hbm_weights, vectors, in_bias, up_bias)


def per_device(
    inputs,
    norm1_gain,
    norm1_shift,
    query_weight,
    query_bias,
    key_weight,
    value_weight,
    value_bias,
    output_weight,
    output_bias,
    norm2_gain,
    norm2_shift,
    expand_weight,
    expand_bias,
    contract_weight,
    contract_bias,
    cotangent,
):
    cols = lax.axis_size("col")
    ranks = lax.axis_size("row")
    row = lax.axis_index("row")
    share = inputs.shape[1]
    units = expand_weight.shape[1]
    zero = jnp.zeros_like(query_bias)
    vectors = jnp.stack(
        [
            norm1_gain,
            norm1_shift,
            output_bias,
            norm2_gain,
            norm2_shift,
            contract_bias,
            zero,
            zero,
        ]
    )
    in_bias = jnp.concatenate([query_bias, zero, value_bias])[None]
    weights = (
        query_weight,
        key_weight,
        value_weight,
        output_weight,
        expand_weight,
        contract_weight,
    )
    (
        outputs,
        input_grad,
        query_grad,
        key_grad,
        value_grad,
        output_grad,
        expand_grad,
        contract_grad,
        small,
    ) = layer((inputs, cotangent), weights, vectors, in_bias, expand_bias[None], cols, ranks)
    piece = share // ranks
    vector = lax.dynamic_slice_in_dim(small[:8], row * piece, piece, 1)
    wide = small[8:].reshape(units)
    expand_bias_grad = lax.dynamic_slice_in_dim(wide, row * (units // ranks), units // ranks, 0)
    return (
        outputs,
        input_grad,
        vector[3],
        vector[4],
        query_grad,
        vector[5],
        key_grad,
        value_grad,
        vector[6],
        output_grad,
        vector[2],
        vector[0],
        vector[1],
        expand_grad,
        expand_bias_grad,
        contract_grad,
        vector[7],
    )


def solution(mesh):
    in_specs = (
        P("row", "col"),
        P("col"),
        P("col"),
        P("row", "col"),
        P("col"),
        P("row", "col"),
        P("row", "col"),
        P("col"),
        P("col", "row"),
        P("col"),
        P("col"),
        P("col"),
        P("row", "col"),
        P("col"),
        P("col", "row"),
        P("col"),
        P("row", "col"),
    )
    out_specs = (
        P("row", "col"),
        P("row", "col"),
        P(("col", "row")),
        P(("col", "row")),
        P("row", "col"),
        P(("col", "row")),
        P("row", "col"),
        P("row", "col"),
        P(("col", "row")),
        P("col", "row"),
        P(("col", "row")),
        P(("col", "row")),
        P(("col", "row")),
        P("row", "col"),
        P(("col", "row")),
        P("col", "row"),
        P(("col", "row")),
    )
    return jax.shard_map(
        per_device, mesh=mesh, in_specs=in_specs, out_specs=out_specs, check_vma=False
    )
```

```python
import functools
import math

import jax
import jax.numpy as jnp
from jax import lax
from jax.experimental import pallas as pl
from jax.experimental.pallas import tpu as pltpu
from jax.sharding import PartitionSpec as P

HEADS = 16
HEAD = 128
LEN = 1024

epsilon = 1e-05
MESH = pl.DeviceIdType.MESH
bf16 = jnp.bfloat16
f32 = jnp.float32


def flip(index, dim):
    step = 1 << dim
    bit = (index // step) % 2
    return index + (1 - 2 * bit) * step


def flip_mask(index, mask):
    dim = 0
    while mask >> dim:
        if (mask >> dim) & 1:
            index = flip(index, dim)
        dim += 1
    return index


def chip_order(chunk, bits):
    dims = list(range(1, bits))
    start = chunk % len(dims)
    return dims[start:] + dims[:start]


def masks_over(dims):
    masks = [0]
    for dim in dims:
        masks = masks + [m | (1 << dim) for m in masks]
    return masks


def remote(src, dst, send, recv, peer, axis="col"):
    return pltpu.make_async_remote_copy(
        src_ref=src,
        dst_ref=dst,
        send_sem=send,
        recv_sem=recv,
        device_id={axis: peer},
        device_id_type=MESH,
    )


def span(index, size):
    return pl.ds(pl.multiple_of(index * size, size), size)


def dot(a, b, ca, cb):
    return lax.dot_general(a, b, (((ca,), (cb,)), ((), ())), preferred_element_type=f32)


def row_stats(values):
    average = jnp.mean(values, axis=1, keepdims=True)
    centred = values - average
    variance = jnp.mean(centred * centred, axis=1, keepdims=True)
    inverse = lax.rsqrt(variance + epsilon)
    return centred * inverse, inverse


def norm_back(upstream, xhat, inverse, gain):
    scaled = upstream * gain
    mean_scaled = jnp.mean(scaled, axis=1, keepdims=True)
    mean_product = jnp.mean(scaled * xhat, axis=1, keepdims=True)
    return inverse * (scaled - mean_scaled - xhat * mean_product)


class Gather:
    def __init__(self, me, bits, chunks, place, sems, base=0):
        self.me, self.bits, self.chunks, self.place = me, bits, chunks, place
        self.chip_send, self.chip_recv, self.mate_send, self.mate_recv = sems
        self.base = base
        self.held = [[me] for _ in range(chunks)]
        self.waiting = [[] for _ in range(chunks)]
        self.mates, self.sent = [], []

    def stage(self, c, s):
        order = chip_order(c, self.bits)
        if s == 0:
            new, base = [self.me], 0
        else:
            for copy in self.waiting[c]:
                copy.wait_recv()
            base = len(self.held[c])
            new = [flip(b, order[s - 1]) for b in self.held[c]]
            self.held[c] = self.held[c] + new
        if s < self.bits - 1:
            copies = []
            for i, b in enumerate(self.held[c]):
                slot = (1 << s) - 1 + i
                home = self.place(b, c)
                copy = remote(
                    home,
                    home,
                    self.chip_send.at[self.base + c, slot],
                    self.chip_recv.at[self.base + c, slot],
                    flip(self.me, order[s]),
                )
                copy.start()
                copies.append(copy)
            self.waiting[c] = copies
            self.sent.extend(copies)
        for i, b in enumerate(new):
            home = self.place(b, c)
            copy = remote(
                home,
                home,
                self.mate_send.at[self.base + c, base + i],
                self.mate_recv.at[self.base + c, base + i],
                flip(self.me, 0),
            )
            copy.start()
            self.mates.append(copy)

    def all(self, s):
        for c in range(self.chunks):
            self.stage(c, s)

    def finish(self):
        for copy in self.sent:
            copy.wait_send()
        for copy in self.mates:
            copy.wait()


class Scatter:
    def __init__(self, me, bits, chunks, partial, rows, first, later, sems):
        self.me, self.bits, self.chunks = me, bits, chunks
        self.partial, self.rows, self.first, self.later = partial, rows, first, later
        self.core_send, self.core_recv, self.chip_send, self.chip_recv = sems
        self.core, self.chip = {}, {}

    def ranked(self, c):
        lead = chip_order(c, self.bits)[0]
        every = masks_over(list(range(1, self.bits)))
        return lead, sorted(every, key=lambda m: (0 if (m >> lead) & 1 else 1, m))

    def base(self, s):
        return sum(1 << (self.bits - 2 - k) for k in range(s))

    def start(self, c):
        mate = flip(self.me, 0)
        for m in self.ranked(c)[1]:
            slot = m >> 1
            copy = remote(
                self.partial.at[self.rows(flip_mask(mate, m), c)],
                self.first.at[slot, c],
                self.core_send.at[c, slot],
                self.core_recv.at[c, slot],
                mate,
            )
            copy.start()
            self.core[c, m] = copy

    def send(self, c, s, m):
        order = chip_order(c, self.bits)
        kept = m & ~(1 << order[s])
        i = self.base(s) + masks_over(order[s + 1 :]).index(kept)
        copy = remote(
            self.first.at[m >> 1, c],
            self.later.at[i, c],
            self.chip_send.at[c, i],
            self.chip_recv.at[c, i],
            flip(self.me, order[s]),
        )
        copy.start()
        self.chip[c, s, kept] = copy

    def add(self, c, s):
        order = chip_order(c, self.bits)
        if s == 0:
            lead, ranked = self.ranked(c)
            for m in ranked:
                self.core[c, m].wait_recv()
                slot = m >> 1
                mine = self.partial[self.rows(flip_mask(self.me, m), c)]
                total = self.first[slot, c].astype(f32) + mine.astype(f32)
                self.first[slot, c] = total.astype(bf16)
                if (m >> lead) & 1:
                    self.send(c, s, m)
        else:
            for i, m in enumerate(masks_over(order[s:])):
                self.chip[c, s - 1, m].wait_recv()
                slot = m >> 1
                here = self.later[self.base(s - 1) + i, c]
                total = self.first[slot, c].astype(f32) + here.astype(f32)
                self.first[slot, c] = total.astype(bf16)
            for m in masks_over(order[s + 1 :]):
                self.send(c, s, m | (1 << order[s]))

    def total(self, c):
        s = self.bits - 2
        self.chip[c, s, 0].wait_recv()
        return self.first[0, c].astype(f32) + self.later[self.base(s), c].astype(f32)

    def begin(self):
        for c in range(self.chunks):
            self.start(c)

    def all(self, s):
        for c in range(self.chunks):
            self.add(c, s)

    def finish(self):
        for copy in list(self.core.values()) + list(self.chip.values()):
            copy.wait_send()


QKV, OUT = 0, 1
UP = (2, 4)
DOWN = (3, 5)
CHUNKS = 4
VMEM_LIMIT = 65024 << 10


def layer_kernel(n, ranks, *refs):
    (
        x_hbm, cot_hbm, q_hbm, k_hbm, v_hbm, o_hbm, up_hbm, down_hbm,
        gain1, shift1, bias_o, gain2, shift2, bias_c, bias_q, bias_v, up_bias,
        out_hbm, xg_hbm, qg_hbm, kg_hbm, vg_hbm, og_hbm, upg_hbm, downg_hbm, small_ref,
        w_in, w_out, w_up, w_down, normed1, down_rows, buf_a, buf_b, first, later,
        qkv, attended, slope_grad, hidden, slots_down, slots_up,
        stage_a, stage_b, middle, middle_grad, x_own, logsum, kv_sum, vectors, sums,
        local_sums, up_sums, in_bias, landed, row_landed,
        local_sem, gather_a, gather_b, gather_c, gather_d,
        scatter_a, scatter_b, scatter_c, scatter_d,
        z_send, z_recv, g_send, g_recv, vec_send, vec_recv, ex_send, ex_recv,
        row_send, row_recv, free_sem,
    ) = refs
    bits = n.bit_length() - 1
    me = lax.axis_index("col")
    row = lax.axis_index("row")
    tokens, width = normed1.shape
    share = width // n
    depth = width // ranks
    units = hidden.shape[1]
    block = tokens // n
    sub = block // CHUNKS
    heads_here = share // HEAD
    in_width = 3 * share
    part = units // 2
    halves = (slice(0, part), slice(part, units))
    in_grad = hidden.at[:, 0:in_width]
    score_scale = 1.0 / math.sqrt(HEAD)
    right, left = row + 1, row - 1
    has_left, has_right = row > 0, row < ranks - 1
    is_end = jnp.logical_or(row == 0, row == ranks - 1)
    is_inner = jnp.logical_not(is_end)

    def local(src, dst, i):
        copy = pltpu.make_async_copy(src, dst, local_sem.at[i])
        copy.start()
        return copy

    def rows(b, c):
        return pl.ds(pl.multiple_of(b * block + c * sub, sub), sub)

    mine = span(me, share)

    def z_block(k, b):
        if k == QKV:
            return w_in.at[span(b, depth)]
        if k == OUT:
            return w_out.at[:, span(b, depth)]
        if k in UP:
            return w_up.at[span(b, depth), halves[UP.index(k)]]
        return w_down.at[halves[DOWN.index(k)], span(b, depth)]

    def z_copy(k, way, hop):
        b = row - hop if way == 0 else row + hop
        peer = right if way == 0 else left
        return remote(
            z_block(k, b), z_block(k, b), z_send.at[k, way, hop], z_recv.at[k, way, hop],
            peer, "row",
        )

    def z_landing(k, way, hop):
        b = row - hop if way == 0 else row + hop
        return remote(
            z_block(k, b), z_block(k, b), z_send.at[k, way, hop - 1],
            z_recv.at[k, way, hop - 1], left if way == 0 else right, "row",
        )

    in_low = row < ranks // 2
    in_high = jnp.logical_not(in_low)

    def z_own(k, to_right=has_right, to_left=has_left):
        @pl.when(jnp.logical_and(has_right, to_right))
        def _():
            z_copy(k, 0, 0).start()

        @pl.when(jnp.logical_and(has_left, to_left))
        def _():
            z_copy(k, 1, 0).start()

    def z_own_end(k):
        z_own(k, is_end, is_end)

    def z_own_inward(k):
        z_own(k, jnp.logical_and(is_inner, in_low), jnp.logical_and(is_inner, in_high))

    def z_own_outward(k):
        z_own(k, jnp.logical_and(is_inner, in_high), jnp.logical_and(is_inner, in_low))

    def z_pass(k, hop):
        @pl.when(row >= hop)
        def _():
            z_landing(k, 0, hop).wait_recv()
            if hop < ranks - 1:

                @pl.when(has_right)
                def _():
                    z_copy(k, 0, hop).start()

        @pl.when(row + hop <= ranks - 1)
        def _():
            z_landing(k, 1, hop).wait_recv()
            if hop < ranks - 1:

                @pl.when(has_left)
                def _():
                    z_copy(k, 1, hop).start()

    def z_sent(k):
        for hop in range(ranks - 1):

            @pl.when(jnp.logical_and(row >= hop, has_right))
            def _():
                z_copy(k, 0, hop).wait_send()

            @pl.when(jnp.logical_and(row + hop <= ranks - 1, has_left))
            def _():
                z_copy(k, 1, hop).wait_send()

    def slot(g, s):
        if g in DOWN:
            return slots_down.at[s, halves[DOWN.index(g)]]
        if g in UP:
            return slots_up.at[s, :, halves[UP.index(g)]]
        if g == OUT:
            return w_down.at[
                pl.ds(pl.multiple_of(depth + (s // ranks) * share, share), share),
                span(lax.rem(s, ranks), depth),
            ]
        return w_up.at[span(s, depth), 0:in_width]

    def last_slot(g):
        if g == QKV:
            return w_down.at[0:depth, 0:in_width]
        return slot(g, ranks)

    def term(g, c, write):
        if g in DOWN:
            half = DOWN.index(g)
            tile = min(256, part)

            def step(i, _):
                columns = span(half * (part // tile) + i, tile)
                value = dot(hidden[:, columns], down_rows[:, span(c, depth)], 0, 0)
                write(span(i, tile), slice(0, depth), value)
                return 0

            lax.fori_loop(0, part // tile, step, 0)
        elif g in UP:
            value = dot(buf_a[:, span(c, depth)], slope_grad[:, halves[UP.index(g)]], 0, 0)
            write(slice(0, depth), slice(0, part), value)
        elif g == OUT:
            value = dot(attended[...], down_rows[:, span(c, depth)], 0, 0)
            write(slice(0, share), slice(0, depth), value)
        else:

            def step(j, _):
                value = dot(normed1[:, span(c, depth)], hidden[:, span(j, share)], 0, 0)
                write(slice(0, depth), span(j, share), value)
                return 0

            lax.fori_loop(0, 3, step, 0)

    def chunk_at(k):
        low = row < ranks // 2
        up_count = ranks - 1 - row
        from_low = jnp.where(k < up_count, ranks - 1 - k, k - up_count)
        from_high = jnp.where(k < row, k, ranks - 1 - (k - row))
        return jnp.where(low, from_low, from_high)

    def g_copy(g, c, way, to_owner=False):
        src = slot(g, c)
        dst = last_slot(g) if to_owner else slot(g, c)
        sem = g_recv.at[g, ranks] if to_owner else g_recv.at[g, c]
        return remote(src, dst, g_send.at[g, c], sem, right if way == 0 else left, "row")

    def g_start(g, c):
        @pl.when(c > row)
        def _():
            g_copy(g, c, 0).start()

        @pl.when(jnp.logical_and(c < row, c == left))
        def _():
            g_copy(g, c, 1, True).start()

        @pl.when(jnp.logical_and(c < row, c != left))
        def _():
            g_copy(g, c, 1).start()

    def g_first(g, begin=0, end=ranks - 1):
        @pl.when(is_end)
        def _():
            def step(k, _):
                c = chunk_at(k)
                here = slot(g, c)

                def write(r, q, value):
                    here[r, q] = value.astype(bf16)

                term(g, c, write)
                g_start(g, c)
                return 0

            lax.fori_loop(begin, end, step, 0)

    def g_pass(g, k):
        @pl.when(jnp.logical_not(is_end))
        def _():
            c = chunk_at(k)
            here = slot(g, c)
            g_copy(g, c, 0).wait_recv()

            def write(r, q, value):
                here[r, q] = (here[r, q].astype(f32) + value).astype(bf16)

            term(g, c, write)
            g_start(g, c)

    def g_own_term(g, stage):
        def write(r, q, value):
            stage[r, q] = value

        term(g, row, write)

    def g_own_add(g, stage, step=64):
        def add(here):
            def body(i, _):
                r = span(i, step)
                stage[r] += here[r].astype(f32)
                return 0

            lax.fori_loop(0, here.shape[0] // step, body, 0)

        @pl.when(has_left)
        def _():
            g_copy(g, row, 0).wait_recv()
            add(slot(g, row))

        @pl.when(has_right)
        def _():
            g_copy(g, row, 1, True).wait_recv()
            add(last_slot(g))

    def g_sent(g):
        for k in range(ranks - 1):
            g_copy(g, chunk_at(k), 0).wait_send()

    x_load = local(x_hbm, normed1.at[:, mine], 0)
    in_loads = [
        local(hbm, stage_a.at[0:depth, i * share : (i + 1) * share], 1 + i)
        for i, hbm in enumerate((q_hbm, k_hbm, v_hbm))
    ]
    o_load = local(o_hbm, stage_b.at[0:share, :], 4)
    cot_load = local(cot_hbm, down_rows.at[:, mine], 5)

    barrier = pltpu.get_barrier_semaphore()
    for i in range(1, n):
        pl.semaphore_signal(
            barrier, inc=1, device_id={"col": lax.rem(me + i, n)}, device_id_type=MESH
        )
    for i in range(1, ranks):
        pl.semaphore_signal(
            barrier, inc=1, device_id={"row": lax.rem(row + i, ranks)}, device_id_type=MESH
        )
    pl.semaphore_wait(barrier, n - 1 + ranks - 1)

    gather_sems = (gather_a, gather_b, gather_c, gather_d)
    scatter_sems = (scatter_a, scatter_b, scatter_c, scatter_d)
    half = tokens // 2

    def feature_place(ref):
        def place(b, c):
            return ref.at[pl.ds(c * half, half), span(b, share)]

        return place

    gather_x = Gather(me, bits, 2, feature_place(normed1), gather_sems)
    gather_g = Gather(me, bits, 2, feature_place(down_rows), gather_sems, 2)
    x_load.wait()
    gather_x.all(0)
    for i, ref in enumerate((gain1, shift1, bias_o, gain2, shift2, bias_c)):
        vectors[i : i + 1, mine] = ref[...]
    in_bias[...] = jnp.zeros(in_bias.shape, f32)
    in_bias[:, 0:share] = bias_q[...]
    in_bias[:, 2 * share : in_width] = bias_v[...]
    vec_copies = []
    for i in range(1, n):
        copy = remote(
            vectors.at[:, mine], vectors.at[:, mine], vec_send.at[i], vec_recv.at[i],
            lax.rem(me + i, n),
        )
        copy.start()
        vec_copies.append(copy)
    for copy in in_loads:
        copy.wait()
    w_in[span(row, depth)] = stage_a[:, 0:in_width].astype(bf16)
    z_own(QKV)
    up_load = local(up_hbm, stage_a, 1)
    o_load.wait()
    w_out[:, span(row, depth)] = stage_b[0:share, :].astype(bf16)
    z_own(OUT)
    down_load = local(down_hbm, stage_b, 2)
    cot_load.wait()
    local_sums[7:8] = jnp.sum(down_rows[:, mine].astype(f32), axis=0, keepdims=True)
    gather_x.all(1)
    up_load.wait()
    w_up[span(row, depth)] = stage_a[...].astype(bf16)
    down_load.wait()
    w_down[:, span(row, depth)] = stage_b[...].astype(bf16)
    for s in range(2, bits - 1):
        gather_x.all(s)
    z_pass(QKV, 1)
    z_pass(OUT, 1)
    gather_x.all(bits - 1)
    gather_g.all(0)
    z_own_end(UP[0])
    z_own_end(DOWN[0])
    gather_x.finish()
    for copy in vec_copies:
        copy.wait_recv()
    x_own[...] = normed1[span(me, block)]

    def norm_step(i, _):
        here = span(i, 64)
        xhat, _ = row_stats(normed1[here].astype(f32))
        normed1[here] = (xhat * vectors[0:1] + vectors[1:2]).astype(bf16)
        return 0

    lax.fori_loop(0, tokens // 64, norm_step, 0)
    for s in range(1, bits - 1):
        gather_g.all(s)
    for hop in range(2, ranks - 1):
        z_pass(QKV, hop)
        z_pass(OUT, hop)
    z_own_inward(UP[0])
    gather_g.all(bits - 1)
    z_own_end(UP[1])
    z_own_end(DOWN[1])
    z_pass(QKV, ranks - 1)

    def qkv_step(j, _):
        columns = span(j, share)
        qkv[:, columns] = (dot(normed1[...], w_in[:, columns], 1, 0) + in_bias[:, columns]).astype(bf16)
        return 0

    lax.fori_loop(0, 3, qkv_step, 0)

    tile = 256

    def slope_of(h):
        number = jnp.full((1, 1), me * heads_here + h + 1, jnp.int32).astype(f32)
        return jnp.exp2(-8.0 / HEADS * number)

    def blocks(h):
        for start in range(0, tokens, LEN):
            for i in range(LEN // tile):
                seen = (i + 1) * tile
                yield slice(start + i * tile, start + seen), slice(start, start + seen), i * tile

    def scores(h, q_rows, k_rows, offset):
        q_columns = slice(h * HEAD, (h + 1) * HEAD)
        k_columns = slice(share + h * HEAD, share + (h + 1) * HEAD)
        raw = dot(qkv[q_rows, q_columns], qkv[k_rows, k_columns], 1, 1) * score_scale
        shape = raw.shape
        distance = lax.broadcasted_iota(jnp.int32, shape, 1) - (
            lax.broadcasted_iota(jnp.int32, shape, 0) + offset
        )
        raw = raw + slope_of(h) * distance.astype(f32)
        return jnp.where(distance <= 0, raw, -jnp.inf)

    def attend(h):
        v_columns = slice(2 * share + h * HEAD, 2 * share + (h + 1) * HEAD)
        for q_rows, k_rows, offset in blocks(h):
            s = scores(h, q_rows, k_rows, offset)
            top = jnp.max(s, axis=1, keepdims=True)
            exponent = jnp.exp(s - top)
            total = jnp.sum(exponent, axis=1, keepdims=True)
            weights = (exponent / total).astype(bf16)
            attended[q_rows, h * HEAD : (h + 1) * HEAD] = dot(
                weights, qkv[k_rows, v_columns], 1, 0
            ).astype(bf16)
            logsum[q_rows, h : h + 1] = top + jnp.log(total)

    for h in range(heads_here):
        attend(h)
    z_own_outward(UP[0])
    z_own_inward(DOWN[0])
    gather_g.finish()
    z_pass(OUT, ranks - 1)

    column_tile = 256

    def branch_step(j, _):
        columns = span(j, column_tile)
        buf_b[:, columns] = dot(attended[...], w_out[:, columns], 1, 0).astype(bf16)
        return 0

    lax.fori_loop(0, width // column_tile, branch_step, 0)

    def scatter_of(partial):
        return Scatter(me, bits, CHUNKS, partial, rows, first, later, scatter_sems)

    def gather_of(ref):
        return Gather(me, bits, CHUNKS, lambda b, c: ref.at[rows(b, c)], gather_sems)

    scatter = scatter_of(buf_b)
    gather = gather_of(buf_a)
    scatter.begin()
    scatter.all(0)
    for s in range(1, bits - 1):
        scatter.all(s)
    z_pass(UP[0], 1)
    z_own_outward(DOWN[0])
    z_own_inward(UP[1])
    for c in range(CHUNKS):
        here = pl.ds(c * sub, sub)
        values = x_own[here].astype(f32) + (scatter.total(c) + vectors[2:3])
        middle[here] = values
        xhat, _ = row_stats(values)
        buf_a[rows(me, c)] = (xhat * vectors[3:4] + vectors[4:5]).astype(bf16)
        gather.stage(c, 0)
    for hop in range(2, ranks - 1):
        z_pass(UP[0], hop)
    for s in range(1, bits - 1):
        gather.all(s)
    scatter.finish()
    gather.all(bits - 1)
    z_pass(DOWN[0], 1)
    z_own_outward(UP[1])
    z_own_inward(DOWN[1])
    gather.finish()
    z_pass(UP[0], ranks - 1)

    row_tile = 512
    row_tiles = tokens // row_tile
    hidden_tiles = row_tiles * (part // column_tile)

    def expand(half):
        def step(t, _):
            here = span(lax.rem(t, row_tiles), row_tile)
            columns = span(half * (part // column_tile) + t // row_tiles, column_tile)
            u = dot(buf_a[here], w_up[:, columns], 1, 0) + up_bias[:, columns]
            square = u * u
            inner = jnp.tanh(0.7978845608 * (u + 0.044715 * (u * square)))
            outer = 0.5 * (1.0 + inner)
            hidden[here, columns] = (u * outer).astype(bf16)
            slope = outer + 0.5 * u * (1.0 - inner * inner) * (
                0.7978845608 * (1.0 + 3.0 * 0.044715 * square)
            )
            slope_grad[here, columns] = slope.astype(bf16)
            return 0

        lax.fori_loop(0, hidden_tiles, step, 0)

    def expand_back(half):
        def step(t, _):
            here = span(lax.rem(t, row_tiles), row_tile)
            columns = span(half * (part // column_tile) + t // row_tiles, column_tile)
            grad = dot(down_rows[here], w_down[columns], 1, 1)
            low = (grad * slope_grad[here, columns].astype(f32)).astype(bf16)
            slope_grad[here, columns] = low
            up_sums[:, columns] += jnp.sum(low.astype(f32), axis=0, keepdims=True)
            return 0

        lax.fori_loop(0, hidden_tiles, step, 0)

    up_sums[...] = jnp.zeros(up_sums.shape, f32)
    expand(0)
    g_first(DOWN[0])
    for hop in range(2, ranks - 1):
        z_pass(DOWN[0], hop)
    z_pass(UP[1], 1)
    z_own_outward(DOWN[1])
    z_pass(DOWN[0], ranks - 1)
    expand_back(0)
    g_first(UP[0])
    for hop in range(2, ranks - 1):
        z_pass(UP[1], hop)
    z_pass(DOWN[1], 1)
    z_pass(UP[1], ranks - 1)
    expand(1)
    g_first(DOWN[1])
    for hop in range(2, ranks):
        z_pass(DOWN[1], hop)
    expand_back(1)
    g_first(UP[1], 0, 1)

    def second_step(t, _):
        here = span(lax.rem(t, row_tiles), row_tile)
        columns = span(t // row_tiles, column_tile)
        buf_b[here, columns] = dot(slope_grad[here], w_up[columns], 1, 1).astype(bf16)
        return 0

    lax.fori_loop(0, row_tiles * (width // column_tile), second_step, 0)
    for g in (DOWN[0], UP[0], DOWN[1]):
        for k in range(ranks - 1):
            g_pass(g, k)
    for half in range(2):
        g_own_term(DOWN[half], stage_b.at[halves[half]])
    scatter = scatter_of(buf_b)
    gather = gather_of(down_rows)
    scatter.begin()
    g_first(UP[1], 1)
    for s in range(bits - 1):
        scatter.all(s)
    g_pass(UP[1], 0)
    sums[...] = jnp.zeros(sums.shape, f32)
    for c in range(CHUNKS):
        here = pl.ds(c * sub, sub)
        xhat, inverse = row_stats(middle[here])
        upstream = scatter.total(c)
        grad = down_rows[rows(me, c)].astype(f32) + norm_back(upstream, xhat, inverse, vectors[3:4])
        middle_grad[here] = grad
        low = grad.astype(bf16)
        down_rows[rows(me, c)] = low
        gather.stage(c, 0)
        sums[0:1] += jnp.sum(upstream * xhat, axis=0, keepdims=True)
        sums[1:2] += jnp.sum(upstream, axis=0, keepdims=True)
        sums[2:3] += jnp.sum(low.astype(f32), axis=0, keepdims=True)
    for s in range(1, bits - 1):
        gather.all(s)
    scatter.finish()

    def contract_step(t, _):
        here = span(lax.rem(t, tokens // row_tile), row_tile)
        columns = span(t // (tokens // row_tile), column_tile)
        buf_b[here, columns] = dot(hidden[here], w_down[:, columns], 1, 0).astype(bf16)
        return 0

    lax.fori_loop(0, (tokens // row_tile) * (width // column_tile), contract_step, 0)
    for k in range(6):
        z_sent(k)

    @pl.when(has_right)
    def _():
        pl.semaphore_signal(free_sem, inc=1, device_id={"row": right}, device_id_type=MESH)

    @pl.when(has_left)
    def _():
        pl.semaphore_signal(free_sem, inc=1, device_id={"row": left}, device_id_type=MESH)

    gather.all(bits - 1)
    for k in range(1, ranks - 1):
        g_pass(UP[1], k)
    gather.finish()
    for half in range(2):
        g_own_add(DOWN[half], stage_b.at[halves[half]])
    down_store = local(stage_b, downg_hbm, 0)

    scatter = scatter_of(buf_b)
    scatter.begin()
    pl.semaphore_wait(free_sem, has_left.astype(jnp.int32) + has_right.astype(jnp.int32))
    g_first(OUT)

    def attended_step(i, _):
        here = span(i, row_tile)
        value = dot(down_rows[here], w_out[...], 1, 1).astype(bf16)
        hidden[here, in_width : in_width + share] = value
        return 0

    lax.fori_loop(0, tokens // row_tile, attended_step, 0)
    down_store.wait()
    if kv_sum.shape[1] == LEN:
        key_sum, value_sum = kv_sum.at[0], kv_sum.at[1]
    else:
        key_sum, value_sum = stage_b.at[:, 0:HEAD], stage_b.at[:, HEAD : 2 * HEAD]

    def attend_back(h):
        q_columns = slice(h * HEAD, (h + 1) * HEAD)
        k_columns = slice(share + h * HEAD, share + (h + 1) * HEAD)
        v_columns = slice(2 * share + h * HEAD, 2 * share + (h + 1) * HEAD)
        d_columns = slice(in_width + h * HEAD, in_width + (h + 1) * HEAD)
        for start in range(0, tokens, LEN):
            sequence = slice(start, start + LEN)
            key_sum[0:LEN] = jnp.zeros((LEN, HEAD), f32)
            value_sum[0:LEN] = jnp.zeros((LEN, HEAD), f32)
            for i in range(LEN // tile):
                seen = (i + 1) * tile
                q_rows = slice(start + i * tile, start + seen)
                k_rows = slice(start, start + seen)
                s = scores(h, q_rows, k_rows, i * tile)
                probability = jnp.exp(s - logsum[q_rows, h : h + 1])
                result_grad = hidden[q_rows, d_columns]
                weight_grad = dot(result_grad, qkv[k_rows, v_columns], 1, 1)
                inner = jnp.sum(probability * weight_grad, axis=1, keepdims=True)
                score_grad = (probability * (weight_grad - inner)).astype(bf16)
                value_sum[0:seen] += dot(probability.astype(bf16), result_grad, 0, 0)
                key_sum[0:seen] += dot(score_grad, qkv[q_rows, q_columns], 0, 0)
                hidden[q_rows, q_columns] = (
                    dot(score_grad, qkv[k_rows, k_columns], 1, 0) * score_scale
                ).astype(bf16)
            hidden[sequence, k_columns] = (key_sum[0:LEN] * score_scale).astype(bf16)
            hidden[sequence, v_columns] = value_sum[0:LEN].astype(bf16)

    for h in range(heads_here):
        attend_back(h)
        if h == 0:
            scatter.all(0)

    g_first(QKV)
    for k in range(ranks - 1):
        g_pass(OUT, k)
    for s in range(1, bits - 1):
        scatter.all(s)

    for half in range(2):
        g_own_term(UP[half], stage_a.at[:, halves[half]])
        g_own_add(UP[half], stage_a.at[:, halves[half]])
    up_store = local(stage_a, upg_hbm, 1)

    def exchange(staged, out, c, base):
        copies = []
        for i in range(1, n):
            peer = lax.rem(me + i, n)
            copy = remote(
                staged.at[:, span(peer, share)], out.at[rows(me, c)],
                ex_send.at[base + c, i], ex_recv.at[base + c, i], peer,
            )
            copy.start()
            copies.append(copy)
        copy = pltpu.make_async_copy(
            staged.at[:, mine], out.at[rows(me, c)], ex_send.at[base + c, 0]
        )
        copy.start()
        return copies + [copy]

    result_copies = []
    for c in range(CHUNKS):
        here = pl.ds(c * sub, sub)
        result = middle[here] + (scatter.total(c) + vectors[5:6])
        buf_b[rows(me, c)] = result.astype(bf16)
    scatter.finish()
    for c in range(CHUNKS):
        result_copies += exchange(buf_b.at[rows(me, c)], out_hbm, c, 0)

    def first_step(t, _):
        here = span(lax.rem(t, tokens // row_tile), row_tile)
        columns = span(t // (tokens // row_tile), column_tile)
        buf_a[here, columns] = dot(hidden[here, 0:in_width], w_in[columns], 1, 1).astype(bf16)
        return 0

    lax.fori_loop(0, (tokens // row_tile) * (width // column_tile), first_step, 0)
    g_pass(QKV, 0)
    for copy in result_copies:
        copy.wait()
    scatter = scatter_of(buf_a)
    scatter.begin()
    local_sums[5:6] = jnp.sum(hidden[:, 0:share].astype(f32), axis=0, keepdims=True)
    local_sums[6:7] = jnp.sum(
        hidden[:, 2 * share : in_width].astype(f32), axis=0, keepdims=True
    )
    for k in range(units // share):
        local_sums[8 + k : 9 + k] = up_sums[:, k * share : (k + 1) * share]
    scatter.all(0)

    g_own_term(OUT, stage_b.at[0:share])
    g_own_add(OUT, stage_b.at[0:share])
    out_store = local(stage_b.at[0:share], og_hbm, 0)
    for s in range(1, bits - 1):
        scatter.all(s)
    if ranks > 2:
        g_pass(QKV, 1)
    input_copies = []
    for c in range(CHUNKS):
        here = pl.ds(c * sub, sub)
        xhat, inverse = row_stats(x_own[here].astype(f32))
        upstream = scatter.total(c)
        middle_grad[here] += norm_back(upstream, xhat, inverse, vectors[0:1])
        input_copies += exchange(middle_grad.at[here], xg_hbm, c, CHUNKS)
        sums[3:4] += jnp.sum(upstream * xhat, axis=0, keepdims=True)
        sums[4:5] += jnp.sum(upstream, axis=0, keepdims=True)
    vec_back = []
    for i in range(1, n):
        peer = lax.rem(me + i, n)
        copy = remote(
            sums.at[:, span(peer, share)], landed.at[i],
            ex_send.at[2 * CHUNKS, i], ex_recv.at[2 * CHUNKS, i], peer,
        )
        copy.start()
        vec_back.append(copy)
    for k in range(2, ranks - 1):
        g_pass(QKV, k)
    summed = sums[:, mine]
    for copy in vec_back:
        copy.wait_recv()
    for i in range(1, n):
        summed = summed + landed[i]
    local_sums[0:5] = summed[0:5]
    row_copies = []
    for i in range(1, ranks):
        copy = remote(
            local_sums, row_landed.at[i], row_send.at[i], row_recv.at[i],
            lax.rem(row + i, ranks), "row",
        )
        copy.start()
        row_copies.append(copy)
    up_store.wait()

    g_own_term(QKV, stage_a.at[:, 0:in_width])
    g_own_add(QKV, stage_a.at[:, 0:in_width])
    in_stores = [
        local(stage_a.at[:, i * share : (i + 1) * share], hbm, 1 + i)
        for i, hbm in enumerate((qg_hbm, kg_hbm, vg_hbm))
    ]
    total = local_sums[...]
    for i, copy in enumerate(row_copies):
        copy.wait_recv()
        total = total + row_landed[i + 1]
    small_ref[...] = total
    for copy in vec_copies + vec_back + row_copies:
        copy.wait_send()
    for g in range(6):
        g_sent(g)
    scatter.finish()
    for copy in input_copies + in_stores + [out_store]:
        copy.wait()


def layer(arrays, hbm_weights, vectors, n, ranks):
    inputs, cotangent = arrays
    tokens, share = inputs.shape
    width = n * share
    depth = hbm_weights[0].shape[0]
    units = vectors[-1].shape[1]
    block = tokens // n
    sub = block // CHUNKS
    half = n // 2
    low = lambda *shape: pltpu.VMEM(shape, bf16)
    wide = lambda *shape: pltpu.VMEM(shape, f32)
    dma = lambda *shape: pltpu.SemaphoreType.DMA(shape)
    vmem = pl.BlockSpec(memory_space=pltpu.VMEM)
    hbm = pl.BlockSpec(memory_space=pl.ANY)
    kernel_heads = share // HEAD
    scratch = [
        low(width, 3 * share),
        low(share, width),
        low(width, units),
        low(units, width),
        low(tokens, width),
        low(tokens, width),
        low(tokens, width),
        low(tokens, width),
        low(half, CHUNKS, sub, width),
        low(half - 1, CHUNKS, sub, width),
        low(tokens, 3 * share),
        low(tokens, share),
        low(tokens, units),
        low(tokens, units),
        low(ranks + 1, units, depth),
        low(ranks + 1, depth, units),
        wide(depth, units),
        wide(units, depth),
        wide(block, width),
        wide(block, width),
        low(block, width),
        wide(tokens, kernel_heads),
        wide(2, 8 if units >= LEN and depth >= 2 * HEAD else LEN, HEAD),
        wide(8, width),
        wide(8, width),
        wide(8 + units // share, share),
        wide(1, units),
        wide(1, 3 * share),
        wide(n, 8, share),
        wide(ranks, 8 + units // share, share),
        dma(8),
        dma(CHUNKS, n),
        dma(CHUNKS, n),
        dma(CHUNKS, n),
        dma(CHUNKS, n),
        dma(CHUNKS, half),
        dma(CHUNKS, half),
        dma(CHUNKS, half),
        dma(CHUNKS, half),
        dma(6, 2, ranks),
        dma(6, 2, ranks),
        dma(6, ranks + 1),
        dma(6, ranks + 1),
        dma(n),
        dma(n),
        dma(2 * CHUNKS + 1, n),
        dma(2 * CHUNKS + 1, n),
        dma(ranks),
        dma(ranks),
        pltpu.SemaphoreType.REGULAR,
    ]
    outs = (
        jax.ShapeDtypeStruct((tokens, share), bf16),
        jax.ShapeDtypeStruct((tokens, share), f32),
        jax.ShapeDtypeStruct((depth, share), f32),
        jax.ShapeDtypeStruct((depth, share), f32),
        jax.ShapeDtypeStruct((depth, share), f32),
        jax.ShapeDtypeStruct((share, depth), f32),
        jax.ShapeDtypeStruct((depth, units), f32),
        jax.ShapeDtypeStruct((units, depth), f32),
        jax.ShapeDtypeStruct((8 + units // share, share), f32),
    )
    return pl.pallas_call(
        functools.partial(layer_kernel, n, ranks),
        out_shape=outs,
        in_specs=[hbm] * 8 + [vmem] * 9,
        out_specs=tuple([hbm] * 8 + [vmem]),
        scratch_shapes=scratch,
        compiler_params=pltpu.CompilerParams(
            collective_id=1, has_side_effects=True, vmem_limit_bytes=VMEM_LIMIT
        ),
    )(inputs, cotangent, *hbm_weights, *vectors)


def settle_kernel(count, *refs):
    sources, targets, held = refs[:count], refs[count : 2 * count], refs[2 * count : 3 * count]
    sems = refs[3 * count]
    inward = [pltpu.make_async_copy(sources[i], held[i], sems.at[0, i]) for i in range(count)]
    outward = [pltpu.make_async_copy(held[i], targets[i], sems.at[1, i]) for i in range(count)]
    for copy in inward:
        copy.start()
    for arrived, copy in zip(inward, outward):
        arrived.wait()
        copy.start()
    for copy in outward:
        copy.wait()


def settle(arrays):
    count = len(arrays)
    hbm = pl.BlockSpec(memory_space=pl.ANY)
    return pl.pallas_call(
        functools.partial(settle_kernel, count),
        out_shape=tuple(jax.ShapeDtypeStruct(a.shape, a.dtype) for a in arrays),
        in_specs=[hbm] * count,
        out_specs=tuple([hbm] * count),
        scratch_shapes=[pltpu.VMEM(a.shape, a.dtype) for a in arrays]
        + [pltpu.SemaphoreType.DMA((2, count))],
        compiler_params=pltpu.CompilerParams(vmem_limit_bytes=VMEM_LIMIT),
    )(*arrays)


def per_device(
    inputs,
    norm1_gain,
    norm1_shift,
    query_weight,
    query_bias,
    key_weight,
    value_weight,
    value_bias,
    output_weight,
    output_bias,
    norm2_gain,
    norm2_shift,
    expand_weight,
    expand_bias,
    contract_weight,
    contract_bias,
    cotangent,
):
    cols = lax.axis_size("col")
    ranks = lax.axis_size("row")
    row = lax.axis_index("row")
    share = inputs.shape[1]
    units = expand_weight.shape[1]
    weights = (
        query_weight,
        key_weight,
        value_weight,
        output_weight,
        expand_weight,
        contract_weight,
    )
    (
        outputs,
        input_grad,
        query_grad,
        key_grad,
        value_grad,
        output_grad,
        expand_grad,
        contract_grad,
        small,
    ) = layer(
        (inputs, cotangent),
        weights,
        [
            vector[None]
            for vector in (
                norm1_gain,
                norm1_shift,
                output_bias,
                norm2_gain,
                norm2_shift,
                contract_bias,
                query_bias,
                value_bias,
                expand_bias,
            )
        ],
        cols,
        ranks,
    )
    (
        outputs,
        input_grad,
        query_grad,
        key_grad,
        value_grad,
        output_grad,
        expand_grad,
        contract_grad,
    ) = settle(
        (
            outputs,
            input_grad,
            query_grad,
            key_grad,
            value_grad,
            output_grad,
            expand_grad,
            contract_grad,
        )
    )
    piece = share // ranks
    vector = lax.dynamic_slice_in_dim(small[:8], row * piece, piece, 1)
    wide = small[8:].reshape(units)
    expand_bias_grad = lax.dynamic_slice_in_dim(wide, row * (units // ranks), units // ranks, 0)
    return (
        outputs,
        input_grad,
        vector[3],
        vector[4],
        query_grad,
        vector[5],
        key_grad,
        value_grad,
        vector[6],
        output_grad,
        vector[2],
        vector[0],
        vector[1],
        expand_grad,
        expand_bias_grad,
        contract_grad,
        vector[7],
    )


def solution(mesh):
    in_specs = (
        P("row", "col"),
        P("col"),
        P("col"),
        P("row", "col"),
        P("col"),
        P("row", "col"),
        P("row", "col"),
        P("col"),
        P("col", "row"),
        P("col"),
        P("col"),
        P("col"),
        P("row", "col"),
        P("col"),
        P("col", "row"),
        P("col"),
        P("row", "col"),
    )
    out_specs = (
        P("row", "col"),
        P("row", "col"),
        P(("col", "row")),
        P(("col", "row")),
        P("row", "col"),
        P(("col", "row")),
        P("row", "col"),
        P("row", "col"),
        P(("col", "row")),
        P("col", "row"),
        P(("col", "row")),
        P(("col", "row")),
        P(("col", "row")),
        P("row", "col"),
        P(("col", "row")),
        P("col", "row"),
        P(("col", "row")),
    )
    return jax.shard_map(
        per_device, mesh=mesh, in_specs=in_specs, out_specs=out_specs, check_vma=False
    )
```

```python
import functools
import math

import jax
import jax.numpy as jnp
from jax import lax
from jax.experimental import pallas as pl
from jax.experimental.pallas import tpu as pltpu
from jax.sharding import PartitionSpec as P

HEADS = 16
HEAD = 128
LEN = 1024

epsilon = 1e-05
MESH = pl.DeviceIdType.MESH
bf16 = jnp.bfloat16
f32 = jnp.float32


def flip(index, dim):
    step = 1 << dim
    bit = (index // step) % 2
    return index + (1 - 2 * bit) * step


def flip_mask(index, mask):
    dim = 0
    while mask >> dim:
        if (mask >> dim) & 1:
            index = flip(index, dim)
        dim += 1
    return index


def chip_order(chunk, bits):
    dims = list(range(1, bits))
    start = chunk % len(dims)
    return dims[start:] + dims[:start]


def masks_over(dims):
    masks = [0]
    for dim in dims:
        masks = masks + [m | (1 << dim) for m in masks]
    return masks


def remote(src, dst, send, recv, peer, axis="col"):
    return pltpu.make_async_remote_copy(
        src_ref=src,
        dst_ref=dst,
        send_sem=send,
        recv_sem=recv,
        device_id={axis: peer},
        device_id_type=MESH,
    )


def span(index, size):
    return pl.ds(pl.multiple_of(index * size, size), size)


def dot(a, b, ca, cb):
    return lax.dot_general(a, b, (((ca,), (cb,)), ((), ())), preferred_element_type=f32)


def row_stats(values):
    average = jnp.mean(values, axis=1, keepdims=True)
    centred = values - average
    variance = jnp.mean(centred * centred, axis=1, keepdims=True)
    inverse = lax.rsqrt(variance + epsilon)
    return centred * inverse, inverse


def norm_back(upstream, xhat, inverse, gain):
    scaled = upstream * gain
    mean_scaled = jnp.mean(scaled, axis=1, keepdims=True)
    mean_product = jnp.mean(scaled * xhat, axis=1, keepdims=True)
    return inverse * (scaled - mean_scaled - xhat * mean_product)


def add_rows(target, other, step=512):
    def body(i, _):
        columns = span(i, step)
        total = target[:, columns].astype(f32) + other[:, columns].astype(f32)
        target[:, columns] = total.astype(bf16)
        return 0

    lax.fori_loop(0, target.shape[1] // step, body, 0)


class Gather:
    def __init__(self, me, bits, chunks, place, sems, base=0):
        self.me, self.bits, self.chunks, self.place = me, bits, chunks, place
        self.chip_send, self.chip_recv, self.mate_send, self.mate_recv = sems
        self.base = base
        self.held = [[me] for _ in range(chunks)]
        self.waiting = [[] for _ in range(chunks)]
        self.mates, self.sent = [], []

    def stage(self, c, s):
        order = chip_order(c, self.bits)
        if s == 0:
            new, base = [self.me], 0
        else:
            for copy in self.waiting[c]:
                copy.wait_recv()
            base = len(self.held[c])
            new = [flip(b, order[s - 1]) for b in self.held[c]]
            self.held[c] = self.held[c] + new
        if s < self.bits - 1:
            copies = []
            for i, b in enumerate(self.held[c]):
                slot = (1 << s) - 1 + i
                home = self.place(b, c)
                copy = remote(
                    home,
                    home,
                    self.chip_send.at[self.base + c, slot],
                    self.chip_recv.at[self.base + c, slot],
                    flip(self.me, order[s]),
                )
                copy.start()
                copies.append(copy)
            self.waiting[c] = copies
            self.sent.extend(copies)
        for i, b in enumerate(new):
            home = self.place(b, c)
            copy = remote(
                home,
                home,
                self.mate_send.at[self.base + c, base + i],
                self.mate_recv.at[self.base + c, base + i],
                flip(self.me, 0),
            )
            copy.start()
            self.mates.append(copy)

    def all(self, s):
        for c in range(self.chunks):
            self.stage(c, s)

    def finish(self):
        for copy in self.sent:
            copy.wait_send()
        for copy in self.mates:
            copy.wait()


class Scatter:
    def __init__(self, me, bits, chunks, partial, rows, first, later, sems):
        self.me, self.bits, self.chunks = me, bits, chunks
        self.partial, self.rows, self.first, self.later = partial, rows, first, later
        self.core_send, self.core_recv, self.chip_send, self.chip_recv = sems
        self.core, self.chip = {}, {}

    def ranked(self, c):
        lead = chip_order(c, self.bits)[0]
        every = masks_over(list(range(1, self.bits)))
        return lead, sorted(every, key=lambda m: (0 if (m >> lead) & 1 else 1, m))

    def base(self, s):
        return sum(1 << (self.bits - 2 - k) for k in range(s))

    def start(self, c):
        mate = flip(self.me, 0)
        for m in self.ranked(c)[1]:
            slot = m >> 1
            copy = remote(
                self.partial.at[self.rows(flip_mask(mate, m), c)],
                self.first.at[slot, c],
                self.core_send.at[c, slot],
                self.core_recv.at[c, slot],
                mate,
            )
            copy.start()
            self.core[c, m] = copy

    def send(self, c, s, m):
        order = chip_order(c, self.bits)
        kept = m & ~(1 << order[s])
        i = self.base(s) + masks_over(order[s + 1 :]).index(kept)
        copy = remote(
            self.first.at[m >> 1, c],
            self.later.at[i, c],
            self.chip_send.at[c, i],
            self.chip_recv.at[c, i],
            flip(self.me, order[s]),
        )
        copy.start()
        self.chip[c, s, kept] = copy

    def add(self, c, s):
        order = chip_order(c, self.bits)
        if s == 0:
            lead, ranked = self.ranked(c)
            for m in ranked:
                self.core[c, m].wait_recv()
                slot = m >> 1
                mine = self.partial.at[self.rows(flip_mask(self.me, m), c)]
                add_rows(self.first.at[slot, c], mine)
                if (m >> lead) & 1:
                    self.send(c, s, m)
        else:
            for i, m in enumerate(masks_over(order[s:])):
                self.chip[c, s - 1, m].wait_recv()
                slot = m >> 1
                add_rows(self.first.at[slot, c], self.later.at[self.base(s - 1) + i, c])
            for m in masks_over(order[s + 1 :]):
                self.send(c, s, m | (1 << order[s]))

    def total(self, c):
        s = self.bits - 2
        self.chip[c, s, 0].wait_recv()
        return self.first[0, c].astype(f32) + self.later[self.base(s), c].astype(f32)

    def begin(self):
        for c in range(self.chunks):
            self.start(c)

    def all(self, s):
        for c in range(self.chunks):
            self.add(c, s)

    def finish(self):
        for copy in list(self.core.values()) + list(self.chip.values()):
            copy.wait_send()


QKV, OUT = 0, 1
UP = (2, 4)
DOWN = (3, 5)
IN = (0, 6)
CHUNKS = 4
VMEM_LIMIT = 65024 << 10


def layer_kernel(n, ranks, *refs):
    (
        x_hbm, cot_hbm, q_hbm, k_hbm, v_hbm, o_hbm, up_hbm, down_hbm,
        gain1, shift1, bias_o, gain2, shift2, bias_c, bias_q, bias_v, up_bias,
        out_hbm, xg_hbm, qg_hbm, kg_hbm, vg_hbm, og_hbm, upg_hbm, downg_hbm, small_ref,
        w_in, w_out, w_up, w_down, normed1, down_rows, buf_a, buf_b, first, later,
        qkv, attended, slope_grad, hidden, slots_down, slots_up,
        stage_a, stage_b, middle, middle_grad, x_own, logsum, kv_sum, vectors, sums,
        local_sums, up_sums, in_bias, landed, row_landed,
        local_sem, gather_a, gather_b, gather_c, gather_d,
        scatter_a, scatter_b, scatter_c, scatter_d,
        z_send, z_recv, g_send, g_recv, vec_send, vec_recv, ex_send, ex_recv,
        row_send, row_recv, free_sem,
    ) = refs
    bits = n.bit_length() - 1
    me = lax.axis_index("col")
    row = lax.axis_index("row")
    tokens, width = normed1.shape
    share = width // n
    depth = width // ranks
    units = hidden.shape[1]
    block = tokens // n
    sub = block // CHUNKS
    heads_here = share // HEAD
    in_width = 3 * share
    part = units // 2
    halves = (slice(0, part), slice(part, units))
    in_split = in_width // (2 * HEAD) * HEAD
    in_parts = (slice(0, in_split), slice(in_split, in_width))
    in_grad = hidden.at[:, 0:in_width]
    score_scale = 1.0 / math.sqrt(HEAD)
    right, left = row + 1, row - 1
    has_left, has_right = row > 0, row < ranks - 1
    is_end = jnp.logical_or(row == 0, row == ranks - 1)
    is_inner = jnp.logical_not(is_end)

    def local(src, dst, i):
        copy = pltpu.make_async_copy(src, dst, local_sem.at[i])
        copy.start()
        return copy

    def rows(b, c):
        return pl.ds(pl.multiple_of(b * block + c * sub, sub), sub)

    mine = span(me, share)

    def z_block(k, b):
        if k in IN:
            return w_in.at[span(b, depth), in_parts[IN.index(k)]]
        if k == OUT:
            return w_out.at[:, span(b, depth)]
        if k in UP:
            return w_up.at[span(b, depth), halves[UP.index(k)]]
        return w_down.at[halves[DOWN.index(k)], span(b, depth)]

    def z_copy(k, way, hop):
        b = row - hop if way == 0 else row + hop
        peer = right if way == 0 else left
        return remote(
            z_block(k, b), z_block(k, b), z_send.at[k, way, hop], z_recv.at[k, way, hop],
            peer, "row",
        )

    def z_landing(k, way, hop):
        b = row - hop if way == 0 else row + hop
        return remote(
            z_block(k, b), z_block(k, b), z_send.at[k, way, hop - 1],
            z_recv.at[k, way, hop - 1], left if way == 0 else right, "row",
        )

    in_low = row < ranks // 2
    in_high = jnp.logical_not(in_low)

    def z_own(k, to_right=has_right, to_left=has_left):
        @pl.when(jnp.logical_and(has_right, to_right))
        def _():
            z_copy(k, 0, 0).start()

        @pl.when(jnp.logical_and(has_left, to_left))
        def _():
            z_copy(k, 1, 0).start()

    def z_own_end(k):
        z_own(k, is_end, is_end)

    def z_own_inward(k):
        z_own(k, jnp.logical_and(is_inner, in_low), jnp.logical_and(is_inner, in_high))

    def z_own_outward(k):
        z_own(k, jnp.logical_and(is_inner, in_high), jnp.logical_and(is_inner, in_low))

    def z_pass(k, hop):
        @pl.when(row >= hop)
        def _():
            z_landing(k, 0, hop).wait_recv()
            if hop < ranks - 1:

                @pl.when(has_right)
                def _():
                    z_copy(k, 0, hop).start()

        @pl.when(row + hop <= ranks - 1)
        def _():
            z_landing(k, 1, hop).wait_recv()
            if hop < ranks - 1:

                @pl.when(has_left)
                def _():
                    z_copy(k, 1, hop).start()

    def z_sent(k):
        for hop in range(ranks - 1):

            @pl.when(jnp.logical_and(row >= hop, has_right))
            def _():
                z_copy(k, 0, hop).wait_send()

            @pl.when(jnp.logical_and(row + hop <= ranks - 1, has_left))
            def _():
                z_copy(k, 1, hop).wait_send()

    def slot(g, s):
        if g in DOWN:
            return slots_down.at[s, halves[DOWN.index(g)]]
        if g in UP:
            return slots_up.at[s, :, halves[UP.index(g)]]
        if g == OUT:
            return w_down.at[
                pl.ds(pl.multiple_of(depth + (s // ranks) * share, share), share),
                span(lax.rem(s, ranks), depth),
            ]
        return w_up.at[span(s, depth), 0:in_width]

    def last_slot(g):
        if g == QKV:
            return w_down.at[0:depth, 0:in_width]
        return slot(g, ranks)

    def term(g, c, write):
        if g in DOWN:
            half = DOWN.index(g)
            tile = min(256, part)

            def step(i, _):
                columns = span(half * (part // tile) + i, tile)
                value = dot(hidden[:, columns], down_rows[:, span(c, depth)], 0, 0)
                write(span(i, tile), slice(0, depth), value)
                return 0

            lax.fori_loop(0, part // tile, step, 0)
        elif g in UP:
            value = dot(buf_a[:, span(c, depth)], slope_grad[:, halves[UP.index(g)]], 0, 0)
            write(slice(0, depth), slice(0, part), value)
        elif g == OUT:
            value = dot(attended[...], down_rows[:, span(c, depth)], 0, 0)
            write(slice(0, share), slice(0, depth), value)
        else:

            def step(j, _):
                value = dot(normed1[:, span(c, depth)], hidden[:, span(j, share)], 0, 0)
                write(slice(0, depth), span(j, share), value)
                return 0

            lax.fori_loop(0, 3, step, 0)

    def chunk_at(k):
        low = row < ranks // 2
        up_count = ranks - 1 - row
        from_low = jnp.where(k < up_count, ranks - 1 - k, k - up_count)
        from_high = jnp.where(k < row, k, ranks - 1 - (k - row))
        return jnp.where(low, from_low, from_high)

    def g_copy(g, c, way, to_owner=False):
        src = slot(g, c)
        dst = last_slot(g) if to_owner else slot(g, c)
        sem = g_recv.at[g, ranks] if to_owner else g_recv.at[g, c]
        return remote(src, dst, g_send.at[g, c], sem, right if way == 0 else left, "row")

    def g_start(g, c):
        @pl.when(c > row)
        def _():
            g_copy(g, c, 0).start()

        @pl.when(jnp.logical_and(c < row, c == left))
        def _():
            g_copy(g, c, 1, True).start()

        @pl.when(jnp.logical_and(c < row, c != left))
        def _():
            g_copy(g, c, 1).start()

    def g_first(g, begin=0, end=ranks - 1):
        @pl.when(is_end)
        def _():
            def step(k, _):
                c = chunk_at(k)
                here = slot(g, c)

                def write(r, q, value):
                    here[r, q] = value.astype(bf16)

                term(g, c, write)
                g_start(g, c)
                return 0

            lax.fori_loop(begin, end, step, 0)

    def g_pass(g, begin=0, end=ranks - 1):
        if begin >= end:
            return

        @pl.when(jnp.logical_not(is_end))
        def _():
            def step(k, _):
                c = chunk_at(k)
                here = slot(g, c)
                g_copy(g, c, 0).wait_recv()

                def write(r, q, value):
                    here[r, q] = (here[r, q].astype(f32) + value).astype(bf16)

                term(g, c, write)
                g_start(g, c)
                return 0

            lax.fori_loop(begin, end, step, 0)

    def g_own_term(g, stage):
        def write(r, q, value):
            stage[r, q] = value

        term(g, row, write)

    def g_own_add(g, stage, step=64):
        def add(here):
            def body(i, _):
                r = span(i, step)
                stage[r] += here[r].astype(f32)
                return 0

            lax.fori_loop(0, here.shape[0] // step, body, 0)

        @pl.when(has_left)
        def _():
            g_copy(g, row, 0).wait_recv()
            add(slot(g, row))

        @pl.when(has_right)
        def _():
            g_copy(g, row, 1, True).wait_recv()
            add(last_slot(g))

    def g_sent(g):
        for k in range(ranks - 1):
            g_copy(g, chunk_at(k), 0).wait_send()

    x_load = local(x_hbm, normed1.at[:, mine], 0)
    in_loads = [
        local(hbm, stage_a.at[0:depth, i * share : (i + 1) * share], 1 + i)
        for i, hbm in enumerate((q_hbm, k_hbm, v_hbm))
    ]
    o_load = local(o_hbm, stage_b.at[0:share, :], 4)
    cot_load = local(cot_hbm, down_rows.at[:, mine], 5)

    barrier = pltpu.get_barrier_semaphore()
    for i in range(1, n):
        pl.semaphore_signal(
            barrier, inc=1, device_id={"col": lax.rem(me + i, n)}, device_id_type=MESH
        )
    for i in range(1, ranks):
        pl.semaphore_signal(
            barrier, inc=1, device_id={"row": lax.rem(row + i, ranks)}, device_id_type=MESH
        )
    pl.semaphore_wait(barrier, n - 1 + ranks - 1)

    gather_sems = (gather_a, gather_b, gather_c, gather_d)
    scatter_sems = (scatter_a, scatter_b, scatter_c, scatter_d)
    half = tokens // 2

    def feature_place(ref):
        def place(b, c):
            return ref.at[pl.ds(c * half, half), span(b, share)]

        return place

    gather_x = Gather(me, bits, 2, feature_place(normed1), gather_sems)
    gather_g = Gather(me, bits, 2, feature_place(down_rows), gather_sems, 2)
    x_load.wait()
    gather_x.all(0)
    for i, ref in enumerate((gain1, shift1, bias_o, gain2, shift2, bias_c)):
        vectors[i : i + 1, mine] = ref[...]
    in_bias[...] = jnp.zeros(in_bias.shape, f32)
    in_bias[:, 0:share] = bias_q[...]
    in_bias[:, 2 * share : in_width] = bias_v[...]
    vec_copies = []
    for i in range(1, n):
        copy = remote(
            vectors.at[:, mine], vectors.at[:, mine], vec_send.at[i], vec_recv.at[i],
            lax.rem(me + i, n),
        )
        copy.start()
        vec_copies.append(copy)
    for copy in in_loads:
        copy.wait()
    w_in[span(row, depth)] = stage_a[:, 0:in_width].astype(bf16)
    z_own(IN[0])
    up_load = local(up_hbm, stage_a, 1)
    o_load.wait()
    w_out[:, span(row, depth)] = stage_b[0:share, :].astype(bf16)
    z_own_outward(OUT)
    down_load = local(down_hbm, stage_b, 2)
    cot_load.wait()
    local_sums[7:8] = jnp.sum(down_rows[:, mine].astype(f32), axis=0, keepdims=True)
    gather_x.all(1)
    up_load.wait()
    w_up[span(row, depth)] = stage_a[...].astype(bf16)
    down_load.wait()
    w_down[:, span(row, depth)] = stage_b[...].astype(bf16)
    for s in range(2, bits - 1):
        gather_x.all(s)
    z_own(IN[1])
    z_pass(IN[0], 1)
    gather_x.all(bits - 1)
    gather_g.all(0)
    z_own_end(OUT)
    z_own_end(UP[0])
    z_own_end(DOWN[0])
    gather_x.finish()
    for copy in vec_copies:
        copy.wait_recv()
    x_own[...] = normed1[span(me, block)]

    def norm_step(i, _):
        here = span(i, 64)
        xhat, _ = row_stats(normed1[here].astype(f32))
        normed1[here] = (xhat * vectors[0:1] + vectors[1:2]).astype(bf16)
        return 0

    lax.fori_loop(0, tokens // 64, norm_step, 0)
    z_pass(IN[1], 1)
    if ranks > 3:
        z_pass(IN[0], 2)
    z_own_inward(OUT)
    for s in range(1, bits - 1):
        gather_g.all(s)
    for hop in range(2, ranks - 1):
        z_pass(IN[1], hop)
        if hop + 1 < ranks - 1:
            z_pass(IN[0], hop + 1)
    gather_g.all(bits - 1)
    z_own_end(UP[1])
    z_own_end(DOWN[1])
    z_pass(IN[0], ranks - 1)
    z_pass(IN[1], ranks - 1)

    def qkv_step(j, _):
        columns = span(j, share)
        qkv[:, columns] = (dot(normed1[...], w_in[:, columns], 1, 0) + in_bias[:, columns]).astype(bf16)
        return 0

    lax.fori_loop(0, 3, qkv_step, 0)
    z_pass(OUT, 1)
    z_own_inward(UP[0])
    tile = 256

    def slope_of(h):
        number = jnp.full((1, 1), me * heads_here + h + 1, jnp.int32).astype(f32)
        return jnp.exp2(-8.0 / HEADS * number)

    def columns_of(which, h):
        return pl.ds(pl.multiple_of(which * share + h * HEAD, HEAD), HEAD)

    def blocks():
        for start in range(0, tokens, LEN):
            for i in range(LEN // tile):
                seen = (i + 1) * tile
                yield slice(start + i * tile, start + seen), slice(start, start + seen), i * tile

    def scores(h, q_rows, k_rows, offset):
        raw = dot(qkv[q_rows, columns_of(0, h)], qkv[k_rows, columns_of(1, h)], 1, 1) * score_scale
        shape = raw.shape
        distance = lax.broadcasted_iota(jnp.int32, shape, 1) - (
            lax.broadcasted_iota(jnp.int32, shape, 0) + offset
        )
        raw = raw + slope_of(h) * distance.astype(f32)
        return jnp.where(distance <= 0, raw, -jnp.inf)

    lane = lax.broadcasted_iota(jnp.int32, (tile, HEAD), 1)

    def attend(h, _):
        for q_rows, k_rows, offset in blocks():
            s = scores(h, q_rows, k_rows, offset)
            top = jnp.max(s, axis=1, keepdims=True)
            exponent = jnp.exp(s - top)
            total = jnp.sum(exponent, axis=1, keepdims=True)
            weights = (exponent / total).astype(bf16)
            attended[q_rows, columns_of(0, h)] = dot(
                weights, qkv[k_rows, columns_of(2, h)], 1, 0
            ).astype(bf16)
            logsum[q_rows] = jnp.where(lane == h, top + jnp.log(total), logsum[q_rows])
        return 0

    logsum[...] = jnp.zeros(logsum.shape, f32)
    lax.fori_loop(0, heads_here, attend, 0)
    for hop in range(2, ranks - 1):
        z_pass(OUT, hop)
    z_own_outward(UP[0])
    z_own_inward(DOWN[0])
    gather_g.finish()
    z_pass(OUT, ranks - 1)

    column_tile = 256

    def branch_step(j, _):
        columns = span(j, column_tile)
        buf_b[:, columns] = dot(attended[...], w_out[:, columns], 1, 0).astype(bf16)
        return 0

    lax.fori_loop(0, width // column_tile, branch_step, 0)

    def scatter_of(partial):
        return Scatter(me, bits, CHUNKS, partial, rows, first, later, scatter_sems)

    def gather_of(ref):
        return Gather(me, bits, CHUNKS, lambda b, c: ref.at[rows(b, c)], gather_sems)

    scatter = scatter_of(buf_b)
    gather = gather_of(buf_a)
    scatter.begin()
    scatter.all(0)
    for s in range(1, bits - 1):
        scatter.all(s)
    z_pass(UP[0], 1)
    z_own_outward(DOWN[0])
    z_own_inward(UP[1])
    for c in range(CHUNKS):
        here = pl.ds(c * sub, sub)
        values = x_own[here].astype(f32) + (scatter.total(c) + vectors[2:3])
        middle[here] = values
        xhat, _ = row_stats(values)
        buf_a[rows(me, c)] = (xhat * vectors[3:4] + vectors[4:5]).astype(bf16)
        gather.stage(c, 0)
    for hop in range(2, ranks - 1):
        z_pass(UP[0], hop)
    for s in range(1, bits - 1):
        gather.all(s)
    scatter.finish()
    gather.all(bits - 1)
    z_pass(DOWN[0], 1)
    z_own_inward(DOWN[1])
    gather.finish()
    z_pass(UP[0], ranks - 1)

    row_tile = 512
    row_tiles = tokens // row_tile
    hidden_tiles = row_tiles * (part // column_tile)

    def expand(half):
        def step(t, _):
            here = span(lax.rem(t, row_tiles), row_tile)
            columns = span(half * (part // column_tile) + t // row_tiles, column_tile)
            u = dot(buf_a[here], w_up[:, columns], 1, 0) + up_bias[:, columns]
            square = u * u
            inner = jnp.tanh(0.7978845608 * (u + 0.044715 * (u * square)))
            outer = 0.5 * (1.0 + inner)
            hidden[here, columns] = (u * outer).astype(bf16)
            slope = outer + 0.5 * u * (1.0 - inner * inner) * (
                0.7978845608 * (1.0 + 3.0 * 0.044715 * square)
            )
            slope_grad[here, columns] = slope.astype(bf16)
            return 0

        lax.fori_loop(0, hidden_tiles, step, 0)

    def expand_back(half):
        def step(t, _):
            here = span(lax.rem(t, row_tiles), row_tile)
            columns = span(half * (part // column_tile) + t // row_tiles, column_tile)
            grad = dot(down_rows[here], w_down[columns], 1, 1)
            low = (grad * slope_grad[here, columns].astype(f32)).astype(bf16)
            slope_grad[here, columns] = low
            up_sums[:, columns] += jnp.sum(low.astype(f32), axis=0, keepdims=True)
            return 0

        lax.fori_loop(0, hidden_tiles, step, 0)

    def second(half):
        def step(t, _):
            here = span(lax.rem(t, row_tiles), row_tile)
            columns = span(t // row_tiles, column_tile)
            grad = dot(slope_grad[here, halves[half]], w_up[columns, halves[half]], 1, 1)
            if half == 1:
                grad = grad + buf_b[here, columns].astype(f32)
            buf_b[here, columns] = grad.astype(bf16)
            return 0

        lax.fori_loop(0, row_tiles * (width // column_tile), step, 0)

    up_sums[...] = jnp.zeros(up_sums.shape, f32)
    expand(0)
    g_first(DOWN[0])
    for hop in range(2, ranks - 1):
        z_pass(DOWN[0], hop)
    z_own_outward(UP[1])
    z_pass(DOWN[0], ranks - 1)
    expand_back(0)
    g_first(UP[0])
    z_pass(UP[1], 1)
    for hop in range(2, ranks - 1):
        z_pass(UP[1], hop)
    z_own_outward(DOWN[1])
    z_pass(UP[1], ranks - 1)
    expand(1)
    g_first(DOWN[1])
    z_pass(DOWN[1], 1)
    for half in range(2):
        g_own_term(DOWN[half], stage_b.at[halves[half]])
    second(0)
    for hop in range(2, ranks):
        z_pass(DOWN[1], hop)
    expand_back(1)
    g_first(UP[1], 0, 1)

    second(1)
    for g in (DOWN[0], UP[0], DOWN[1]):
        g_pass(g)
    scatter = scatter_of(buf_b)
    gather = gather_of(down_rows)
    scatter.begin()
    g_first(UP[1], 1)
    for s in range(bits - 1):
        scatter.all(s)
    g_pass(UP[1], 0, 1)
    sums[...] = jnp.zeros(sums.shape, f32)
    for c in range(CHUNKS):
        here = pl.ds(c * sub, sub)
        xhat, inverse = row_stats(middle[here])
        upstream = scatter.total(c)
        grad = down_rows[rows(me, c)].astype(f32) + norm_back(upstream, xhat, inverse, vectors[3:4])
        middle_grad[here] = grad
        low = grad.astype(bf16)
        down_rows[rows(me, c)] = low
        gather.stage(c, 0)
        sums[0:1] += jnp.sum(upstream * xhat, axis=0, keepdims=True)
        sums[1:2] += jnp.sum(upstream, axis=0, keepdims=True)
        sums[2:3] += jnp.sum(low.astype(f32), axis=0, keepdims=True)
    for s in range(1, bits - 1):
        gather.all(s)
    scatter.finish()

    def contract_step(t, _):
        here = span(lax.rem(t, tokens // row_tile), row_tile)
        columns = span(t // (tokens // row_tile), column_tile)
        buf_b[here, columns] = dot(hidden[here], w_down[:, columns], 1, 0).astype(bf16)
        return 0

    lax.fori_loop(0, (tokens // row_tile) * (width // column_tile), contract_step, 0)
    for k in range(7):
        z_sent(k)

    @pl.when(has_right)
    def _():
        pl.semaphore_signal(free_sem, inc=1, device_id={"row": right}, device_id_type=MESH)

    @pl.when(has_left)
    def _():
        pl.semaphore_signal(free_sem, inc=1, device_id={"row": left}, device_id_type=MESH)

    gather.all(bits - 1)
    g_pass(UP[1], 1)
    gather.finish()
    for half in range(2):
        g_own_add(DOWN[half], stage_b.at[halves[half]])
    down_store = local(stage_b, downg_hbm, 0)

    scatter = scatter_of(buf_b)
    scatter.begin()
    pl.semaphore_wait(free_sem, has_left.astype(jnp.int32) + has_right.astype(jnp.int32))
    g_first(OUT)

    def attended_step(i, _):
        here = span(i, row_tile)
        value = dot(down_rows[here], w_out[...], 1, 1).astype(bf16)
        hidden[here, in_width : in_width + share] = value
        return 0

    lax.fori_loop(0, tokens // row_tile, attended_step, 0)
    down_store.wait()
    if kv_sum.shape[1] == LEN:
        key_sum, value_sum = kv_sum.at[0], kv_sum.at[1]
    else:
        key_sum, value_sum = stage_b.at[:, 0:HEAD], stage_b.at[:, HEAD : 2 * HEAD]

    def attend_back(h, _):
        for start in range(0, tokens, LEN):
            sequence = slice(start, start + LEN)
            key_sum[0:LEN] = jnp.zeros((LEN, HEAD), f32)
            value_sum[0:LEN] = jnp.zeros((LEN, HEAD), f32)
            for i in range(LEN // tile):
                seen = (i + 1) * tile
                q_rows = slice(start + i * tile, start + seen)
                k_rows = slice(start, start + seen)
                s = scores(h, q_rows, k_rows, i * tile)
                kept = jnp.sum(
                    jnp.where(lane == h, logsum[q_rows], 0.0), axis=1, keepdims=True
                )
                probability = jnp.exp(s - kept)
                result_grad = hidden[q_rows, columns_of(3, h)]
                weight_grad = dot(result_grad, qkv[k_rows, columns_of(2, h)], 1, 1)
                inner = jnp.sum(probability * weight_grad, axis=1, keepdims=True)
                score_grad = (probability * (weight_grad - inner)).astype(bf16)
                value_sum[0:seen] += dot(probability.astype(bf16), result_grad, 0, 0)
                key_sum[0:seen] += dot(score_grad, qkv[q_rows, columns_of(0, h)], 0, 0)
                hidden[q_rows, columns_of(0, h)] = (
                    dot(score_grad, qkv[k_rows, columns_of(1, h)], 1, 0) * score_scale
                ).astype(bf16)
            hidden[sequence, columns_of(1, h)] = (key_sum[0:LEN] * score_scale).astype(bf16)
            hidden[sequence, columns_of(2, h)] = value_sum[0:LEN].astype(bf16)
        return 0

    scatter.all(0)
    lax.fori_loop(0, heads_here, attend_back, 0)

    g_first(QKV)
    g_pass(OUT)
    for s in range(1, bits - 1):
        scatter.all(s)

    for half in range(2):
        g_own_term(UP[half], stage_a.at[:, halves[half]])
        g_own_add(UP[half], stage_a.at[:, halves[half]])
    up_store = local(stage_a, upg_hbm, 1)

    def exchange(staged, out, c, base):
        copies = []
        for i in range(1, n):
            peer = lax.rem(me + i, n)
            copy = remote(
                staged.at[:, span(peer, share)], out.at[rows(me, c)],
                ex_send.at[base + c, i], ex_recv.at[base + c, i], peer,
            )
            copy.start()
            copies.append(copy)
        copy = pltpu.make_async_copy(
            staged.at[:, mine], out.at[rows(me, c)], ex_send.at[base + c, 0]
        )
        copy.start()
        return copies + [copy]

    result_copies = []
    for c in range(CHUNKS):
        here = pl.ds(c * sub, sub)
        result = middle[here] + (scatter.total(c) + vectors[5:6])
        buf_b[rows(me, c)] = result.astype(bf16)
    scatter.finish()
    for c in range(CHUNKS):
        result_copies += exchange(buf_b.at[rows(me, c)], out_hbm, c, 0)

    def first_step(t, _):
        here = span(lax.rem(t, tokens // row_tile), row_tile)
        columns = span(t // (tokens // row_tile), column_tile)
        buf_a[here, columns] = dot(hidden[here, 0:in_width], w_in[columns], 1, 1).astype(bf16)
        return 0

    lax.fori_loop(0, (tokens // row_tile) * (width // column_tile), first_step, 0)
    g_pass(QKV, 0, 1)
    for copy in result_copies:
        copy.wait()
    scatter = scatter_of(buf_a)
    scatter.begin()
    local_sums[5:6] = jnp.sum(hidden[:, 0:share].astype(f32), axis=0, keepdims=True)
    local_sums[6:7] = jnp.sum(
        hidden[:, 2 * share : in_width].astype(f32), axis=0, keepdims=True
    )
    for k in range(units // share):
        local_sums[8 + k : 9 + k] = up_sums[:, k * share : (k + 1) * share]
    scatter.all(0)

    g_own_term(OUT, stage_b.at[0:share])
    g_own_add(OUT, stage_b.at[0:share])
    out_store = local(stage_b.at[0:share], og_hbm, 0)
    for s in range(1, bits - 1):
        scatter.all(s)
    g_pass(QKV, 1)
    input_copies = []
    for c in range(CHUNKS):
        here = pl.ds(c * sub, sub)
        xhat, inverse = row_stats(x_own[here].astype(f32))
        upstream = scatter.total(c)
        middle_grad[here] += norm_back(upstream, xhat, inverse, vectors[0:1])
        input_copies += exchange(middle_grad.at[here], xg_hbm, c, CHUNKS)
        sums[3:4] += jnp.sum(upstream * xhat, axis=0, keepdims=True)
        sums[4:5] += jnp.sum(upstream, axis=0, keepdims=True)
    vec_back = []
    for i in range(1, n):
        peer = lax.rem(me + i, n)
        copy = remote(
            sums.at[:, span(peer, share)], landed.at[i],
            ex_send.at[2 * CHUNKS, i], ex_recv.at[2 * CHUNKS, i], peer,
        )
        copy.start()
        vec_back.append(copy)
    up_store.wait()
    g_own_term(QKV, stage_a.at[:, 0:in_width])
    summed = sums[:, mine]
    for copy in vec_back:
        copy.wait_recv()
    for i in range(1, n):
        summed = summed + landed[i]
    local_sums[0:5] = summed[0:5]
    row_copies = []
    for i in range(1, ranks):
        copy = remote(
            local_sums, row_landed.at[i], row_send.at[i], row_recv.at[i],
            lax.rem(row + i, ranks), "row",
        )
        copy.start()
        row_copies.append(copy)
    g_own_add(QKV, stage_a.at[:, 0:in_width])
    in_stores = [
        local(stage_a.at[:, i * share : (i + 1) * share], hbm, 1 + i)
        for i, hbm in enumerate((qg_hbm, kg_hbm, vg_hbm))
    ]
    total = local_sums[...]
    for i, copy in enumerate(row_copies):
        copy.wait_recv()
        total = total + row_landed[i + 1]
    small_ref[...] = total
    for copy in vec_copies + vec_back + row_copies:
        copy.wait_send()
    for g in range(6):
        g_sent(g)
    scatter.finish()
    for copy in input_copies + in_stores + [out_store]:
        copy.wait()


def layer(arrays, hbm_weights, vectors, n, ranks):
    inputs, cotangent = arrays
    tokens, share = inputs.shape
    width = n * share
    depth = hbm_weights[0].shape[0]
    units = vectors[-1].shape[1]
    block = tokens // n
    sub = block // CHUNKS
    half = n // 2
    low = lambda *shape: pltpu.VMEM(shape, bf16)
    wide = lambda *shape: pltpu.VMEM(shape, f32)
    dma = lambda *shape: pltpu.SemaphoreType.DMA(shape)
    vmem = pl.BlockSpec(memory_space=pltpu.VMEM)
    hbm = pl.BlockSpec(memory_space=pl.ANY)
    scratch = [
        low(width, 3 * share),
        low(share, width),
        low(width, units),
        low(units, width),
        low(tokens, width),
        low(tokens, width),
        low(tokens, width),
        low(tokens, width),
        low(half, CHUNKS, sub, width),
        low(half - 1, CHUNKS, sub, width),
        low(tokens, 3 * share),
        low(tokens, share),
        low(tokens, units),
        low(tokens, units),
        low(ranks + 1, units, depth),
        low(ranks + 1, depth, units),
        wide(depth, units),
        wide(units, depth),
        wide(block, width),
        wide(block, width),
        low(block, width),
        wide(tokens, HEAD),
        wide(2, 8 if units >= LEN and depth >= 2 * HEAD else LEN, HEAD),
        wide(8, width),
        wide(8, width),
        wide(8 + units // share, share),
        wide(1, units),
        wide(1, 3 * share),
        wide(n, 8, share),
        wide(ranks, 8 + units // share, share),
        dma(8),
        dma(CHUNKS, n),
        dma(CHUNKS, n),
        dma(CHUNKS, n),
        dma(CHUNKS, n),
        dma(CHUNKS, half),
        dma(CHUNKS, half),
        dma(CHUNKS, half),
        dma(CHUNKS, half),
        dma(7, 2, ranks),
        dma(7, 2, ranks),
        dma(6, ranks + 1),
        dma(6, ranks + 1),
        dma(n),
        dma(n),
        dma(2 * CHUNKS + 1, n),
        dma(2 * CHUNKS + 1, n),
        dma(ranks),
        dma(ranks),
        pltpu.SemaphoreType.REGULAR,
    ]
    outs = (
        jax.ShapeDtypeStruct((tokens, share), bf16),
        jax.ShapeDtypeStruct((tokens, share), f32),
        jax.ShapeDtypeStruct((depth, share), f32),
        jax.ShapeDtypeStruct((depth, share), f32),
        jax.ShapeDtypeStruct((depth, share), f32),
        jax.ShapeDtypeStruct((share, depth), f32),
        jax.ShapeDtypeStruct((depth, units), f32),
        jax.ShapeDtypeStruct((units, depth), f32),
        jax.ShapeDtypeStruct((8 + units // share, share), f32),
    )
    return pl.pallas_call(
        functools.partial(layer_kernel, n, ranks),
        out_shape=outs,
        in_specs=[hbm] * 8 + [vmem] * 9,
        out_specs=tuple([hbm] * 8 + [vmem]),
        scratch_shapes=scratch,
        compiler_params=pltpu.CompilerParams(
            collective_id=1, has_side_effects=True, vmem_limit_bytes=VMEM_LIMIT
        ),
    )(inputs, cotangent, *hbm_weights, *vectors)


def settle_kernel(count, *refs):
    sources, targets, held = refs[:count], refs[count : 2 * count], refs[2 * count : 3 * count]
    sems = refs[3 * count]
    inward = [pltpu.make_async_copy(sources[i], held[i], sems.at[0, i]) for i in range(count)]
    outward = [pltpu.make_async_copy(held[i], targets[i], sems.at[1, i]) for i in range(count)]
    for copy in inward:
        copy.start()
    for arrived, copy in zip(inward, outward):
        arrived.wait()
        copy.start()
    for copy in outward:
        copy.wait()


def settle(arrays):
    count = len(arrays)
    hbm = pl.BlockSpec(memory_space=pl.ANY)
    return pl.pallas_call(
        functools.partial(settle_kernel, count),
        out_shape=tuple(jax.ShapeDtypeStruct(a.shape, a.dtype) for a in arrays),
        in_specs=[hbm] * count,
        out_specs=tuple([hbm] * count),
        scratch_shapes=[pltpu.VMEM(a.shape, a.dtype) for a in arrays]
        + [pltpu.SemaphoreType.DMA((2, count))],
        compiler_params=pltpu.CompilerParams(vmem_limit_bytes=VMEM_LIMIT),
    )(*arrays)


def per_device(
    inputs,
    norm1_gain,
    norm1_shift,
    query_weight,
    query_bias,
    key_weight,
    value_weight,
    value_bias,
    output_weight,
    output_bias,
    norm2_gain,
    norm2_shift,
    expand_weight,
    expand_bias,
    contract_weight,
    contract_bias,
    cotangent,
):
    cols = lax.axis_size("col")
    ranks = lax.axis_size("row")
    row = lax.axis_index("row")
    share = inputs.shape[1]
    units = expand_weight.shape[1]
    weights = (
        query_weight,
        key_weight,
        value_weight,
        output_weight,
        expand_weight,
        contract_weight,
    )
    (
        outputs,
        input_grad,
        query_grad,
        key_grad,
        value_grad,
        output_grad,
        expand_grad,
        contract_grad,
        small,
    ) = layer(
        (inputs, cotangent),
        weights,
        [
            vector[None]
            for vector in (
                norm1_gain,
                norm1_shift,
                output_bias,
                norm2_gain,
                norm2_shift,
                contract_bias,
                query_bias,
                value_bias,
                expand_bias,
            )
        ],
        cols,
        ranks,
    )
    (
        outputs,
        input_grad,
        query_grad,
        key_grad,
        value_grad,
        output_grad,
        expand_grad,
        contract_grad,
    ) = settle(
        (
            outputs,
            input_grad,
            query_grad,
            key_grad,
            value_grad,
            output_grad,
            expand_grad,
            contract_grad,
        )
    )
    piece = share // ranks
    vector = lax.dynamic_slice_in_dim(small[:8], row * piece, piece, 1)
    wide = small[8:].reshape(units)
    expand_bias_grad = lax.dynamic_slice_in_dim(wide, row * (units // ranks), units // ranks, 0)
    return (
        outputs,
        input_grad,
        vector[3],
        vector[4],
        query_grad,
        vector[5],
        key_grad,
        value_grad,
        vector[6],
        output_grad,
        vector[2],
        vector[0],
        vector[1],
        expand_grad,
        expand_bias_grad,
        contract_grad,
        vector[7],
    )


def solution(mesh):
    in_specs = (
        P("row", "col"),
        P("col"),
        P("col"),
        P("row", "col"),
        P("col"),
        P("row", "col"),
        P("row", "col"),
        P("col"),
        P("col", "row"),
        P("col"),
        P("col"),
        P("col"),
        P("row", "col"),
        P("col"),
        P("col", "row"),
        P("col"),
        P("row", "col"),
    )
    out_specs = (
        P("row", "col"),
        P("row", "col"),
        P(("col", "row")),
        P(("col", "row")),
        P("row", "col"),
        P(("col", "row")),
        P("row", "col"),
        P("row", "col"),
        P(("col", "row")),
        P("col", "row"),
        P(("col", "row")),
        P(("col", "row")),
        P(("col", "row")),
        P("row", "col"),
        P(("col", "row")),
        P("col", "row"),
        P(("col", "row")),
    )
    return jax.shard_map(
        per_device, mesh=mesh, in_specs=in_specs, out_specs=out_specs, check_vma=False
    )
```

```python
import functools
import math

import jax
import jax.numpy as jnp
from jax import lax
from jax.experimental import pallas as pl
from jax.experimental.pallas import tpu as pltpu
from jax.sharding import PartitionSpec as P

HEADS = 16
HEAD = 128
LEN = 1024

epsilon = 1e-05
MESH = pl.DeviceIdType.MESH
bf16 = jnp.bfloat16
f32 = jnp.float32


def flip(index, dim):
    step = 1 << dim
    bit = (index // step) % 2
    return index + (1 - 2 * bit) * step


def flip_mask(index, mask):
    dim = 0
    while mask >> dim:
        if (mask >> dim) & 1:
            index = flip(index, dim)
        dim += 1
    return index


def chip_order(chunk, bits):
    dims = list(range(1, bits))
    start = chunk % len(dims)
    return dims[start:] + dims[:start]


def masks_over(dims):
    masks = [0]
    for dim in dims:
        masks = masks + [m | (1 << dim) for m in masks]
    return masks


def remote(src, dst, send, recv, peer, axis="col"):
    return pltpu.make_async_remote_copy(
        src_ref=src,
        dst_ref=dst,
        send_sem=send,
        recv_sem=recv,
        device_id={axis: peer},
        device_id_type=MESH,
    )


def span(index, size):
    return pl.ds(pl.multiple_of(index * size, size), size)


def dot(a, b, ca, cb):
    return lax.dot_general(a, b, (((ca,), (cb,)), ((), ())), preferred_element_type=f32)


def row_stats(values):
    average = jnp.mean(values, axis=1, keepdims=True)
    centred = values - average
    variance = jnp.mean(centred * centred, axis=1, keepdims=True)
    inverse = lax.rsqrt(variance + epsilon)
    return centred * inverse, inverse


def norm_back(upstream, xhat, inverse, gain):
    scaled = upstream * gain
    mean_scaled = jnp.mean(scaled, axis=1, keepdims=True)
    mean_product = jnp.mean(scaled * xhat, axis=1, keepdims=True)
    return inverse * (scaled - mean_scaled - xhat * mean_product)


def add_rows(target, other, step=512):
    def body(i, _):
        columns = span(i, step)
        total = target[:, columns].astype(f32) + other[:, columns].astype(f32)
        target[:, columns] = total.astype(bf16)
        return 0

    lax.fori_loop(0, target.shape[1] // step, body, 0)


class Gather:
    def __init__(self, me, bits, chunks, place, sems, base=0):
        self.me, self.bits, self.chunks, self.place = me, bits, chunks, place
        self.chip_send, self.chip_recv, self.mate_send, self.mate_recv = sems
        self.base = base
        self.held = [[me] for _ in range(chunks)]
        self.waiting = [[] for _ in range(chunks)]
        self.mates, self.sent = [], []

    def stage(self, c, s):
        order = chip_order(c, self.bits)
        if s == 0:
            new, base = [self.me], 0
        else:
            for copy in self.waiting[c]:
                copy.wait_recv()
            base = len(self.held[c])
            new = [flip(b, order[s - 1]) for b in self.held[c]]
            self.held[c] = self.held[c] + new
        if s < self.bits - 1:
            copies = []
            for i, b in enumerate(self.held[c]):
                slot = (1 << s) - 1 + i
                home = self.place(b, c)
                copy = remote(
                    home,
                    home,
                    self.chip_send.at[self.base + c, slot],
                    self.chip_recv.at[self.base + c, slot],
                    flip(self.me, order[s]),
                )
                copy.start()
                copies.append(copy)
            self.waiting[c] = copies
            self.sent.extend(copies)
        for i, b in enumerate(new):
            home = self.place(b, c)
            copy = remote(
                home,
                home,
                self.mate_send.at[self.base + c, base + i],
                self.mate_recv.at[self.base + c, base + i],
                flip(self.me, 0),
            )
            copy.start()
            self.mates.append(copy)

    def all(self, s):
        for c in range(self.chunks):
            self.stage(c, s)

    def finish(self):
        for copy in self.sent:
            copy.wait_send()
        for copy in self.mates:
            copy.wait()


class Scatter:
    def __init__(self, me, bits, chunks, partial, rows, first, later, sems):
        self.me, self.bits, self.chunks = me, bits, chunks
        self.partial, self.rows, self.first, self.later = partial, rows, first, later
        self.core_send, self.core_recv, self.chip_send, self.chip_recv = sems
        self.core, self.chip = {}, {}

    def ranked(self, c):
        lead = chip_order(c, self.bits)[0]
        every = masks_over(list(range(1, self.bits)))
        return lead, sorted(every, key=lambda m: (0 if (m >> lead) & 1 else 1, m))

    def base(self, s):
        return sum(1 << (self.bits - 2 - k) for k in range(s))

    def start(self, c):
        mate = flip(self.me, 0)
        for m in self.ranked(c)[1]:
            slot = m >> 1
            copy = remote(
                self.partial.at[self.rows(flip_mask(mate, m), c)],
                self.first.at[slot, c],
                self.core_send.at[c, slot],
                self.core_recv.at[c, slot],
                mate,
            )
            copy.start()
            self.core[c, m] = copy

    def send(self, c, s, m):
        order = chip_order(c, self.bits)
        kept = m & ~(1 << order[s])
        i = self.base(s) + masks_over(order[s + 1 :]).index(kept)
        copy = remote(
            self.first.at[m >> 1, c],
            self.later.at[i, c],
            self.chip_send.at[c, i],
            self.chip_recv.at[c, i],
            flip(self.me, order[s]),
        )
        copy.start()
        self.chip[c, s, kept] = copy

    def add(self, c, s):
        order = chip_order(c, self.bits)
        if s == 0:
            lead, ranked = self.ranked(c)
            for m in ranked:
                self.core[c, m].wait_recv()
                slot = m >> 1
                mine = self.partial.at[self.rows(flip_mask(self.me, m), c)]
                add_rows(self.first.at[slot, c], mine)
                if (m >> lead) & 1:
                    self.send(c, s, m)
        else:
            for i, m in enumerate(masks_over(order[s:])):
                self.chip[c, s - 1, m].wait_recv()
                slot = m >> 1
                add_rows(self.first.at[slot, c], self.later.at[self.base(s - 1) + i, c])
            for m in masks_over(order[s + 1 :]):
                self.send(c, s, m | (1 << order[s]))

    def total(self, c):
        s = self.bits - 2
        self.chip[c, s, 0].wait_recv()
        return self.first[0, c].astype(f32) + self.later[self.base(s), c].astype(f32)

    def begin(self):
        for c in range(self.chunks):
            self.start(c)

    def all(self, s):
        for c in range(self.chunks):
            self.add(c, s)

    def finish(self):
        for copy in list(self.core.values()) + list(self.chip.values()):
            copy.wait_send()


QKV, OUT = 0, 1
UP = (2, 4)
DOWN = (3, 5)
IN = (0, 6)
DOWN_PARTS = (3, 5, 7)
CHUNKS = 4
VMEM_LIMIT = 65024 << 10


def layer_kernel(n, ranks, *refs):
    (
        x_hbm, cot_hbm, q_hbm, k_hbm, v_hbm, o_hbm, up_hbm, down_hbm,
        gain1, shift1, bias_o, gain2, shift2, bias_c, bias_q, bias_v, up_bias,
        out_hbm, xg_hbm, qg_hbm, kg_hbm, vg_hbm, og_hbm, upg_hbm, downg_hbm, small_ref,
        w_in, w_out, w_up, w_down, normed1, down_rows, buf_a, buf_b, first, later,
        qkv, attended, slope_grad, hidden, slots_down, slots_up,
        stage_a, stage_b, middle, middle_grad, x_own, logsum, kv_sum, vectors, sums,
        local_sums, up_sums, in_bias, landed, row_landed,
        local_sem, gather_a, gather_b, gather_c, gather_d,
        scatter_a, scatter_b, scatter_c, scatter_d,
        z_send, z_recv, g_send, g_recv, vec_send, vec_recv, ex_send, ex_recv,
        row_send, row_recv, free_sem,
    ) = refs
    bits = n.bit_length() - 1
    me = lax.axis_index("col")
    row = lax.axis_index("row")
    tokens, width = normed1.shape
    share = width // n
    depth = width // ranks
    units = hidden.shape[1]
    block = tokens // n
    sub = block // CHUNKS
    heads_here = share // HEAD
    in_width = 3 * share
    part = units // 2
    halves = (slice(0, part), slice(part, units))
    quarter = part // 2
    down_parts = (slice(0, part), slice(part, part + quarter), slice(part + quarter, units))
    in_split = in_width // (2 * HEAD) * HEAD
    in_parts = (slice(0, in_split), slice(in_split, in_width))
    in_grad = hidden.at[:, 0:in_width]
    score_scale = 1.0 / math.sqrt(HEAD)
    right, left = row + 1, row - 1
    has_left, has_right = row > 0, row < ranks - 1
    is_end = jnp.logical_or(row == 0, row == ranks - 1)
    is_inner = jnp.logical_not(is_end)

    def local(src, dst, i):
        copy = pltpu.make_async_copy(src, dst, local_sem.at[i])
        copy.start()
        return copy

    def rows(b, c):
        return pl.ds(pl.multiple_of(b * block + c * sub, sub), sub)

    mine = span(me, share)

    def z_block(k, b):
        if k in IN:
            return w_in.at[span(b, depth), in_parts[IN.index(k)]]
        if k == OUT:
            return w_out.at[:, span(b, depth)]
        if k in UP:
            return w_up.at[span(b, depth), halves[UP.index(k)]]
        return w_down.at[down_parts[DOWN_PARTS.index(k)], span(b, depth)]

    def z_copy(k, way, hop):
        b = row - hop if way == 0 else row + hop
        peer = right if way == 0 else left
        return remote(
            z_block(k, b), z_block(k, b), z_send.at[k, way, hop], z_recv.at[k, way, hop],
            peer, "row",
        )

    def z_landing(k, way, hop):
        b = row - hop if way == 0 else row + hop
        return remote(
            z_block(k, b), z_block(k, b), z_send.at[k, way, hop - 1],
            z_recv.at[k, way, hop - 1], left if way == 0 else right, "row",
        )

    in_low = row < ranks // 2
    in_high = jnp.logical_not(in_low)

    def z_own(k, to_right=has_right, to_left=has_left):
        @pl.when(jnp.logical_and(has_right, to_right))
        def _():
            z_copy(k, 0, 0).start()

        @pl.when(jnp.logical_and(has_left, to_left))
        def _():
            z_copy(k, 1, 0).start()

    def z_own_end(k):
        z_own(k, is_end, is_end)

    def z_own_inward(k):
        z_own(k, jnp.logical_and(is_inner, in_low), jnp.logical_and(is_inner, in_high))

    def z_own_outward(k):
        z_own(k, jnp.logical_and(is_inner, in_high), jnp.logical_and(is_inner, in_low))

    def z_pass(k, hop):
        @pl.when(row >= hop)
        def _():
            z_landing(k, 0, hop).wait_recv()
            if hop < ranks - 1:

                @pl.when(has_right)
                def _():
                    z_copy(k, 0, hop).start()

        @pl.when(row + hop <= ranks - 1)
        def _():
            z_landing(k, 1, hop).wait_recv()
            if hop < ranks - 1:

                @pl.when(has_left)
                def _():
                    z_copy(k, 1, hop).start()

    def z_sent(k):
        for hop in range(ranks - 1):

            @pl.when(jnp.logical_and(row >= hop, has_right))
            def _():
                z_copy(k, 0, hop).wait_send()

            @pl.when(jnp.logical_and(row + hop <= ranks - 1, has_left))
            def _():
                z_copy(k, 1, hop).wait_send()

    def slot(g, s):
        if g in DOWN:
            return slots_down.at[s, halves[DOWN.index(g)]]
        if g in UP:
            return slots_up.at[s, :, halves[UP.index(g)]]
        if g == OUT:
            return w_down.at[
                pl.ds(pl.multiple_of(depth + (s // ranks) * share, share), share),
                span(lax.rem(s, ranks), depth),
            ]
        return w_up.at[span(s, depth), 0:in_width]

    def last_slot(g):
        if g == QKV:
            return w_down.at[0:depth, 0:in_width]
        return slot(g, ranks)

    def term(g, c, write):
        if g in DOWN:
            half = DOWN.index(g)
            tile = min(256, part)

            def step(i, _):
                columns = span(half * (part // tile) + i, tile)
                value = dot(hidden[:, columns], down_rows[:, span(c, depth)], 0, 0)
                write(span(i, tile), slice(0, depth), value)
                return 0

            lax.fori_loop(0, part // tile, step, 0)
        elif g in UP:
            value = dot(buf_a[:, span(c, depth)], slope_grad[:, halves[UP.index(g)]], 0, 0)
            write(slice(0, depth), slice(0, part), value)
        elif g == OUT:
            value = dot(attended[...], down_rows[:, span(c, depth)], 0, 0)
            write(slice(0, share), slice(0, depth), value)
        else:

            def step(j, _):
                value = dot(normed1[:, span(c, depth)], hidden[:, span(j, share)], 0, 0)
                write(slice(0, depth), span(j, share), value)
                return 0

            lax.fori_loop(0, 3, step, 0)

    def chunk_at(k, mixed=False):
        ups, downs = ranks - 1 - row, row
        if mixed and ranks == 4:
            from_low = jnp.where(
                k == 0, ranks - 1, jnp.where(k <= downs, k - 1, ranks - 1 - (k - downs))
            )
            from_high = jnp.where(k == 0, 0, jnp.where(k <= ups, ranks - k, k - ups))
        else:
            from_low = jnp.where(k < ups, ranks - 1 - k, k - ups)
            from_high = jnp.where(k < downs, k, ranks - 1 - (k - downs))
        return jnp.where(row < ranks // 2, from_low, from_high)

    def g_copy(g, c, way, to_owner=False):
        src = slot(g, c)
        dst = last_slot(g) if to_owner else slot(g, c)
        sem = g_recv.at[g, ranks] if to_owner else g_recv.at[g, c]
        return remote(src, dst, g_send.at[g, c], sem, right if way == 0 else left, "row")

    def g_start(g, c):
        @pl.when(c > row)
        def _():
            g_copy(g, c, 0).start()

        @pl.when(jnp.logical_and(c < row, c == left))
        def _():
            g_copy(g, c, 1, True).start()

        @pl.when(jnp.logical_and(c < row, c != left))
        def _():
            g_copy(g, c, 1).start()

    def g_first(g, begin=0, end=ranks - 1):
        if begin >= end:
            return

        @pl.when(is_end)
        def _():
            def step(k, _):
                c = chunk_at(k)
                here = slot(g, c)

                def write(r, q, value):
                    here[r, q] = value.astype(bf16)

                term(g, c, write)
                g_start(g, c)
                return 0

            lax.fori_loop(begin, end, step, 0)

    def g_pass(g, begin=0, end=ranks - 1):
        if begin >= end:
            return

        @pl.when(jnp.logical_not(is_end))
        def _():
            def step(k, _):
                c = chunk_at(k, g == QKV)
                here = slot(g, c)
                g_copy(g, c, 0).wait_recv()

                def write(r, q, value):
                    here[r, q] = (here[r, q].astype(f32) + value).astype(bf16)

                term(g, c, write)
                g_start(g, c)
                return 0

            lax.fori_loop(begin, end, step, 0)

    def g_own_term(g, stage):
        def write(r, q, value):
            stage[r, q] = value

        term(g, row, write)

    def g_own_add(g, stage, step=64):
        def add(here):
            def body(i, _):
                r = span(i, step)
                stage[r] += here[r].astype(f32)
                return 0

            lax.fori_loop(0, here.shape[0] // step, body, 0)

        @pl.when(has_left)
        def _():
            g_copy(g, row, 0).wait_recv()
            add(slot(g, row))

        @pl.when(has_right)
        def _():
            g_copy(g, row, 1, True).wait_recv()
            add(last_slot(g))

    def g_sent(g):
        for k in range(ranks - 1):
            g_copy(g, chunk_at(k), 0).wait_send()

    x_load = local(x_hbm, normed1.at[:, mine], 0)
    in_loads = [
        local(hbm, stage_a.at[0:depth, i * share : (i + 1) * share], 1 + i)
        for i, hbm in enumerate((q_hbm, k_hbm, v_hbm))
    ]
    o_load = local(o_hbm, stage_b.at[0:share, :], 4)
    cot_load = local(cot_hbm, down_rows.at[:, mine], 5)

    barrier = pltpu.get_barrier_semaphore()
    for i in range(1, n):
        pl.semaphore_signal(
            barrier, inc=1, device_id={"col": lax.rem(me + i, n)}, device_id_type=MESH
        )
    for i in range(1, ranks):
        pl.semaphore_signal(
            barrier, inc=1, device_id={"row": lax.rem(row + i, ranks)}, device_id_type=MESH
        )
    pl.semaphore_wait(barrier, n - 1 + ranks - 1)

    gather_sems = (gather_a, gather_b, gather_c, gather_d)
    scatter_sems = (scatter_a, scatter_b, scatter_c, scatter_d)
    half = tokens // 2

    def feature_place(ref):
        def place(b, c):
            return ref.at[pl.ds(c * half, half), span(b, share)]

        return place

    gather_x = Gather(me, bits, 2, feature_place(normed1), gather_sems)
    gather_g = Gather(me, bits, 2, feature_place(down_rows), gather_sems, 2)
    x_load.wait()
    gather_x.all(0)
    for i, ref in enumerate((gain1, shift1, bias_o, gain2, shift2, bias_c)):
        vectors[i : i + 1, mine] = ref[...]
    in_bias[...] = jnp.zeros(in_bias.shape, f32)
    in_bias[:, 0:share] = bias_q[...]
    in_bias[:, 2 * share : in_width] = bias_v[...]
    vec_copies = []
    for i in range(1, n):
        copy = remote(
            vectors.at[:, mine], vectors.at[:, mine], vec_send.at[i], vec_recv.at[i],
            lax.rem(me + i, n),
        )
        copy.start()
        vec_copies.append(copy)
    for copy in in_loads:
        copy.wait()
    w_in[span(row, depth)] = stage_a[:, 0:in_width].astype(bf16)
    z_own(IN[0])
    up_load = local(up_hbm, stage_a, 1)
    o_load.wait()
    w_out[:, span(row, depth)] = stage_b[0:share, :].astype(bf16)
    z_own_outward(OUT)
    down_load = local(down_hbm, stage_b, 2)
    cot_load.wait()
    local_sums[7:8] = jnp.sum(down_rows[:, mine].astype(f32), axis=0, keepdims=True)
    gather_x.all(1)
    up_load.wait()
    w_up[span(row, depth)] = stage_a[...].astype(bf16)
    down_load.wait()
    w_down[:, span(row, depth)] = stage_b[...].astype(bf16)
    for s in range(2, bits - 1):
        gather_x.all(s)
    z_own(IN[1])
    z_pass(IN[0], 1)
    gather_x.all(bits - 1)
    gather_g.all(0)
    z_own_end(OUT)
    z_own_end(UP[0])
    z_own_end(DOWN[0])
    gather_x.finish()
    for copy in vec_copies:
        copy.wait_recv()
    x_own[...] = normed1[span(me, block)]

    def norm_step(i, _):
        here = span(i, 64)
        xhat, _ = row_stats(normed1[here].astype(f32))
        normed1[here] = (xhat * vectors[0:1] + vectors[1:2]).astype(bf16)
        return 0

    lax.fori_loop(0, tokens // 64, norm_step, 0)
    z_pass(IN[1], 1)
    if ranks > 3:
        z_pass(IN[0], 2)
    z_own_inward(OUT)
    for s in range(1, bits - 1):
        gather_g.all(s)
    for hop in range(2, ranks - 1):
        z_pass(IN[1], hop)
        if hop + 1 < ranks - 1:
            z_pass(IN[0], hop + 1)
    gather_g.all(bits - 1)
    z_own_end(UP[1])
    z_own_end(DOWN_PARTS[1])
    z_own_end(DOWN_PARTS[2])
    z_pass(IN[0], ranks - 1)
    z_pass(IN[1], ranks - 1)

    def qkv_step(j, _):
        columns = span(j, share)
        qkv[:, columns] = (dot(normed1[...], w_in[:, columns], 1, 0) + in_bias[:, columns]).astype(bf16)
        return 0

    lax.fori_loop(0, 3, qkv_step, 0)
    z_pass(OUT, 1)
    z_own_inward(UP[0])
    tile = 256

    def slope_of(h):
        number = jnp.full((1, 1), me * heads_here + h + 1, jnp.int32).astype(f32)
        return jnp.exp2(-8.0 / HEADS * number)

    def columns_of(which, h):
        return pl.ds(pl.multiple_of(which * share + h * HEAD, HEAD), HEAD)

    def blocks():
        for start in range(0, tokens, LEN):
            for i in range(LEN // tile):
                seen = (i + 1) * tile
                yield slice(start + i * tile, start + seen), slice(start, start + seen), i * tile

    def scores(h, q_rows, k_rows, offset):
        raw = dot(qkv[q_rows, columns_of(0, h)], qkv[k_rows, columns_of(1, h)], 1, 1) * score_scale
        shape = raw.shape
        distance = lax.broadcasted_iota(jnp.int32, shape, 1) - (
            lax.broadcasted_iota(jnp.int32, shape, 0) + offset
        )
        raw = raw + slope_of(h) * distance.astype(f32)
        return jnp.where(distance <= 0, raw, -jnp.inf)

    lane = lax.broadcasted_iota(jnp.int32, (tile, HEAD), 1)

    def attend(h, _):
        for q_rows, k_rows, offset in blocks():
            s = scores(h, q_rows, k_rows, offset)
            top = jnp.max(s, axis=1, keepdims=True)
            exponent = jnp.exp(s - top)
            total = jnp.sum(exponent, axis=1, keepdims=True)
            weights = (exponent / total).astype(bf16)
            attended[q_rows, columns_of(0, h)] = dot(
                weights, qkv[k_rows, columns_of(2, h)], 1, 0
            ).astype(bf16)
            logsum[q_rows] = jnp.where(lane == h, top + jnp.log(total), logsum[q_rows])
        return 0

    logsum[...] = jnp.zeros(logsum.shape, f32)
    lax.fori_loop(0, heads_here, attend, 0)
    for hop in range(2, ranks - 1):
        z_pass(OUT, hop)
    z_own_outward(UP[0])
    z_own_inward(DOWN[0])
    gather_g.finish()
    z_pass(OUT, ranks - 1)

    column_tile = 256

    def branch_step(j, _):
        columns = span(j, column_tile)
        buf_b[:, columns] = dot(attended[...], w_out[:, columns], 1, 0).astype(bf16)
        return 0

    lax.fori_loop(0, width // column_tile, branch_step, 0)

    def scatter_of(partial):
        return Scatter(me, bits, CHUNKS, partial, rows, first, later, scatter_sems)

    def gather_of(ref):
        return Gather(me, bits, CHUNKS, lambda b, c: ref.at[rows(b, c)], gather_sems)

    scatter = scatter_of(buf_b)
    gather = gather_of(buf_a)
    scatter.begin()
    scatter.all(0)
    for s in range(1, bits - 1):
        scatter.all(s)
    z_pass(UP[0], 1)
    z_own_inward(UP[1])
    for c in range(CHUNKS):
        here = pl.ds(c * sub, sub)
        values = x_own[here].astype(f32) + (scatter.total(c) + vectors[2:3])
        middle[here] = values
        xhat, _ = row_stats(values)
        buf_a[rows(me, c)] = (xhat * vectors[3:4] + vectors[4:5]).astype(bf16)
        gather.stage(c, 0)
    for hop in range(2, ranks - 1):
        z_pass(UP[0], hop)
    for s in range(1, bits - 1):
        gather.all(s)
    z_own_outward(DOWN[0])
    scatter.finish()
    gather.all(bits - 1)
    z_own_inward(DOWN_PARTS[1])
    z_own_inward(DOWN_PARTS[2])
    gather.finish()
    z_pass(UP[0], ranks - 1)

    row_tile = 512
    row_tiles = tokens // row_tile
    hidden_tiles = row_tiles * (part // column_tile)

    def expand(half):
        def step(t, _):
            here = span(lax.rem(t, row_tiles), row_tile)
            columns = span(half * (part // column_tile) + t // row_tiles, column_tile)
            u = dot(buf_a[here], w_up[:, columns], 1, 0) + up_bias[:, columns]
            square = u * u
            inner = jnp.tanh(0.7978845608 * (u + 0.044715 * (u * square)))
            outer = 0.5 * (1.0 + inner)
            hidden[here, columns] = (u * outer).astype(bf16)
            slope = outer + 0.5 * u * (1.0 - inner * inner) * (
                0.7978845608 * (1.0 + 3.0 * 0.044715 * square)
            )
            slope_grad[here, columns] = slope.astype(bf16)
            return 0

        lax.fori_loop(0, hidden_tiles, step, 0)

    def expand_back(piece):
        rows_here = down_parts[piece]
        step_size = min(column_tile, rows_here.stop - rows_here.start)
        begin = rows_here.start // step_size
        steps = (rows_here.stop - rows_here.start) // step_size

        def step(t, _):
            here = span(lax.rem(t, row_tiles), row_tile)
            columns = span(begin + t // row_tiles, step_size)
            grad = dot(down_rows[here], w_down[columns], 1, 1)
            low = (grad * slope_grad[here, columns].astype(f32)).astype(bf16)
            slope_grad[here, columns] = low
            up_sums[:, columns] += jnp.sum(low.astype(f32), axis=0, keepdims=True)
            return 0

        lax.fori_loop(0, row_tiles * steps, step, 0)

    def second(piece):
        inner = down_parts[piece]

        def step(t, _):
            here = span(lax.rem(t, row_tiles), row_tile)
            columns = span(t // row_tiles, column_tile)
            grad = dot(slope_grad[here, inner], w_up[columns, inner], 1, 1)
            if piece > 0:
                grad = grad + buf_b[here, columns].astype(f32)
            buf_b[here, columns] = grad.astype(bf16)
            return 0

        lax.fori_loop(0, row_tiles * (width // column_tile), step, 0)

    up_sums[...] = jnp.zeros(up_sums.shape, f32)
    expand(0)
    g_first(DOWN[0])
    for hop in range(1, ranks - 1):
        z_pass(DOWN[0], hop)
    z_own_outward(UP[1])
    z_pass(DOWN[0], ranks - 1)
    expand_back(0)
    g_first(UP[0])
    z_pass(UP[1], 1)
    for hop in range(2, ranks - 1):
        z_pass(UP[1], hop)
    z_own_outward(DOWN_PARTS[1])
    z_pass(UP[1], ranks - 1)
    expand(1)
    g_first(DOWN[1])
    z_pass(DOWN_PARTS[1], 1)
    for half in range(2):
        g_own_term(DOWN[half], stage_b.at[halves[half]])
    second(0)
    for hop in range(2, ranks):
        z_pass(DOWN_PARTS[1], hop)
    expand_back(1)
    z_own_outward(DOWN_PARTS[2])
    z_pass(DOWN_PARTS[2], 1)
    second(1)
    for hop in range(2, ranks):
        z_pass(DOWN_PARTS[2], hop)
    expand_back(2)
    g_first(UP[1], 0, 1)
    second(2)
    g_pass(DOWN[0])
    g_pass(UP[0])
    g_pass(DOWN[1])
    scatter = scatter_of(buf_b)
    gather = gather_of(down_rows)
    scatter.begin()
    scatter.all(0)
    g_first(UP[1], 1)
    for s in range(1, bits - 1):
        scatter.all(s)
    g_pass(UP[1], 0, 1)
    sums[...] = jnp.zeros(sums.shape, f32)
    for c in range(CHUNKS):
        here = pl.ds(c * sub, sub)
        xhat, inverse = row_stats(middle[here])
        upstream = scatter.total(c)
        grad = down_rows[rows(me, c)].astype(f32) + norm_back(upstream, xhat, inverse, vectors[3:4])
        middle_grad[here] = grad
        low = grad.astype(bf16)
        down_rows[rows(me, c)] = low
        gather.stage(c, 0)
        sums[0:1] += jnp.sum(upstream * xhat, axis=0, keepdims=True)
        sums[1:2] += jnp.sum(upstream, axis=0, keepdims=True)
        sums[2:3] += jnp.sum(low.astype(f32), axis=0, keepdims=True)
    for s in range(1, bits - 1):
        gather.all(s)
    scatter.finish()

    def contract_step(t, _):
        here = span(lax.rem(t, tokens // row_tile), row_tile)
        columns = span(t // (tokens // row_tile), column_tile)
        buf_b[here, columns] = dot(hidden[here], w_down[:, columns], 1, 0).astype(bf16)
        return 0

    lax.fori_loop(0, (tokens // row_tile) * (width // column_tile), contract_step, 0)
    for k in range(8):
        z_sent(k)

    @pl.when(has_right)
    def _():
        pl.semaphore_signal(free_sem, inc=1, device_id={"row": right}, device_id_type=MESH)

    @pl.when(has_left)
    def _():
        pl.semaphore_signal(free_sem, inc=1, device_id={"row": left}, device_id_type=MESH)

    gather.all(bits - 1)
    g_pass(UP[1], 1)
    for half in range(2):
        g_own_add(DOWN[half], stage_b.at[halves[half]])
    down_store = local(stage_b, downg_hbm, 0)
    gather.finish()

    scatter = scatter_of(buf_b)
    scatter.begin()
    pl.semaphore_wait(free_sem, has_left.astype(jnp.int32) + has_right.astype(jnp.int32))
    g_first(OUT, 0, 2)

    def attended_step(i, _):
        here = span(i, row_tile)
        value = dot(down_rows[here], w_out[...], 1, 1).astype(bf16)
        hidden[here, in_width : in_width + share] = value
        return 0

    lax.fori_loop(0, tokens // row_tile, attended_step, 0)
    down_store.wait()
    if kv_sum.shape[1] == LEN:
        key_sum, value_sum = kv_sum.at[0], kv_sum.at[1]
    else:
        key_sum, value_sum = stage_b.at[:, 0:HEAD], stage_b.at[:, HEAD : 2 * HEAD]

    def attend_back(h, _):
        for start in range(0, tokens, LEN):
            sequence = slice(start, start + LEN)
            key_sum[0:LEN] = jnp.zeros((LEN, HEAD), f32)
            value_sum[0:LEN] = jnp.zeros((LEN, HEAD), f32)
            for i in range(LEN // tile):
                seen = (i + 1) * tile
                q_rows = slice(start + i * tile, start + seen)
                k_rows = slice(start, start + seen)
                s = scores(h, q_rows, k_rows, i * tile)
                kept = jnp.sum(
                    jnp.where(lane == h, logsum[q_rows], 0.0), axis=1, keepdims=True
                )
                probability = jnp.exp(s - kept)
                result_grad = hidden[q_rows, columns_of(3, h)]
                weight_grad = dot(result_grad, qkv[k_rows, columns_of(2, h)], 1, 1)
                inner = jnp.sum(probability * weight_grad, axis=1, keepdims=True)
                score_grad = (probability * (weight_grad - inner)).astype(bf16)
                value_sum[0:seen] += dot(probability.astype(bf16), result_grad, 0, 0)
                key_sum[0:seen] += dot(score_grad, qkv[q_rows, columns_of(0, h)], 0, 0)
                hidden[q_rows, columns_of(0, h)] = (
                    dot(score_grad, qkv[k_rows, columns_of(1, h)], 1, 0) * score_scale
                ).astype(bf16)
            hidden[sequence, columns_of(1, h)] = (key_sum[0:LEN] * score_scale).astype(bf16)
            hidden[sequence, columns_of(2, h)] = value_sum[0:LEN].astype(bf16)
        return 0

    scatter.all(0)
    lax.fori_loop(0, heads_here, attend_back, 0)

    g_first(QKV, 0, 1)
    g_first(OUT, 2)
    g_pass(OUT, 0, 2)
    for s in range(1, bits - 1):
        scatter.all(s)

    for half in range(2):
        g_own_term(UP[half], stage_a.at[:, halves[half]])
        g_own_add(UP[half], stage_a.at[:, halves[half]])
    up_store = local(stage_a, upg_hbm, 1)
    g_first(QKV, 1, 2)

    def exchange(staged, out, c, base):
        copies = []
        for i in range(1, n):
            peer = lax.rem(me + i, n)
            copy = remote(
                staged.at[:, span(peer, share)], out.at[rows(me, c)],
                ex_send.at[base + c, i], ex_recv.at[base + c, i], peer,
            )
            copy.start()
            copies.append(copy)
        copy = pltpu.make_async_copy(
            staged.at[:, mine], out.at[rows(me, c)], ex_send.at[base + c, 0]
        )
        copy.start()
        return copies + [copy]

    result_copies = []
    for c in range(CHUNKS):
        here = pl.ds(c * sub, sub)
        result = middle[here] + (scatter.total(c) + vectors[5:6])
        buf_b[rows(me, c)] = result.astype(bf16)
    scatter.finish()
    for c in range(CHUNKS):
        result_copies += exchange(buf_b.at[rows(me, c)], out_hbm, c, 0)

    def first_step(t, _):
        here = span(lax.rem(t, tokens // row_tile), row_tile)
        columns = span(t // (tokens // row_tile), column_tile)
        buf_a[here, columns] = dot(hidden[here, 0:in_width], w_in[columns], 1, 1).astype(bf16)
        return 0

    lax.fori_loop(0, (tokens // row_tile) * (width // column_tile), first_step, 0)
    g_pass(OUT, 2)
    g_pass(QKV, 0, 1)
    for copy in result_copies:
        copy.wait()
    scatter = scatter_of(buf_a)
    scatter.begin()
    g_first(QKV, 2)
    local_sums[5:6] = jnp.sum(hidden[:, 0:share].astype(f32), axis=0, keepdims=True)
    local_sums[6:7] = jnp.sum(
        hidden[:, 2 * share : in_width].astype(f32), axis=0, keepdims=True
    )
    for k in range(units // share):
        local_sums[8 + k : 9 + k] = up_sums[:, k * share : (k + 1) * share]
    scatter.all(0)

    g_own_term(OUT, stage_b.at[0:share])
    g_own_add(OUT, stage_b.at[0:share])
    out_store = local(stage_b.at[0:share], og_hbm, 0)
    for s in range(1, bits - 1):
        scatter.all(s)
    g_pass(QKV, 1)
    input_copies = []
    for c in range(CHUNKS):
        here = pl.ds(c * sub, sub)
        xhat, inverse = row_stats(x_own[here].astype(f32))
        upstream = scatter.total(c)
        middle_grad[here] += norm_back(upstream, xhat, inverse, vectors[0:1])
        sums[3:4] += jnp.sum(upstream * xhat, axis=0, keepdims=True)
        sums[4:5] += jnp.sum(upstream, axis=0, keepdims=True)
    vec_back = []
    for i in range(1, n):
        peer = lax.rem(me + i, n)
        copy = remote(
            sums.at[:, span(peer, share)], landed.at[i],
            ex_send.at[2 * CHUNKS, i], ex_recv.at[2 * CHUNKS, i], peer,
        )
        copy.start()
        vec_back.append(copy)
    for c in range(CHUNKS):
        input_copies += exchange(middle_grad.at[pl.ds(c * sub, sub)], xg_hbm, c, CHUNKS)
    summed = sums[:, mine]
    for copy in vec_back:
        copy.wait_recv()
    for i in range(1, n):
        summed = summed + landed[i]
    local_sums[0:5] = summed[0:5]
    row_copies = []
    for i in range(1, ranks):
        copy = remote(
            local_sums, row_landed.at[i], row_send.at[i], row_recv.at[i],
            lax.rem(row + i, ranks), "row",
        )
        copy.start()
        row_copies.append(copy)
    up_store.wait()
    g_own_term(QKV, stage_a.at[:, 0:in_width])
    g_own_add(QKV, stage_a.at[:, 0:in_width])
    in_stores = [
        local(stage_a.at[:, i * share : (i + 1) * share], hbm, 1 + i)
        for i, hbm in enumerate((qg_hbm, kg_hbm, vg_hbm))
    ]
    total = local_sums[...]
    for i, copy in enumerate(row_copies):
        copy.wait_recv()
        total = total + row_landed[i + 1]
    small_ref[...] = total
    for copy in vec_copies + vec_back + row_copies:
        copy.wait_send()
    for g in range(6):
        g_sent(g)
    scatter.finish()
    for copy in input_copies + in_stores + [out_store]:
        copy.wait()


def layer(arrays, hbm_weights, vectors, n, ranks):
    inputs, cotangent = arrays
    tokens, share = inputs.shape
    width = n * share
    depth = hbm_weights[0].shape[0]
    units = vectors[-1].shape[1]
    block = tokens // n
    sub = block // CHUNKS
    half = n // 2
    low = lambda *shape: pltpu.VMEM(shape, bf16)
    wide = lambda *shape: pltpu.VMEM(shape, f32)
    dma = lambda *shape: pltpu.SemaphoreType.DMA(shape)
    vmem = pl.BlockSpec(memory_space=pltpu.VMEM)
    hbm = pl.BlockSpec(memory_space=pl.ANY)
    scratch = [
        low(width, 3 * share),
        low(share, width),
        low(width, units),
        low(units, width),
        low(tokens, width),
        low(tokens, width),
        low(tokens, width),
        low(tokens, width),
        low(half, CHUNKS, sub, width),
        low(half - 1, CHUNKS, sub, width),
        low(tokens, 3 * share),
        low(tokens, share),
        low(tokens, units),
        low(tokens, units),
        low(ranks + 1, units, depth),
        low(ranks + 1, depth, units),
        wide(depth, units),
        wide(units, depth),
        wide(block, width),
        wide(block, width),
        low(block, width),
        wide(tokens, HEAD),
        wide(2, 8 if units >= LEN and depth >= 2 * HEAD else LEN, HEAD),
        wide(8, width),
        wide(8, width),
        wide(8 + units // share, share),
        wide(1, units),
        wide(1, 3 * share),
        wide(n, 8, share),
        wide(ranks, 8 + units // share, share),
        dma(8),
        dma(CHUNKS, n),
        dma(CHUNKS, n),
        dma(CHUNKS, n),
        dma(CHUNKS, n),
        dma(CHUNKS, half),
        dma(CHUNKS, half),
        dma(CHUNKS, half),
        dma(CHUNKS, half),
        dma(8, 2, ranks),
        dma(8, 2, ranks),
        dma(6, ranks + 1),
        dma(6, ranks + 1),
        dma(n),
        dma(n),
        dma(2 * CHUNKS + 1, n),
        dma(2 * CHUNKS + 1, n),
        dma(ranks),
        dma(ranks),
        pltpu.SemaphoreType.REGULAR,
    ]
    outs = (
        jax.ShapeDtypeStruct((tokens, share), bf16),
        jax.ShapeDtypeStruct((tokens, share), f32),
        jax.ShapeDtypeStruct((depth, share), f32),
        jax.ShapeDtypeStruct((depth, share), f32),
        jax.ShapeDtypeStruct((depth, share), f32),
        jax.ShapeDtypeStruct((share, depth), f32),
        jax.ShapeDtypeStruct((depth, units), f32),
        jax.ShapeDtypeStruct((units, depth), f32),
        jax.ShapeDtypeStruct((8 + units // share, share), f32),
    )
    return pl.pallas_call(
        functools.partial(layer_kernel, n, ranks),
        out_shape=outs,
        in_specs=[hbm] * 8 + [vmem] * 9,
        out_specs=tuple([hbm] * 8 + [vmem]),
        scratch_shapes=scratch,
        compiler_params=pltpu.CompilerParams(
            collective_id=1, has_side_effects=True, vmem_limit_bytes=VMEM_LIMIT
        ),
    )(inputs, cotangent, *hbm_weights, *vectors)


def settle_kernel(count, *refs):
    sources, targets, held = refs[:count], refs[count : 2 * count], refs[2 * count : 3 * count]
    sems = refs[3 * count]
    inward = [pltpu.make_async_copy(sources[i], held[i], sems.at[0, i]) for i in range(count)]
    outward = [pltpu.make_async_copy(held[i], targets[i], sems.at[1, i]) for i in range(count)]
    for copy in inward:
        copy.start()
    for arrived, copy in zip(inward, outward):
        arrived.wait()
        copy.start()
    for copy in outward:
        copy.wait()


def settle(arrays):
    count = len(arrays)
    hbm = pl.BlockSpec(memory_space=pl.ANY)
    return pl.pallas_call(
        functools.partial(settle_kernel, count),
        out_shape=tuple(jax.ShapeDtypeStruct(a.shape, a.dtype) for a in arrays),
        in_specs=[hbm] * count,
        out_specs=tuple([hbm] * count),
        scratch_shapes=[pltpu.VMEM(a.shape, a.dtype) for a in arrays]
        + [pltpu.SemaphoreType.DMA((2, count))],
        compiler_params=pltpu.CompilerParams(vmem_limit_bytes=VMEM_LIMIT),
    )(*arrays)


def per_device(
    inputs,
    norm1_gain,
    norm1_shift,
    query_weight,
    query_bias,
    key_weight,
    value_weight,
    value_bias,
    output_weight,
    output_bias,
    norm2_gain,
    norm2_shift,
    expand_weight,
    expand_bias,
    contract_weight,
    contract_bias,
    cotangent,
):
    cols = lax.axis_size("col")
    ranks = lax.axis_size("row")
    row = lax.axis_index("row")
    share = inputs.shape[1]
    units = expand_weight.shape[1]
    weights = (
        query_weight,
        key_weight,
        value_weight,
        output_weight,
        expand_weight,
        contract_weight,
    )
    (
        outputs,
        input_grad,
        query_grad,
        key_grad,
        value_grad,
        output_grad,
        expand_grad,
        contract_grad,
        small,
    ) = layer(
        (inputs, cotangent),
        weights,
        [
            vector[None]
            for vector in (
                norm1_gain,
                norm1_shift,
                output_bias,
                norm2_gain,
                norm2_shift,
                contract_bias,
                query_bias,
                value_bias,
                expand_bias,
            )
        ],
        cols,
        ranks,
    )
    (
        outputs,
        input_grad,
        query_grad,
        key_grad,
        value_grad,
        output_grad,
        expand_grad,
        contract_grad,
    ) = settle(
        (
            outputs,
            input_grad,
            query_grad,
            key_grad,
            value_grad,
            output_grad,
            expand_grad,
            contract_grad,
        )
    )
    piece = share // ranks
    vector = lax.dynamic_slice_in_dim(small[:8], row * piece, piece, 1)
    wide = small[8:].reshape(units)
    expand_bias_grad = lax.dynamic_slice_in_dim(wide, row * (units // ranks), units // ranks, 0)
    return (
        outputs,
        input_grad,
        vector[3],
        vector[4],
        query_grad,
        vector[5],
        key_grad,
        value_grad,
        vector[6],
        output_grad,
        vector[2],
        vector[0],
        vector[1],
        expand_grad,
        expand_bias_grad,
        contract_grad,
        vector[7],
    )


def solution(mesh):
    in_specs = (
        P("row", "col"),
        P("col"),
        P("col"),
        P("row", "col"),
        P("col"),
        P("row", "col"),
        P("row", "col"),
        P("col"),
        P("col", "row"),
        P("col"),
        P("col"),
        P("col"),
        P("row", "col"),
        P("col"),
        P("col", "row"),
        P("col"),
        P("row", "col"),
    )
    out_specs = (
        P("row", "col"),
        P("row", "col"),
        P(("col", "row")),
        P(("col", "row")),
        P("row", "col"),
        P(("col", "row")),
        P("row", "col"),
        P("row", "col"),
        P(("col", "row")),
        P("col", "row"),
        P(("col", "row")),
        P(("col", "row")),
        P(("col", "row")),
        P("row", "col"),
        P(("col", "row")),
        P("col", "row"),
        P(("col", "row")),
    )
    return jax.shard_map(
        per_device, mesh=mesh, in_specs=in_specs, out_specs=out_specs, check_vma=False
    )
```

```python
import functools
import math

import jax
import jax.numpy as jnp
from jax import lax
from jax.experimental import pallas as pl
from jax.experimental.pallas import tpu as pltpu
from jax.sharding import PartitionSpec as P

HEADS = 16
HEAD = 128
LEN = 1024

epsilon = 1e-05
MESH = pl.DeviceIdType.MESH
bf16 = jnp.bfloat16
f32 = jnp.float32


def flip(index, dim):
    step = 1 << dim
    bit = (index // step) % 2
    return index + (1 - 2 * bit) * step


def flip_mask(index, mask):
    dim = 0
    while mask >> dim:
        if (mask >> dim) & 1:
            index = flip(index, dim)
        dim += 1
    return index


def chip_order(chunk, bits):
    dims = list(range(1, bits))
    start = chunk % len(dims)
    return dims[start:] + dims[:start]


def masks_over(dims):
    masks = [0]
    for dim in dims:
        masks = masks + [m | (1 << dim) for m in masks]
    return masks


def remote(src, dst, send, recv, peer, axis="col"):
    return pltpu.make_async_remote_copy(
        src_ref=src,
        dst_ref=dst,
        send_sem=send,
        recv_sem=recv,
        device_id={axis: peer},
        device_id_type=MESH,
    )


def span(index, size):
    return pl.ds(pl.multiple_of(index * size, size), size)


def dot(a, b, ca, cb):
    return lax.dot_general(a, b, (((ca,), (cb,)), ((), ())), preferred_element_type=f32)


def row_stats(values):
    average = jnp.mean(values, axis=1, keepdims=True)
    centred = values - average
    variance = jnp.mean(centred * centred, axis=1, keepdims=True)
    inverse = lax.rsqrt(variance + epsilon)
    return centred * inverse, inverse


def norm_back(upstream, xhat, inverse, gain):
    scaled = upstream * gain
    mean_scaled = jnp.mean(scaled, axis=1, keepdims=True)
    mean_product = jnp.mean(scaled * xhat, axis=1, keepdims=True)
    return inverse * (scaled - mean_scaled - xhat * mean_product)


def add_rows(target, other, step=512):
    def body(i, _):
        columns = span(i, step)
        total = target[:, columns].astype(f32) + other[:, columns].astype(f32)
        target[:, columns] = total.astype(bf16)
        return 0

    lax.fori_loop(0, target.shape[1] // step, body, 0)


class Gather:
    def __init__(self, me, bits, chunks, place, sems, base=0):
        self.me, self.bits, self.chunks, self.place = me, bits, chunks, place
        self.chip_send, self.chip_recv, self.mate_send, self.mate_recv = sems
        self.base = base
        self.held = [[me] for _ in range(chunks)]
        self.waiting = [[] for _ in range(chunks)]
        self.mates, self.sent = [], []

    def stage(self, c, s):
        order = chip_order(c, self.bits)
        if s == 0:
            new, base = [self.me], 0
        else:
            for copy in self.waiting[c]:
                copy.wait_recv()
            base = len(self.held[c])
            new = [flip(b, order[s - 1]) for b in self.held[c]]
            self.held[c] = self.held[c] + new
        if s < self.bits - 1:
            copies = []
            for i, b in enumerate(self.held[c]):
                slot = (1 << s) - 1 + i
                home = self.place(b, c)
                copy = remote(
                    home,
                    home,
                    self.chip_send.at[self.base + c, slot],
                    self.chip_recv.at[self.base + c, slot],
                    flip(self.me, order[s]),
                )
                copy.start()
                copies.append(copy)
            self.waiting[c] = copies
            self.sent.extend(copies)
        for i, b in enumerate(new):
            home = self.place(b, c)
            copy = remote(
                home,
                home,
                self.mate_send.at[self.base + c, base + i],
                self.mate_recv.at[self.base + c, base + i],
                flip(self.me, 0),
            )
            copy.start()
            self.mates.append(copy)

    def all(self, s):
        for c in range(self.chunks):
            self.stage(c, s)

    def finish(self):
        for copy in self.sent:
            copy.wait_send()
        for copy in self.mates:
            copy.wait()


class Scatter:
    def __init__(self, me, bits, chunks, partial, rows, first, later, sems):
        self.me, self.bits, self.chunks = me, bits, chunks
        self.partial, self.rows, self.first, self.later = partial, rows, first, later
        self.core_send, self.core_recv, self.chip_send, self.chip_recv = sems
        self.core, self.chip = {}, {}

    def ranked(self, c):
        lead = chip_order(c, self.bits)[0]
        every = masks_over(list(range(1, self.bits)))
        return lead, sorted(every, key=lambda m: (0 if (m >> lead) & 1 else 1, m))

    def base(self, s):
        return sum(1 << (self.bits - 2 - k) for k in range(s))

    def start(self, c):
        mate = flip(self.me, 0)
        for m in self.ranked(c)[1]:
            slot = m >> 1
            copy = remote(
                self.partial.at[self.rows(flip_mask(mate, m), c)],
                self.first.at[slot, c],
                self.core_send.at[c, slot],
                self.core_recv.at[c, slot],
                mate,
            )
            copy.start()
            self.core[c, m] = copy

    def send(self, c, s, m):
        order = chip_order(c, self.bits)
        kept = m & ~(1 << order[s])
        i = self.base(s) + masks_over(order[s + 1 :]).index(kept)
        copy = remote(
            self.first.at[m >> 1, c],
            self.later.at[i, c],
            self.chip_send.at[c, i],
            self.chip_recv.at[c, i],
            flip(self.me, order[s]),
        )
        copy.start()
        self.chip[c, s, kept] = copy

    def add(self, c, s):
        order = chip_order(c, self.bits)
        if s == 0:
            lead, ranked = self.ranked(c)
            for m in ranked:
                self.core[c, m].wait_recv()
                slot = m >> 1
                mine = self.partial.at[self.rows(flip_mask(self.me, m), c)]
                add_rows(self.first.at[slot, c], mine)
                if (m >> lead) & 1:
                    self.send(c, s, m)
        else:
            for i, m in enumerate(masks_over(order[s:])):
                self.chip[c, s - 1, m].wait_recv()
                slot = m >> 1
                add_rows(self.first.at[slot, c], self.later.at[self.base(s - 1) + i, c])
            for m in masks_over(order[s + 1 :]):
                self.send(c, s, m | (1 << order[s]))

    def total(self, c):
        s = self.bits - 2
        self.chip[c, s, 0].wait_recv()
        return self.first[0, c].astype(f32) + self.later[self.base(s), c].astype(f32)

    def begin(self):
        for c in range(self.chunks):
            self.start(c)

    def all(self, s):
        for c in range(self.chunks):
            self.add(c, s)

    def finish(self):
        for copy in list(self.core.values()) + list(self.chip.values()):
            copy.wait_send()


QKV, OUT = 0, 1
UP = (2, 4)
DOWN = (3, 5)
IN = (0, 6)
DOWN_PARTS = (3, 5, 7)


def chunks_of(block):
    return max(1, min(8, block // 16))

VMEM_LIMIT = 65024 << 10


def layer_kernel(n, ranks, *refs):
    (
        x_hbm, cot_hbm, q_hbm, k_hbm, v_hbm, o_hbm, up_hbm, down_hbm,
        gain1, shift1, bias_o, gain2, shift2, bias_c, bias_q, bias_v, up_bias,
        out_hbm, xg_hbm, qg_hbm, kg_hbm, vg_hbm, og_hbm, upg_hbm, downg_hbm, small_ref,
        w_in, w_out, w_up, w_down, normed1, down_rows, buf_a, buf_b, first, later,
        qkv, attended, slope_grad, hidden, slots_down, slots_up,
        stage_a, stage_b, middle, middle_grad, x_own, logsum, kv_sum, vectors, sums,
        local_sums, up_sums, in_bias, landed, row_landed,
        local_sem, gather_a, gather_b, gather_c, gather_d,
        scatter_a, scatter_b, scatter_c, scatter_d,
        z_send, z_recv, g_send, g_recv, vec_send, vec_recv, ex_send, ex_recv,
        row_send, row_recv, free_sem,
    ) = refs
    bits = n.bit_length() - 1
    me = lax.axis_index("col")
    row = lax.axis_index("row")
    tokens, width = normed1.shape
    share = width // n
    depth = width // ranks
    units = hidden.shape[1]
    block = tokens // n
    chunks = chunks_of(block)
    sub = block // chunks
    heads_here = share // HEAD
    in_width = 3 * share
    part = units // 2
    halves = (slice(0, part), slice(part, units))
    quarter = part // 2
    down_parts = (slice(0, part), slice(part, part + quarter), slice(part + quarter, units))
    in_split = in_width // (2 * HEAD) * HEAD
    in_parts = (slice(0, in_split), slice(in_split, in_width))
    in_grad = hidden.at[:, 0:in_width]
    score_scale = 1.0 / math.sqrt(HEAD)
    right, left = row + 1, row - 1
    has_left, has_right = row > 0, row < ranks - 1
    is_end = jnp.logical_or(row == 0, row == ranks - 1)
    is_inner = jnp.logical_not(is_end)

    def local(src, dst, i):
        copy = pltpu.make_async_copy(src, dst, local_sem.at[i])
        copy.start()
        return copy

    def rows(b, c):
        return pl.ds(pl.multiple_of(b * block + c * sub, sub), sub)

    mine = span(me, share)

    def z_block(k, b):
        if k in IN:
            return w_in.at[span(b, depth), in_parts[IN.index(k)]]
        if k == OUT:
            return w_out.at[:, span(b, depth)]
        if k in UP:
            return w_up.at[span(b, depth), halves[UP.index(k)]]
        return w_down.at[down_parts[DOWN_PARTS.index(k)], span(b, depth)]

    def z_copy(k, way, hop):
        b = row - hop if way == 0 else row + hop
        peer = right if way == 0 else left
        return remote(
            z_block(k, b), z_block(k, b), z_send.at[k, way, hop], z_recv.at[k, way, hop],
            peer, "row",
        )

    def z_landing(k, way, hop):
        b = row - hop if way == 0 else row + hop
        return remote(
            z_block(k, b), z_block(k, b), z_send.at[k, way, hop - 1],
            z_recv.at[k, way, hop - 1], left if way == 0 else right, "row",
        )

    in_low = row < ranks // 2
    in_high = jnp.logical_not(in_low)

    def z_own(k, to_right=has_right, to_left=has_left):
        @pl.when(jnp.logical_and(has_right, to_right))
        def _():
            z_copy(k, 0, 0).start()

        @pl.when(jnp.logical_and(has_left, to_left))
        def _():
            z_copy(k, 1, 0).start()

    def z_own_end(k):
        z_own(k, is_end, is_end)

    def z_own_inward(k):
        z_own(k, jnp.logical_and(is_inner, in_low), jnp.logical_and(is_inner, in_high))

    def z_own_outward(k):
        z_own(k, jnp.logical_and(is_inner, in_high), jnp.logical_and(is_inner, in_low))

    def z_pass(k, hop):
        @pl.when(row >= hop)
        def _():
            z_landing(k, 0, hop).wait_recv()
            if hop < ranks - 1:

                @pl.when(has_right)
                def _():
                    z_copy(k, 0, hop).start()

        @pl.when(row + hop <= ranks - 1)
        def _():
            z_landing(k, 1, hop).wait_recv()
            if hop < ranks - 1:

                @pl.when(has_left)
                def _():
                    z_copy(k, 1, hop).start()

    def z_sent(k):
        for hop in range(ranks - 1):

            @pl.when(jnp.logical_and(row >= hop, has_right))
            def _():
                z_copy(k, 0, hop).wait_send()

            @pl.when(jnp.logical_and(row + hop <= ranks - 1, has_left))
            def _():
                z_copy(k, 1, hop).wait_send()

    def slot(g, s):
        if g in DOWN:
            return slots_down.at[s, halves[DOWN.index(g)]]
        if g in UP:
            return slots_up.at[s, :, halves[UP.index(g)]]
        if g == OUT:
            return w_down.at[
                pl.ds(pl.multiple_of(depth + (s // ranks) * share, share), share),
                span(lax.rem(s, ranks), depth),
            ]
        return w_up.at[span(s, depth), 0:in_width]

    def last_slot(g):
        if g == QKV:
            return w_down.at[0:depth, 0:in_width]
        return slot(g, ranks)

    def term(g, c, write):
        if g in DOWN:
            half = DOWN.index(g)
            tile = min(256, part)

            def step(i, _):
                columns = span(half * (part // tile) + i, tile)
                value = dot(hidden[:, columns], down_rows[:, span(c, depth)], 0, 0)
                write(span(i, tile), slice(0, depth), value)
                return 0

            lax.fori_loop(0, part // tile, step, 0)
        elif g in UP:
            value = dot(buf_a[:, span(c, depth)], slope_grad[:, halves[UP.index(g)]], 0, 0)
            write(slice(0, depth), slice(0, part), value)
        elif g == OUT:
            value = dot(attended[...], down_rows[:, span(c, depth)], 0, 0)
            write(slice(0, share), slice(0, depth), value)
        else:

            def step(j, _):
                value = dot(normed1[:, span(c, depth)], hidden[:, span(j, share)], 0, 0)
                write(slice(0, depth), span(j, share), value)
                return 0

            lax.fori_loop(0, 3, step, 0)

    def chunk_at(k, mixed=False):
        ups, downs = ranks - 1 - row, row
        if mixed and ranks == 4:
            from_low = jnp.where(
                k == 0, ranks - 1, jnp.where(k <= downs, k - 1, ranks - 1 - (k - downs))
            )
            from_high = jnp.where(k == 0, 0, jnp.where(k <= ups, ranks - k, k - ups))
        else:
            from_low = jnp.where(k < ups, ranks - 1 - k, k - ups)
            from_high = jnp.where(k < downs, k, ranks - 1 - (k - downs))
        return jnp.where(row < ranks // 2, from_low, from_high)

    def g_copy(g, c, way, to_owner=False):
        src = slot(g, c)
        dst = last_slot(g) if to_owner else slot(g, c)
        sem = g_recv.at[g, ranks] if to_owner else g_recv.at[g, c]
        return remote(src, dst, g_send.at[g, c], sem, right if way == 0 else left, "row")

    def g_start(g, c):
        @pl.when(c > row)
        def _():
            g_copy(g, c, 0).start()

        @pl.when(jnp.logical_and(c < row, c == left))
        def _():
            g_copy(g, c, 1, True).start()

        @pl.when(jnp.logical_and(c < row, c != left))
        def _():
            g_copy(g, c, 1).start()

    def g_first(g, begin=0, end=ranks - 1):
        if begin >= end:
            return

        @pl.when(is_end)
        def _():
            def step(k, _):
                c = chunk_at(k)
                here = slot(g, c)

                def write(r, q, value):
                    here[r, q] = value.astype(bf16)

                term(g, c, write)
                g_start(g, c)
                return 0

            lax.fori_loop(begin, end, step, 0)

    def g_pass(g, begin=0, end=ranks - 1):
        if begin >= end:
            return

        @pl.when(jnp.logical_not(is_end))
        def _():
            def step(k, _):
                c = chunk_at(k, g == QKV)
                here = slot(g, c)
                g_copy(g, c, 0).wait_recv()

                def write(r, q, value):
                    here[r, q] = (here[r, q].astype(f32) + value).astype(bf16)

                term(g, c, write)
                g_start(g, c)
                return 0

            lax.fori_loop(begin, end, step, 0)

    def g_own_term(g, stage):
        def write(r, q, value):
            stage[r, q] = value

        term(g, row, write)

    def g_own_add(g, stage, step=64):
        def add(here):
            def body(i, _):
                r = span(i, step)
                stage[r] += here[r].astype(f32)
                return 0

            lax.fori_loop(0, here.shape[0] // step, body, 0)

        @pl.when(has_left)
        def _():
            g_copy(g, row, 0).wait_recv()
            add(slot(g, row))

        @pl.when(has_right)
        def _():
            g_copy(g, row, 1, True).wait_recv()
            add(last_slot(g))

    def g_sent(g):
        for k in range(ranks - 1):
            g_copy(g, chunk_at(k), 0).wait_send()

    x_load = local(x_hbm, normed1.at[:, mine], 0)
    in_loads = [
        local(hbm, stage_a.at[0:depth, i * share : (i + 1) * share], 1 + i)
        for i, hbm in enumerate((q_hbm, k_hbm, v_hbm))
    ]
    o_load = local(o_hbm, stage_b.at[0:share, :], 4)
    cot_load = local(cot_hbm, down_rows.at[:, mine], 5)

    barrier = pltpu.get_barrier_semaphore()
    for i in range(1, n):
        pl.semaphore_signal(
            barrier, inc=1, device_id={"col": lax.rem(me + i, n)}, device_id_type=MESH
        )
    for i in range(1, ranks):
        pl.semaphore_signal(
            barrier, inc=1, device_id={"row": lax.rem(row + i, ranks)}, device_id_type=MESH
        )
    pl.semaphore_wait(barrier, n - 1 + ranks - 1)

    gather_sems = (gather_a, gather_b, gather_c, gather_d)
    scatter_sems = (scatter_a, scatter_b, scatter_c, scatter_d)
    half = tokens // 2

    def feature_place(ref):
        def place(b, c):
            return ref.at[pl.ds(c * half, half), span(b, share)]

        return place

    gather_x = Gather(me, bits, 2, feature_place(normed1), gather_sems)
    gather_g = Gather(me, bits, 2, feature_place(down_rows), gather_sems, 2)
    x_load.wait()
    gather_x.all(0)
    for i, ref in enumerate((gain1, shift1, bias_o, gain2, shift2, bias_c)):
        vectors[i : i + 1, mine] = ref[...]
    in_bias[...] = jnp.zeros(in_bias.shape, f32)
    in_bias[:, 0:share] = bias_q[...]
    in_bias[:, 2 * share : in_width] = bias_v[...]
    vec_copies = []
    for i in range(1, n):
        copy = remote(
            vectors.at[:, mine], vectors.at[:, mine], vec_send.at[i], vec_recv.at[i],
            lax.rem(me + i, n),
        )
        copy.start()
        vec_copies.append(copy)
    for copy in in_loads:
        copy.wait()
    w_in[span(row, depth)] = stage_a[:, 0:in_width].astype(bf16)
    z_own(IN[0])
    up_load = local(up_hbm, stage_a, 1)
    o_load.wait()
    w_out[:, span(row, depth)] = stage_b[0:share, :].astype(bf16)
    z_own_outward(OUT)
    down_load = local(down_hbm, stage_b, 2)
    cot_load.wait()
    local_sums[7:8] = jnp.sum(down_rows[:, mine].astype(f32), axis=0, keepdims=True)
    gather_x.all(1)
    up_load.wait()
    w_up[span(row, depth)] = stage_a[...].astype(bf16)
    down_load.wait()
    w_down[:, span(row, depth)] = stage_b[...].astype(bf16)
    for s in range(2, bits - 1):
        gather_x.all(s)
    z_own(IN[1])
    z_pass(IN[0], 1)
    gather_x.all(bits - 1)
    gather_g.all(0)
    z_own_end(OUT)
    z_own_end(UP[0])
    z_own_end(DOWN[0])
    gather_x.finish()
    for copy in vec_copies:
        copy.wait_recv()
    x_own[...] = normed1[span(me, block)]

    def norm_step(i, _):
        here = span(i, 64)
        xhat, _ = row_stats(normed1[here].astype(f32))
        normed1[here] = (xhat * vectors[0:1] + vectors[1:2]).astype(bf16)
        return 0

    lax.fori_loop(0, tokens // 64, norm_step, 0)
    z_pass(IN[1], 1)
    if ranks > 3:
        z_pass(IN[0], 2)
    z_own_inward(OUT)
    for s in range(1, bits - 1):
        gather_g.all(s)
    for hop in range(2, ranks - 1):
        z_pass(IN[1], hop)
        if hop + 1 < ranks - 1:
            z_pass(IN[0], hop + 1)
    gather_g.all(bits - 1)
    z_own_end(UP[1])
    z_own_end(DOWN_PARTS[1])
    z_own_end(DOWN_PARTS[2])
    z_pass(IN[0], ranks - 1)
    z_pass(IN[1], ranks - 1)

    def qkv_step(j, _):
        columns = span(j, share)
        qkv[:, columns] = (dot(normed1[...], w_in[:, columns], 1, 0) + in_bias[:, columns]).astype(bf16)
        return 0

    lax.fori_loop(0, 3, qkv_step, 0)
    z_pass(OUT, 1)
    z_own_inward(UP[0])
    tile = 256

    def slope_of(h):
        number = jnp.full((1, 1), me * heads_here + h + 1, jnp.int32).astype(f32)
        return jnp.exp2(-8.0 / HEADS * number)

    def columns_of(which, h):
        return pl.ds(pl.multiple_of(which * share + h * HEAD, HEAD), HEAD)

    def blocks():
        for start in range(0, tokens, LEN):
            for i in range(LEN // tile):
                seen = (i + 1) * tile
                yield slice(start + i * tile, start + seen), slice(start, start + seen), i * tile

    def scores(h, q_rows, k_rows, offset):
        raw = dot(qkv[q_rows, columns_of(0, h)], qkv[k_rows, columns_of(1, h)], 1, 1) * score_scale
        shape = raw.shape
        distance = lax.broadcasted_iota(jnp.int32, shape, 1) - (
            lax.broadcasted_iota(jnp.int32, shape, 0) + offset
        )
        raw = raw + slope_of(h) * distance.astype(f32)
        return jnp.where(distance <= 0, raw, -jnp.inf)

    lane = lax.broadcasted_iota(jnp.int32, (tile, HEAD), 1)

    def attend(h, _):
        for q_rows, k_rows, offset in blocks():
            s = scores(h, q_rows, k_rows, offset)
            top = jnp.max(s, axis=1, keepdims=True)
            exponent = jnp.exp(s - top)
            total = jnp.sum(exponent, axis=1, keepdims=True)
            weights = (exponent / total).astype(bf16)
            attended[q_rows, columns_of(0, h)] = dot(
                weights, qkv[k_rows, columns_of(2, h)], 1, 0
            ).astype(bf16)
            logsum[q_rows] = jnp.where(lane == h, top + jnp.log(total), logsum[q_rows])
        return 0

    logsum[...] = jnp.zeros(logsum.shape, f32)
    lax.fori_loop(0, heads_here, attend, 0)
    for hop in range(2, ranks - 1):
        z_pass(OUT, hop)
    z_own_outward(UP[0])
    z_own_inward(DOWN[0])
    gather_g.finish()
    z_pass(OUT, ranks - 1)

    column_tile = 256

    def branch_step(j, _):
        columns = span(j, column_tile)
        buf_b[:, columns] = dot(attended[...], w_out[:, columns], 1, 0).astype(bf16)
        return 0

    lax.fori_loop(0, width // column_tile, branch_step, 0)

    def scatter_of(partial):
        return Scatter(me, bits, chunks, partial, rows, first, later, scatter_sems)

    def gather_of(ref):
        return Gather(me, bits, chunks, lambda b, c: ref.at[rows(b, c)], gather_sems)

    scatter = scatter_of(buf_b)
    gather = gather_of(buf_a)
    scatter.begin()
    scatter.all(0)
    for s in range(1, bits - 1):
        scatter.all(s)
    z_pass(UP[0], 1)
    z_own_inward(UP[1])
    for c in range(chunks):
        here = pl.ds(c * sub, sub)
        values = x_own[here].astype(f32) + (scatter.total(c) + vectors[2:3])
        middle[here] = values
        xhat, _ = row_stats(values)
        buf_a[rows(me, c)] = (xhat * vectors[3:4] + vectors[4:5]).astype(bf16)
        gather.stage(c, 0)
    for hop in range(2, ranks - 1):
        z_pass(UP[0], hop)
    for s in range(1, bits - 1):
        gather.all(s)
    z_own_outward(DOWN[0])
    scatter.finish()
    gather.all(bits - 1)
    z_own_inward(DOWN_PARTS[1])
    z_own_inward(DOWN_PARTS[2])
    gather.finish()
    z_pass(UP[0], ranks - 1)

    row_tile = 512
    row_tiles = tokens // row_tile
    hidden_tiles = row_tiles * (part // column_tile)

    def expand(half):
        def step(t, _):
            here = span(lax.rem(t, row_tiles), row_tile)
            columns = span(half * (part // column_tile) + t // row_tiles, column_tile)
            u = dot(buf_a[here], w_up[:, columns], 1, 0) + up_bias[:, columns]
            square = u * u
            inner = jnp.tanh(0.7978845608 * (u + 0.044715 * (u * square)))
            outer = 0.5 * (1.0 + inner)
            hidden[here, columns] = (u * outer).astype(bf16)
            slope = outer + 0.5 * u * (1.0 - inner * inner) * (
                0.7978845608 * (1.0 + 3.0 * 0.044715 * square)
            )
            slope_grad[here, columns] = slope.astype(bf16)
            return 0

        lax.fori_loop(0, hidden_tiles, step, 0)

    def expand_back(piece):
        rows_here = down_parts[piece]
        step_size = min(column_tile, rows_here.stop - rows_here.start)
        begin = rows_here.start // step_size
        steps = (rows_here.stop - rows_here.start) // step_size

        def step(t, _):
            here = span(lax.rem(t, row_tiles), row_tile)
            columns = span(begin + t // row_tiles, step_size)
            grad = dot(down_rows[here], w_down[columns], 1, 1)
            low = (grad * slope_grad[here, columns].astype(f32)).astype(bf16)
            slope_grad[here, columns] = low
            up_sums[:, columns] += jnp.sum(low.astype(f32), axis=0, keepdims=True)
            return 0

        lax.fori_loop(0, row_tiles * steps, step, 0)

    def second(piece):
        inner = down_parts[piece]

        def step(t, _):
            here = span(lax.rem(t, row_tiles), row_tile)
            columns = span(t // row_tiles, column_tile)
            grad = dot(slope_grad[here, inner], w_up[columns, inner], 1, 1)
            if piece > 0:
                grad = grad + buf_b[here, columns].astype(f32)
            buf_b[here, columns] = grad.astype(bf16)
            return 0

        lax.fori_loop(0, row_tiles * (width // column_tile), step, 0)

    up_sums[...] = jnp.zeros(up_sums.shape, f32)
    expand(0)
    g_first(DOWN[0])
    for hop in range(1, ranks - 1):
        z_pass(DOWN[0], hop)
    z_own_outward(UP[1])
    z_pass(DOWN[0], ranks - 1)
    expand_back(0)
    g_first(UP[0])
    z_pass(UP[1], 1)
    for hop in range(2, ranks - 1):
        z_pass(UP[1], hop)
    z_own_outward(DOWN_PARTS[1])
    z_pass(UP[1], ranks - 1)
    expand(1)
    g_first(DOWN[1])
    z_pass(DOWN_PARTS[1], 1)
    for half in range(2):
        g_own_term(DOWN[half], stage_b.at[halves[half]])
    second(0)
    for hop in range(2, ranks):
        z_pass(DOWN_PARTS[1], hop)
    expand_back(1)
    z_own_outward(DOWN_PARTS[2])
    z_pass(DOWN_PARTS[2], 1)
    second(1)
    for hop in range(2, ranks):
        z_pass(DOWN_PARTS[2], hop)
    expand_back(2)
    g_first(UP[1], 0, 1)
    second(2)
    g_pass(DOWN[0])
    g_pass(UP[0])
    g_pass(DOWN[1])
    scatter = scatter_of(buf_b)
    gather = gather_of(down_rows)
    scatter.begin()
    scatter.all(0)
    g_first(UP[1], 1)
    for s in range(1, bits - 1):
        scatter.all(s)
    g_pass(UP[1], 0, 1)
    sums[...] = jnp.zeros(sums.shape, f32)
    for c in range(chunks):
        here = pl.ds(c * sub, sub)
        xhat, inverse = row_stats(middle[here])
        upstream = scatter.total(c)
        grad = down_rows[rows(me, c)].astype(f32) + norm_back(upstream, xhat, inverse, vectors[3:4])
        middle_grad[here] = grad
        low = grad.astype(bf16)
        down_rows[rows(me, c)] = low
        gather.stage(c, 0)
        sums[0:1] += jnp.sum(upstream * xhat, axis=0, keepdims=True)
        sums[1:2] += jnp.sum(upstream, axis=0, keepdims=True)
        sums[2:3] += jnp.sum(low.astype(f32), axis=0, keepdims=True)
    for s in range(1, bits - 1):
        gather.all(s)
    scatter.finish()

    def contract_step(t, _):
        here = span(lax.rem(t, tokens // row_tile), row_tile)
        columns = span(t // (tokens // row_tile), column_tile)
        buf_b[here, columns] = dot(hidden[here], w_down[:, columns], 1, 0).astype(bf16)
        return 0

    lax.fori_loop(0, (tokens // row_tile) * (width // column_tile), contract_step, 0)
    for k in range(8):
        z_sent(k)

    @pl.when(has_right)
    def _():
        pl.semaphore_signal(free_sem, inc=1, device_id={"row": right}, device_id_type=MESH)

    @pl.when(has_left)
    def _():
        pl.semaphore_signal(free_sem, inc=1, device_id={"row": left}, device_id_type=MESH)

    gather.all(bits - 1)
    g_pass(UP[1], 1)
    for half in range(2):
        g_own_add(DOWN[half], stage_b.at[halves[half]])
    down_store = local(stage_b, downg_hbm, 0)
    gather.finish()

    scatter = scatter_of(buf_b)
    scatter.begin()
    pl.semaphore_wait(free_sem, has_left.astype(jnp.int32) + has_right.astype(jnp.int32))
    g_first(OUT, 0, 2)

    def attended_step(i, _):
        here = span(i, row_tile)
        value = dot(down_rows[here], w_out[...], 1, 1).astype(bf16)
        hidden[here, in_width : in_width + share] = value
        return 0

    lax.fori_loop(0, tokens // row_tile, attended_step, 0)
    down_store.wait()
    if kv_sum.shape[1] == LEN:
        key_sum, value_sum = kv_sum.at[0], kv_sum.at[1]
    else:
        key_sum, value_sum = stage_b.at[:, 0:HEAD], stage_b.at[:, HEAD : 2 * HEAD]

    def attend_back(h, _):
        for start in range(0, tokens, LEN):
            sequence = slice(start, start + LEN)
            key_sum[0:LEN] = jnp.zeros((LEN, HEAD), f32)
            value_sum[0:LEN] = jnp.zeros((LEN, HEAD), f32)
            for i in range(LEN // tile):
                seen = (i + 1) * tile
                q_rows = slice(start + i * tile, start + seen)
                k_rows = slice(start, start + seen)
                s = scores(h, q_rows, k_rows, i * tile)
                kept = jnp.sum(
                    jnp.where(lane == h, logsum[q_rows], 0.0), axis=1, keepdims=True
                )
                probability = jnp.exp(s - kept)
                result_grad = hidden[q_rows, columns_of(3, h)]
                weight_grad = dot(result_grad, qkv[k_rows, columns_of(2, h)], 1, 1)
                inner = jnp.sum(probability * weight_grad, axis=1, keepdims=True)
                score_grad = (probability * (weight_grad - inner)).astype(bf16)
                value_sum[0:seen] += dot(probability.astype(bf16), result_grad, 0, 0)
                key_sum[0:seen] += dot(score_grad, qkv[q_rows, columns_of(0, h)], 0, 0)
                hidden[q_rows, columns_of(0, h)] = (
                    dot(score_grad, qkv[k_rows, columns_of(1, h)], 1, 0) * score_scale
                ).astype(bf16)
            hidden[sequence, columns_of(1, h)] = (key_sum[0:LEN] * score_scale).astype(bf16)
            hidden[sequence, columns_of(2, h)] = value_sum[0:LEN].astype(bf16)
        return 0

    scatter.all(0)
    lax.fori_loop(0, heads_here, attend_back, 0)

    g_first(QKV, 0, 1)
    g_first(OUT, 2)
    g_pass(OUT, 0, 2)
    for s in range(1, bits - 1):
        scatter.all(s)

    for half in range(2):
        g_own_term(UP[half], stage_a.at[:, halves[half]])
        g_own_add(UP[half], stage_a.at[:, halves[half]])
    up_store = local(stage_a, upg_hbm, 1)
    g_first(QKV, 1, 2)

    def exchange(staged, out, c, base):
        copies = []
        for i in range(1, n):
            peer = lax.rem(me + i, n)
            copy = remote(
                staged.at[:, span(peer, share)], out.at[rows(me, c)],
                ex_send.at[base + c, i], ex_recv.at[base + c, i], peer,
            )
            copy.start()
            copies.append(copy)
        copy = pltpu.make_async_copy(
            staged.at[:, mine], out.at[rows(me, c)], ex_send.at[base + c, 0]
        )
        copy.start()
        return copies + [copy]

    result_copies = []
    for c in range(chunks):
        here = pl.ds(c * sub, sub)
        result = middle[here] + (scatter.total(c) + vectors[5:6])
        buf_b[rows(me, c)] = result.astype(bf16)
    scatter.finish()
    for c in range(chunks):
        result_copies += exchange(buf_b.at[rows(me, c)], out_hbm, c, 0)

    def first_step(t, _):
        here = span(lax.rem(t, tokens // row_tile), row_tile)
        columns = span(t // (tokens // row_tile), column_tile)
        buf_a[here, columns] = dot(hidden[here, 0:in_width], w_in[columns], 1, 1).astype(bf16)
        return 0

    lax.fori_loop(0, (tokens // row_tile) * (width // column_tile), first_step, 0)
    g_pass(OUT, 2)
    g_pass(QKV, 0, 1)
    for copy in result_copies:
        copy.wait()
    scatter = scatter_of(buf_a)
    scatter.begin()
    g_first(QKV, 2)
    local_sums[5:6] = jnp.sum(hidden[:, 0:share].astype(f32), axis=0, keepdims=True)
    local_sums[6:7] = jnp.sum(
        hidden[:, 2 * share : in_width].astype(f32), axis=0, keepdims=True
    )
    for k in range(units // share):
        local_sums[8 + k : 9 + k] = up_sums[:, k * share : (k + 1) * share]
    scatter.all(0)

    g_own_term(OUT, stage_b.at[0:share])
    g_own_add(OUT, stage_b.at[0:share])
    out_store = local(stage_b.at[0:share], og_hbm, 0)
    for s in range(1, bits - 1):
        scatter.all(s)
    g_pass(QKV, 1)
    input_copies = []
    for c in range(chunks):
        here = pl.ds(c * sub, sub)
        xhat, inverse = row_stats(x_own[here].astype(f32))
        upstream = scatter.total(c)
        middle_grad[here] += norm_back(upstream, xhat, inverse, vectors[0:1])
        sums[3:4] += jnp.sum(upstream * xhat, axis=0, keepdims=True)
        sums[4:5] += jnp.sum(upstream, axis=0, keepdims=True)
    vec_back = []
    for i in range(1, n):
        peer = lax.rem(me + i, n)
        copy = remote(
            sums.at[:, span(peer, share)], landed.at[i],
            ex_send.at[chunks, i], ex_recv.at[chunks, i], peer,
        )
        copy.start()
        vec_back.append(copy)
    for c in range(chunks):
        input_copies += exchange(middle_grad.at[pl.ds(c * sub, sub)], xg_hbm, c, 0)
    summed = sums[:, mine]
    for copy in vec_back:
        copy.wait_recv()
    for i in range(1, n):
        summed = summed + landed[i]
    local_sums[0:5] = summed[0:5]
    row_copies = []
    for i in range(1, ranks):
        copy = remote(
            local_sums, row_landed.at[i], row_send.at[i], row_recv.at[i],
            lax.rem(row + i, ranks), "row",
        )
        copy.start()
        row_copies.append(copy)
    up_store.wait()
    g_own_term(QKV, stage_a.at[:, 0:in_width])
    g_own_add(QKV, stage_a.at[:, 0:in_width])
    in_stores = [
        local(stage_a.at[:, i * share : (i + 1) * share], hbm, 1 + i)
        for i, hbm in enumerate((qg_hbm, kg_hbm, vg_hbm))
    ]
    total = local_sums[...]
    for i, copy in enumerate(row_copies):
        copy.wait_recv()
        total = total + row_landed[i + 1]
    small_ref[...] = total
    for copy in vec_copies + vec_back + row_copies:
        copy.wait_send()
    for g in range(6):
        g_sent(g)
    scatter.finish()
    for copy in input_copies + in_stores + [out_store]:
        copy.wait()


def layer(arrays, hbm_weights, vectors, n, ranks):
    inputs, cotangent = arrays
    tokens, share = inputs.shape
    width = n * share
    depth = hbm_weights[0].shape[0]
    units = vectors[-1].shape[1]
    block = tokens // n
    chunks = chunks_of(block)
    sub = block // chunks
    half = n // 2
    low = lambda *shape: pltpu.VMEM(shape, bf16)
    wide = lambda *shape: pltpu.VMEM(shape, f32)
    dma = lambda *shape: pltpu.SemaphoreType.DMA(shape)
    vmem = pl.BlockSpec(memory_space=pltpu.VMEM)
    hbm = pl.BlockSpec(memory_space=pl.ANY)
    scratch = [
        low(width, 3 * share),
        low(share, width),
        low(width, units),
        low(units, width),
        low(tokens, width),
        low(tokens, width),
        low(tokens, width),
        low(tokens, width),
        low(half, chunks, sub, width),
        low(half - 1, chunks, sub, width),
        low(tokens, 3 * share),
        low(tokens, share),
        low(tokens, units),
        low(tokens, units),
        low(ranks + 1, units, depth),
        low(ranks + 1, depth, units),
        wide(depth, units),
        wide(units, depth),
        wide(block, width),
        wide(block, width),
        low(block, width),
        wide(tokens, HEAD),
        wide(2, 8 if units >= LEN and depth >= 2 * HEAD else LEN, HEAD),
        wide(8, width),
        wide(8, width),
        wide(8 + units // share, share),
        wide(1, units),
        wide(1, 3 * share),
        wide(n, 8, share),
        wide(ranks, 8 + units // share, share),
        dma(8),
        dma(max(chunks, 4), half),
        dma(max(chunks, 4), half),
        dma(max(chunks, 4), half),
        dma(max(chunks, 4), half),
        dma(chunks, half),
        dma(chunks, half),
        dma(chunks, half),
        dma(chunks, half),
        dma(8, 2, ranks - 1),
        dma(8, 2, ranks - 1),
        dma(6, ranks + 1),
        dma(6, ranks + 1),
        dma(n),
        dma(n),
        dma(chunks + 1, n),
        dma(chunks + 1, n),
        dma(ranks),
        dma(ranks),
        pltpu.SemaphoreType.REGULAR,
    ]
    outs = (
        jax.ShapeDtypeStruct((tokens, share), bf16),
        jax.ShapeDtypeStruct((tokens, share), f32),
        jax.ShapeDtypeStruct((depth, share), f32),
        jax.ShapeDtypeStruct((depth, share), f32),
        jax.ShapeDtypeStruct((depth, share), f32),
        jax.ShapeDtypeStruct((share, depth), f32),
        jax.ShapeDtypeStruct((depth, units), f32),
        jax.ShapeDtypeStruct((units, depth), f32),
        jax.ShapeDtypeStruct((8 + units // share, share), f32),
    )
    return pl.pallas_call(
        functools.partial(layer_kernel, n, ranks),
        out_shape=outs,
        in_specs=[hbm] * 8 + [vmem] * 9,
        out_specs=tuple([hbm] * 8 + [vmem]),
        scratch_shapes=scratch,
        compiler_params=pltpu.CompilerParams(
            collective_id=1, has_side_effects=True, vmem_limit_bytes=VMEM_LIMIT
        ),
    )(inputs, cotangent, *hbm_weights, *vectors)


def settle_kernel(count, *refs):
    sources, targets, held = refs[:count], refs[count : 2 * count], refs[2 * count : 3 * count]
    sems = refs[3 * count]
    inward = [pltpu.make_async_copy(sources[i], held[i], sems.at[0, i]) for i in range(count)]
    outward = [pltpu.make_async_copy(held[i], targets[i], sems.at[1, i]) for i in range(count)]
    for copy in inward:
        copy.start()
    for arrived, copy in zip(inward, outward):
        arrived.wait()
        copy.start()
    for copy in outward:
        copy.wait()


def settle(arrays):
    count = len(arrays)
    hbm = pl.BlockSpec(memory_space=pl.ANY)
    return pl.pallas_call(
        functools.partial(settle_kernel, count),
        out_shape=tuple(jax.ShapeDtypeStruct(a.shape, a.dtype) for a in arrays),
        in_specs=[hbm] * count,
        out_specs=tuple([hbm] * count),
        scratch_shapes=[pltpu.VMEM(a.shape, a.dtype) for a in arrays]
        + [pltpu.SemaphoreType.DMA((2, count))],
        compiler_params=pltpu.CompilerParams(vmem_limit_bytes=VMEM_LIMIT),
    )(*arrays)


def per_device(
    inputs,
    norm1_gain,
    norm1_shift,
    query_weight,
    query_bias,
    key_weight,
    value_weight,
    value_bias,
    output_weight,
    output_bias,
    norm2_gain,
    norm2_shift,
    expand_weight,
    expand_bias,
    contract_weight,
    contract_bias,
    cotangent,
):
    cols = lax.axis_size("col")
    ranks = lax.axis_size("row")
    row = lax.axis_index("row")
    share = inputs.shape[1]
    units = expand_weight.shape[1]
    weights = (
        query_weight,
        key_weight,
        value_weight,
        output_weight,
        expand_weight,
        contract_weight,
    )
    (
        outputs,
        input_grad,
        query_grad,
        key_grad,
        value_grad,
        output_grad,
        expand_grad,
        contract_grad,
        small,
    ) = layer(
        (inputs, cotangent),
        weights,
        [
            vector[None]
            for vector in (
                norm1_gain,
                norm1_shift,
                output_bias,
                norm2_gain,
                norm2_shift,
                contract_bias,
                query_bias,
                value_bias,
                expand_bias,
            )
        ],
        cols,
        ranks,
    )
    (
        outputs,
        input_grad,
        query_grad,
        key_grad,
        value_grad,
        output_grad,
        expand_grad,
        contract_grad,
    ) = settle(
        (
            outputs,
            input_grad,
            query_grad,
            key_grad,
            value_grad,
            output_grad,
            expand_grad,
            contract_grad,
        )
    )
    piece = share // ranks
    vector = lax.dynamic_slice_in_dim(small[:8], row * piece, piece, 1)
    wide = small[8:].reshape(units)
    expand_bias_grad = lax.dynamic_slice_in_dim(wide, row * (units // ranks), units // ranks, 0)
    return (
        outputs,
        input_grad,
        vector[3],
        vector[4],
        query_grad,
        vector[5],
        key_grad,
        value_grad,
        vector[6],
        output_grad,
        vector[2],
        vector[0],
        vector[1],
        expand_grad,
        expand_bias_grad,
        contract_grad,
        vector[7],
    )


def solution(mesh):
    in_specs = (
        P("row", "col"),
        P("col"),
        P("col"),
        P("row", "col"),
        P("col"),
        P("row", "col"),
        P("row", "col"),
        P("col"),
        P("col", "row"),
        P("col"),
        P("col"),
        P("col"),
        P("row", "col"),
        P("col"),
        P("col", "row"),
        P("col"),
        P("row", "col"),
    )
    out_specs = (
        P("row", "col"),
        P("row", "col"),
        P(("col", "row")),
        P(("col", "row")),
        P("row", "col"),
        P(("col", "row")),
        P("row", "col"),
        P("row", "col"),
        P(("col", "row")),
        P("col", "row"),
        P(("col", "row")),
        P(("col", "row")),
        P(("col", "row")),
        P("row", "col"),
        P(("col", "row")),
        P("col", "row"),
        P(("col", "row")),
    )
    return jax.shard_map(
        per_device, mesh=mesh, in_specs=in_specs, out_specs=out_specs, check_vma=False
    )
```
